32 devices in a mesh: chan: 16 (over z, x, core), tm: 2 (over y).
Axes of the slice: x: 2, y: 2, z: 4, core: 2. Of those that a mesh axis runs over, the one named last changes fastest.
Arguments:
- samples: bfloat16 [96, 2, 2048], P('chan', 'tm'), may hold values from -6 to 6
- dead_flags: int32 [96], P('chan'), may hold values 0 or 1
- pair_mask: int32 [96, 96], P('chan', 'tm'), may hold values 0 or 1
Outputs:
- xcorr: float32 [96, 96, 301], P('chan', 'tm')
The draws below stay inside these ranges and needn't reach their ends.
All inputs are finite; a program needn't handle non-finite values. No bound on the sum of `dead_flags` or of `pair_mask` on one device may be relied on, other than what follows from the above.
Results may differ from the reference program's by a relative error of at most 0.0095.
Values may be sent and summed in bfloat16 or wider, within the bound.
A program may use at most 64 MiB of HBM per device.

```python
import math
import jax
import jax.numpy as jnp
from jax import lax

L = 2048
F = 768
LAGS = 301
CHANNELS = 96
SUBWIN = 2


def with_ends(drawn, own_key, low, high):
    extent = drawn.shape
    index_at = [jax.random.randint(jax.random.fold_in(own_key, axis), (), 0, extent[axis]) for axis in range(len(extent))]
    drawn = drawn.at[tuple(index_at)].set(low)
    longest = extent.index(max(extent))
    index_at[longest] = (index_at[longest] + 1) % extent[longest]
    return drawn.at[tuple(index_at)].set(high)


def shard_levels(stream_key, shape, pieces, low, high):
    gain, own = 1.0, jax.random.fold_in(stream_key, 6)
    for axis_at, parts in pieces:
        steps = jnp.exp(jax.random.uniform(jax.random.fold_in(own, axis_at), (parts,), jnp.float32, low / len(pieces), high / len(pieces)))
        gain = gain * jnp.repeat(steps, shape[axis_at] // parts).reshape([-1 if axis == axis_at else 1 for axis in range(len(shape))])
    return gain


def bell_draw(key, extent, deviation, reach, pieces=(), held_as=jnp.bfloat16):
    entries = deviation * jax.random.normal(key, extent, jnp.float32)
    if pieces:
        entries = entries * shard_levels(key, extent, pieces, -0.22, 0.18)
    return jnp.clip(entries, -reach, reach).astype(held_as)


def setup_inputs(seed: int = 0) -> dict:
    splits = jax.random.split(jax.random.key(seed), 4)
    return {
        "samples": bell_draw(splits[0], (CHANNELS, SUBWIN, L), 1.0, 6.0, ((0, 16), (1, 2))),
        "dead_flags": with_ends((jax.random.randint(splits[1], (CHANNELS,), 0, 8) < 1).astype(jnp.int32), jax.random.fold_in(splits[1], 1), 0, 1),
        "pair_mask": with_ends((jax.random.randint(splits[2], (CHANNELS, CHANNELS), 0, 4) < 3).astype(jnp.int32), jax.random.fold_in(splits[2], 1), 0, 1),
    }


def taper_window(length):
    sample_index = jnp.arange(length, dtype=jnp.float32)
    return 0.5 - 0.5 * jnp.cos(2.0 * math.pi * (sample_index + 0.5) / length)

def forward_table(length, bins):
    sample_index = jnp.arange(length, dtype=jnp.int32)
    frequency = jnp.arange(1, bins + 1, dtype=jnp.int32)
    phase_index = sample_index[:, None] * frequency[None, :] % length
    angles = 2.0 * math.pi / length * phase_index.astype(jnp.float32)
    return jnp.concatenate([jnp.cos(angles), -jnp.sin(angles)], axis=1).astype(jnp.bfloat16)

def lag_table(length, bins, lags, factor):
    frequency = jnp.arange(1, bins + 1, dtype=jnp.int32)
    shifts = jnp.arange(lags, dtype=jnp.int32) - (lags - 1) // 2
    phase_index = jnp.mod(frequency[:, None] * shifts[None, :], length)
    angles = 2.0 * math.pi / length * phase_index.astype(jnp.float32)
    table_values = jnp.concatenate([jnp.cos(angles), -jnp.sin(angles)], axis=0) * factor
    return table_values.astype(jnp.bfloat16)

def whiten(samples, dead_flags, table_values):
    channel_count, windows, length = samples.shape
    bins = table_values.shape[1] // 2
    traces = samples.astype(jnp.float32)
    traces = traces - lax.optimization_barrier(jnp.mean(traces, axis=-1, keepdims=True))
    tapered = (traces * taper_window(length)).astype(jnp.bfloat16)
    spectra = jnp.dot(tapered.reshape(channel_count * windows, length), table_values, preferred_element_type=jnp.float32)
    real_part = spectra[:, :bins]
    imag_part = spectra[:, bins:]
    energy = real_part * real_part + imag_part * imag_part
    mean_energy = lax.optimization_barrier(jnp.mean(energy, axis=-1, keepdims=True))
    inverse_scale = lax.rsqrt(energy + 0.25 * mean_energy + 1e-06)
    alive_rows = jnp.repeat((1 - dead_flags).astype(jnp.float32), windows)[:, None]
    whitened = jnp.concatenate([real_part * inverse_scale, imag_part * inverse_scale], axis=1) * alive_rows
    return whitened.astype(jnp.bfloat16).reshape(channel_count, windows, 2 * bins)

def correlate(receivers, sources, lag_weights):
    bins = receivers.shape[-1] // 2
    rec_values = receivers.astype(jnp.float32)
    src_values = sources.astype(jnp.float32)
    rec_re = rec_values[:, None, :, :bins]
    rec_im = rec_values[:, None, :, bins:]
    src_re = src_values[None, :, :, :bins]
    src_im = src_values[None, :, :, bins:]
    cross_re = rec_re * src_re + rec_im * src_im
    cross_im = rec_im * src_re - rec_re * src_im
    cross = jnp.concatenate([cross_re, cross_im], axis=-1).astype(jnp.bfloat16)
    result = jnp.einsum('rgwk,kl->wrgl', cross.astype(jnp.float32), lag_weights.astype(jnp.float32))
    return result.astype(jnp.bfloat16)

def reference(samples, dead_flags, pair_mask):
    channel_count, windows, length = samples.shape
    table_values = forward_table(length, F)
    whitened = whiten(samples, dead_flags, table_values)
    lag_weights = lag_table(length, F, LAGS, 1.0 / math.sqrt(SUBWIN * F))
    block_size = math.gcd(channel_count, 8)
    blocks = whitened.reshape(channel_count // block_size, block_size, windows, 2 * F)

    def one_block(receivers):
        per_window = correlate(receivers, whitened, lag_weights)
        return lax.optimization_barrier(jnp.sum(per_window.astype(jnp.float32), axis=0))
    stacked = lax.map(one_block, blocks).reshape(channel_count, channel_count, LAGS)
    return stacked * pair_mask.astype(jnp.float32)[..., None]
```

```python
import functools
import math

import jax
import jax.numpy as jnp
import numpy as np
from jax import lax
from jax.experimental import pallas as pl
from jax.experimental.pallas import tpu as pltpu
from jax.sharding import PartitionSpec as P

F = 768
LAGS = 301


def taper_window(length):
    sample_index = jnp.arange(length, dtype=jnp.float32)
    return 0.5 - 0.5 * jnp.cos(2.0 * math.pi * (sample_index + 0.5) / length)


def forward_table(length, bins):
    sample_index = jnp.arange(length, dtype=jnp.int32)
    frequency = jnp.arange(1, bins + 1, dtype=jnp.int32)
    phase_index = sample_index[:, None] * frequency[None, :] % length
    angles = 2.0 * math.pi / length * phase_index.astype(jnp.float32)
    return jnp.concatenate([jnp.cos(angles), -jnp.sin(angles)], axis=1).astype(jnp.bfloat16)


def lag_table(length, bins, lags, factor):
    frequency = jnp.arange(1, bins + 1, dtype=jnp.int32)
    shifts = jnp.arange(lags, dtype=jnp.int32) - (lags - 1) // 2
    phase_index = jnp.mod(frequency[:, None] * shifts[None, :], length)
    angles = 2.0 * math.pi / length * phase_index.astype(jnp.float32)
    table_values = jnp.concatenate([jnp.cos(angles), -jnp.sin(angles)], axis=0) * factor
    return table_values.astype(jnp.bfloat16)


def whiten(samples, dead_flags, table_values):
    channel_count, windows, length = samples.shape
    bins = table_values.shape[1] // 2
    traces = samples.astype(jnp.float32)
    traces = traces - jnp.mean(traces, axis=-1, keepdims=True)
    tapered = (traces * taper_window(length)).astype(jnp.bfloat16)
    spectra = jnp.dot(
        tapered.reshape(channel_count * windows, length),
        table_values,
        preferred_element_type=jnp.float32,
    )
    real_part = spectra[:, :bins]
    imag_part = spectra[:, bins:]
    energy = real_part * real_part + imag_part * imag_part
    mean_energy = jnp.mean(energy, axis=-1, keepdims=True)
    inverse_scale = lax.rsqrt(energy + 0.25 * mean_energy + 1e-06)
    alive_rows = jnp.repeat((1 - dead_flags).astype(jnp.float32), windows)[:, None]
    whitened = (
        jnp.concatenate([real_part * inverse_scale, imag_part * inverse_scale], axis=1) * alive_rows
    )
    return whitened.astype(jnp.bfloat16).reshape(channel_count, windows, 2 * bins)


def correlate(receivers, sources, lag_weights):
    bins = receivers.shape[-1] // 2
    rec_values = receivers.astype(jnp.float32)
    src_values = sources.astype(jnp.float32)
    rec_re = rec_values[:, None, :, :bins]
    rec_im = rec_values[:, None, :, bins:]
    src_re = src_values[None, :, :, :bins]
    src_im = src_values[None, :, :, bins:]
    cross_re = rec_re * src_re + rec_im * src_im
    cross_im = rec_im * src_re - rec_re * src_im
    cross = jnp.concatenate([cross_re, cross_im], axis=-1).astype(jnp.bfloat16)
    result = jnp.einsum("rgwk,kl->wrgl", cross, lag_weights, preferred_element_type=jnp.float32)
    return result.astype(jnp.bfloat16)


def pick_group(source_count, rows_each):
    chosen = 1
    for candidate in range(1, source_count + 1):
        if source_count % candidate == 0 and candidate * rows_each <= 1024:
            chosen = candidate
    return chosen


def per_device(samples, dead_flags, pair_mask):
    block_size, local_windows, length = samples.shape
    table_values = forward_table(length, F)
    whitened = whiten(samples, dead_flags, table_values)
    subwin = local_windows * lax.axis_size("tm")
    lag_weights = lag_table(length, F, LAGS, 1.0 / math.sqrt(subwin * F))
    incoming = lax.all_gather(whitened, "chan", axis=0, tiled=True)
    source_count = incoming.shape[0]
    group_size = pick_group(source_count, block_size * local_windows)
    grouped = incoming.reshape(source_count // group_size, group_size, local_windows, 2 * F)

    def one_group(group_sources):
        return correlate(whitened, group_sources, lag_weights)[0]

    results = lax.map(one_group, grouped)
    placed = jnp.transpose(results, (1, 0, 2, 3)).reshape(block_size, source_count, LAGS)
    shares = lax.psum_scatter(
        placed.astype(jnp.float32).astype(jnp.bfloat16), "tm", scatter_dimension=1, tiled=True
    ).astype(jnp.float32)
    return shares * pair_mask.astype(jnp.float32)[..., None]


RADIX = 16
LANES = 128
ROWS = 8
MESH = pl.DeviceIdType.MESH


def bin_order(bins):
    share = bins // RADIX
    place = np.arange(bins)
    return place // share + 1 + RADIX * (place % share)


def split_tables(length, bins):
    depth, share = length // RADIX, bins // RADIX
    phases = share // math.gcd(share, LANES)
    steps, lanes = np.arange(depth)[:, None], np.arange(LANES)[None, :]
    table = []
    for phase in range(phases):
        angle = 2.0 * np.pi / depth * (steps * ((phase * LANES + lanes) % share) % depth)
        cos, sin = np.cos(angle), np.sin(angle)
        table.append(np.block([[cos, -sin], [sin, cos]]))
    turn = 2.0 * np.pi / length * (np.arange(1, RADIX + 1)[:, None] * np.arange(depth)[None, :] % length)
    return np.stack(table), np.stack([np.cos(turn), np.sin(turn)])


def ordered_lag_table(length, order, lags, factor):
    shifts = np.arange(lags) - (lags - 1) // 2
    angles = 2.0 * np.pi / length * np.mod(order[:, None] * shifts[None, :], length)
    values = np.concatenate([np.cos(angles), -np.sin(angles)], axis=0) * factor
    padded = -(-lags // LANES) * LANES
    return np.pad(values, ((0, 0), (0, padded - lags))).astype(np.float32)


def packing(block, length):
    width = block * length // ROWS
    tail = length - width
    return width, tail, width // tail if tail > 0 else 0


def packs(block, length):
    width, tail, chunks = packing(block, length)
    full = block < ROWS and block * length % (ROWS * LANES) == 0
    return full and tail % LANES == 0 and width % tail == 0 and (ROWS - block) * chunks == block


def stage_one(pieces):
    half = RADIX // 2
    sums = [pieces[a] + pieces[RADIX - a] for a in range(1, half)]
    diffs = [pieces[a] - pieces[RADIX - a] for a in range(1, half)]
    even = pieces[0] + pieces[half]
    odd = pieces[0] - pieces[half]

    def real(k):
        total = even if k % 2 == 0 else odd
        for a in range(1, half):
            total = total + sums[a - 1] * float(np.cos(2 * np.pi * a * k / RADIX))
        return total

    def imag(k):
        total = diffs[0] * float(-np.sin(2 * np.pi * k / RADIX))
        for a in range(2, half):
            total = total + diffs[a - 1] * float(-np.sin(2 * np.pi * a * k / RADIX))
        return total

    return [real(k) for k in range(half + 1)], [imag(k) for k in range(1, half)]


def twisted(pieces, turns):
    half = RADIX // 2
    reals, imags = stage_one(pieces)
    rows = []
    for k in range(1, RADIX + 1):
        low = min(k, RADIX - k)
        cos, sin, re = turns[0, k - 1 : k], turns[1, k - 1 : k], reals[low]
        if low == 0 or low == half:
            rows.append(jnp.concatenate([re * cos, -re * sin], axis=1))
            continue
        im = imags[low - 1] if k < half else -imags[low - 1]
        rows.append(jnp.concatenate([re * cos + im * sin, im * cos - re * sin], axis=1))
    return rows


def fused_kernel(
    sizes, samples_hbm, dead_hbm, mask_hbm, taper_hbm, turn_hbm, table_ref, lag_ref, out_ref, keep_ref,
    samples_ref, dead_ref, maskv, taper_ref, turn_ref, padded, packed, own, src, rec, recf, srcf, cross, table, lagv,
    table_sem, send_sem, pair_sem, fwd_sem, src_sem, rec_sem, gate,
):
    chans, tms, block, group, bins = sizes
    me_c, me_t = lax.axis_index("chan"), lax.axis_index("tm")
    core = me_c % 2
    columns = chans // 2
    barrier = pltpu.get_barrier_semaphore()
    sibling = me_c + 1 - 2 * core
    load_samples = pltpu.make_async_copy(samples_hbm, samples_ref, table_sem.at[2])
    load_samples.start()
    load_dead = pltpu.make_async_copy(dead_hbm, dead_ref, table_sem.at[4])
    load_dead.start()
    load_mask = pltpu.make_async_copy(mask_hbm, maskv, table_sem.at[5])
    load_mask.start()
    load_taper = pltpu.make_async_copy(taper_hbm, taper_ref, table_sem.at[3])
    load_taper.start()
    load_turn = pltpu.make_async_copy(turn_hbm, turn_ref, table_sem.at[6])
    load_turn.start()
    load_table = pltpu.make_async_copy(table_ref, table, table_sem.at[0])
    load_table.start()
    load_lag = pltpu.make_async_copy(lag_ref, lagv, table_sem.at[1])
    load_lag.start()

    half = group // 2
    chip = me_c // 2
    part = (chip >= columns // 2).astype(jnp.int32)
    for i in range(half // 2):
        for w in range(tms):
            from_chip = (me_t * group + core * half) // 2 + i

            @pl.when(jnp.logical_not(jnp.logical_and(from_chip == chip, w == me_t)))
            def _():
                pl.semaphore_signal(
                    barrier, inc=1, device_id=(2 * from_chip + part, w), device_id_type=MESH
                )

    for step in range(1, tms):
        pl.semaphore_signal(
            barrier, inc=1, device_id=(2 * chip, (me_t + step) % tms), device_id_type=MESH
        )
    pl.semaphore_signal(barrier, inc=1, device_id=(sibling, me_t), device_id_type=MESH)

    length = samples_ref.shape[-1]
    depth = length // RADIX
    load_samples.wait()
    load_taper.wait()
    traces = samples_ref[...].astype(jnp.float32)
    traces = traces - jnp.mean(traces, axis=-1, keepdims=True)
    padded[block:, :] = jnp.zeros((ROWS - block, length), jnp.float32)
    padded[:block, :] = (traces * taper_ref[...]).astype(jnp.bfloat16).astype(jnp.float32)
    load_turn.wait()
    rows = twisted([padded[:, a * depth : (a + 1) * depth] for a in range(RADIX)], turn_ref)
    load_dead.wait()
    row = lax.broadcasted_iota(jnp.int32, (ROWS, 1), 0)
    alive = jnp.zeros((ROWS, 1), jnp.float32)
    for r in range(block):
        alive = jnp.where(row == r, (1 - dead_ref[r]).astype(jnp.float32), alive)
    load_table.wait()
    share = bins // RADIX
    phases = table.shape[0]
    tiles = bins // LANES
    lane = lax.broadcasted_iota(jnp.int32, (1, LANES), 1)
    parts = [None] * tiles
    energy_sum = jnp.zeros((ROWS, LANES), jnp.float32)
    for phase in range(phases):
        members = []
        for tile in range(phase, tiles, phases):
            first, last = tile * LANES // share, (tile * LANES + LANES - 1) // share
            members += [(tile, r) for r in range(first, last + 1)]
        lhs = jnp.concatenate([rows[r] for _, r in members], axis=0).astype(jnp.bfloat16)
        spec = jnp.dot(lhs, table[phase], preferred_element_type=jnp.float32)
        for tile in range(phase, tiles, phases):
            re = im = None
            for index, (which, r) in enumerate(members):
                if which != tile:
                    continue
                now = spec[index * ROWS : (index + 1) * ROWS]
                begin = r * share - tile * LANES
                re = now[:, :LANES] if re is None else jnp.where(lane >= begin, now[:, :LANES], re)
                im = now[:, LANES:] if im is None else jnp.where(lane >= begin, now[:, LANES:], im)
            energy = re * re + im * im
            energy_sum = energy_sum + energy
            parts[tile] = (re, im, energy)
    width, tail, chunks = packing(block, 2 * bins)

    def pack(start, piece):
        if start < width:
            packed[:block, start : start + LANES] = piece[:block]
            return
        for r in range(block):
            first = (r % chunks) * tail + start - width
            packed[block + r // chunks : block + r // chunks + 1, first : first + LANES] = piece[r : r + 1]

    def unpack(values, store):
        store(slice(0, block), slice(0, width), values[:block])
        for r in range(block):
            first = (r % chunks) * tail
            store(
                slice(r, r + 1), slice(width, width + tail),
                values[block + r // chunks : block + r // chunks + 1, first : first + tail],
            )

    mean_energy = jnp.sum(energy_sum, axis=-1, keepdims=True) / bins
    for tile, (re, im, energy) in enumerate(parts):
        scale = lax.rsqrt(energy + 0.25 * mean_energy + 1e-06)
        pack(tile * LANES, re * scale * alive)
        pack(bins + tile * LANES, im * scale * alive)
    own[...] = packed[...].astype(jnp.bfloat16)

    to_t = me_c // group
    slot = me_c % group
    to_half, at = slot // half, slot % half
    keeps = jnp.logical_and(to_t == me_t, to_half == core)
    entered = columns // 2 + 1 - jnp.logical_and(to_t == me_t, part == core).astype(jnp.int32)

    def open_gate():
        pl.semaphore_signal(gate, inc=1, device_id=(sibling, me_t), device_id_type=MESH)

    def stays(i):
        return jnp.logical_and(keeps, i == chip)

    def push(i):
        return pltpu.make_async_remote_copy(
            src_ref=own, dst_ref=src.at[to_half, at, me_t],
            send_sem=send_sem.at[i], recv_sem=src_sem.at[to_half, at, me_t],
            device_id=(2 * i + to_half, to_t), device_id_type=MESH,
        )

    def start_push(i):
        @pl.when(jnp.logical_not(stays(i)))
        def _():
            push(i).start()

        @pl.when(stays(i))
        def _():
            pltpu.make_async_copy(own, src.at[to_half, at, me_t], src_sem.at[to_half, at, me_t]).start()

    def pair_copy(step):
        return pltpu.make_async_remote_copy(
            src_ref=own, dst_ref=rec.at[me_t],
            send_sem=pair_sem.at[step], recv_sem=rec_sem.at[me_t],
            device_id=(me_c, (me_t + step) % tms), device_id_type=MESH,
        )

    own_rec = pltpu.make_async_copy(own, rec.at[me_t], pair_sem.at[0])
    own_rec.start()

    @pl.when(core == 0)
    def _():
        pl.semaphore_wait(barrier, entered + 2 * (tms - 1))
        open_gate()

    @pl.when(core == 1)
    def _():
        pl.semaphore_wait(gate, 1)

    for i in range(columns // 2):
        start_push(i)
    for step in range(1, tms):
        pair_copy(step).start()

    @pl.when(core == 0)
    def _():
        pl.semaphore_wait(gate, 1)

    @pl.when(core == 1)
    def _():
        pl.semaphore_wait(barrier, entered)
        open_gate()

    for i in range(columns // 2, columns):
        start_push(i)

    def arrival(h, i, w):
        return pltpu.make_async_copy(own, src.at[h, i, w], src_sem.at[h, i, w])

    def forward(i, w):
        return pltpu.make_async_remote_copy(
            src_ref=src.at[core, i, w], dst_ref=src.at[core, i, w],
            send_sem=fwd_sem.at[i, w], recv_sem=src_sem.at[core, i, w],
            device_id=(sibling, me_t), device_id_type=MESH,
        )

    sources = half * block
    lags = out_ref.shape[-1]

    def correlate_half(h):
        for i in range(half):
            for w in range(tms):

                def store(rows, lanes, piece):
                    srcf[w, i * block + rows.start : i * block + rows.stop, lanes] = piece

                unpack(src[h, i, w].astype(jnp.float32), store)
        for tile in range(bins // LANES):
            lanes = slice(tile * LANES, (tile + 1) * LANES)
            lanes_im = slice(bins + tile * LANES, bins + (tile + 1) * LANES)
            rec_re = [recf[w, :, lanes] for w in range(tms)]
            rec_im = [recf[w, :, lanes_im] for w in range(tms)]
            src_re = [srcf[w, :, lanes] for w in range(tms)]
            src_im = [srcf[w, :, lanes_im] for w in range(tms)]
            for r in range(block):
                total_re = total_im = None
                for w in range(tms):
                    a, c = rec_re[w][r : r + 1, :], rec_im[w][r : r + 1, :]
                    now_re = a * src_re[w] + c * src_im[w]
                    now_im = c * src_re[w] - a * src_im[w]
                    total_re = now_re if total_re is None else total_re + now_re
                    total_im = now_im if total_im is None else total_im + now_im
                cross[r * sources : (r + 1) * sources, lanes] = total_re.astype(jnp.bfloat16)
                cross[r * sources : (r + 1) * sources, lanes_im] = total_im.astype(jnp.bfloat16)
        result = jnp.dot(cross[...], lagv[...], preferred_element_type=jnp.float32)
        for r in range(block):
            out_ref[r, pl.ds(pl.multiple_of(h * sources, sources), sources), :] = result[
                r * sources : (r + 1) * sources, :lags
            ]

    for i in range(half):
        for w in range(tms):
            arrival(core, i, w).wait()
            forward(i, w).start()
    load_mask.wait()
    keep_ref[...] = maskv[...].astype(jnp.float32)
    load_lag.wait()
    own_rec.wait()
    for step in range(1, tms):
        from_t = (me_t + step) % tms
        pltpu.make_async_copy(own, rec.at[from_t], rec_sem.at[from_t]).wait()

    for w in range(tms):

        def store_rec(rows, lanes, piece):
            recf[w, rows, lanes] = piece

        unpack(rec[w].astype(jnp.float32), store_rec)

    @pl.loop(0, 2)
    def _(turn):
        @pl.when(turn == 1)
        def _():
            for i in range(half):
                for w in range(tms):
                    arrival(1 - core, i, w).wait()

        correlate_half((core + turn) % 2)

    for i in range(columns):

        @pl.when(jnp.logical_not(stays(i)))
        def _():
            push(i).wait_send()

    for step in range(1, tms):
        pair_copy(step).wait_send()
    for i in range(half):
        for w in range(tms):
            forward(i, w).wait_send()


def fused_device(chans, tms, samples, dead_flags, pair_mask):
    block, _, length = samples.shape
    sources = pair_mask.shape[1]
    group = sources // block
    table, turns = split_tables(length, F)
    lag_weights = ordered_lag_table(length, bin_order(F), LAGS, 1.0 / math.sqrt(tms * F))
    at = np.arange(length)
    taper = (0.5 - 0.5 * np.cos(2.0 * np.pi * (at + 0.5) / length))[None, :].astype(np.float32)
    vmem, hbm = pl.BlockSpec(memory_space=pltpu.VMEM), pl.BlockSpec(memory_space=pltpu.HBM)
    sem = pltpu.SemaphoreType.DMA
    half = group // 2
    width = packing(block, 2 * F)[0]
    result, keep = pl.pallas_call(
        functools.partial(fused_kernel, (chans, tms, block, group, F)),
        out_shape=[
            pltpu.VMEM((block, sources, LAGS), jnp.float32),
            pltpu.VMEM((block, sources), jnp.float32),
        ],
        in_specs=[hbm] * 7,
        out_specs=[vmem] * 2,
        scratch_shapes=[
            pltpu.VMEM((block, length), jnp.bfloat16),
            pltpu.SMEM((block,), jnp.int32),
            pltpu.VMEM((block, sources), jnp.int32),
            pltpu.VMEM((1, length), jnp.float32),
            pltpu.VMEM(turns.shape, jnp.float32),
            pltpu.VMEM((ROWS, length), jnp.float32),
            pltpu.VMEM((ROWS, width), jnp.float32),
            pltpu.VMEM((ROWS, width), jnp.bfloat16),
            pltpu.VMEM((2, half, tms, ROWS, width), jnp.bfloat16),
            pltpu.VMEM((tms, ROWS, width), jnp.bfloat16),
            pltpu.VMEM((tms, block, 2 * F), jnp.float32),
            pltpu.VMEM((tms, half * block, 2 * F), jnp.float32),
            pltpu.VMEM((block * half * block, 2 * F), jnp.bfloat16),
            pltpu.VMEM(table.shape, jnp.bfloat16),
            pltpu.VMEM(lag_weights.shape, jnp.bfloat16),
            sem((7,)), sem((chans // 2,)), sem((tms,)), sem((half, tms)), sem((2, half, tms)), sem((tms,)),
            pltpu.SemaphoreType.REGULAR,
        ],
        compiler_params=pltpu.CompilerParams(
            collective_id=0, has_side_effects=True, vmem_limit_bytes=24 * 1024 * 1024
        ),
    )(
        *(
            pltpu.with_memory_space_constraint(operand, pltpu.HBM)
            for operand in (
                samples.reshape(block, length), dead_flags, pair_mask, jnp.asarray(taper),
                jnp.asarray(turns, jnp.float32),
                jnp.asarray(table, jnp.bfloat16), jnp.asarray(lag_weights, jnp.bfloat16),
            )
        )
    )
    return result * keep[..., None]


def dispatch(chans, tms, samples, dead_flags, pair_mask):
    block, windows, length = samples.shape
    sources = pair_mask.shape[1]
    whole_blocks = sources % (4 * block) == 0 and chans % 4 == 0 and sources % 16 == 0 and block * chans == sources * tms
    aligned = length == RADIX * LANES and F % LANES == 0 and F % RADIX == 0 and windows == 1
    if whole_blocks and aligned and packs(block, 2 * F):
        return fused_device(chans, tms, samples, dead_flags, pair_mask)
    return per_device(samples, dead_flags, pair_mask)


def solution(mesh):
    in_specs = (P("chan", "tm", None), P("chan"), P("chan", "tm"))
    out_specs = P("chan", "tm", None)
    chans, tms = mesh.shape["chan"], mesh.shape["tm"]
    return jax.shard_map(
        functools.partial(dispatch, chans, tms),
        mesh=mesh, in_specs=in_specs, out_specs=out_specs, check_vma=False,
    )
```

```python
import functools
import math

import jax
import jax.numpy as jnp
import numpy as np
from jax import lax
from jax.experimental import pallas as pl
from jax.experimental.pallas import tpu as pltpu
from jax.sharding import PartitionSpec as P

F = 768
LAGS = 301


def taper_window(length):
    sample_index = jnp.arange(length, dtype=jnp.float32)
    return 0.5 - 0.5 * jnp.cos(2.0 * math.pi * (sample_index + 0.5) / length)


def forward_table(length, bins):
    sample_index = jnp.arange(length, dtype=jnp.int32)
    frequency = jnp.arange(1, bins + 1, dtype=jnp.int32)
    phase_index = sample_index[:, None] * frequency[None, :] % length
    angles = 2.0 * math.pi / length * phase_index.astype(jnp.float32)
    return jnp.concatenate([jnp.cos(angles), -jnp.sin(angles)], axis=1).astype(jnp.bfloat16)


def lag_table(length, bins, lags, factor):
    frequency = jnp.arange(1, bins + 1, dtype=jnp.int32)
    shifts = jnp.arange(lags, dtype=jnp.int32) - (lags - 1) // 2
    phase_index = jnp.mod(frequency[:, None] * shifts[None, :], length)
    angles = 2.0 * math.pi / length * phase_index.astype(jnp.float32)
    table_values = jnp.concatenate([jnp.cos(angles), -jnp.sin(angles)], axis=0) * factor
    return table_values.astype(jnp.bfloat16)


def whiten(samples, dead_flags, table_values):
    channel_count, windows, length = samples.shape
    bins = table_values.shape[1] // 2
    traces = samples.astype(jnp.float32)
    traces = traces - jnp.mean(traces, axis=-1, keepdims=True)
    tapered = (traces * taper_window(length)).astype(jnp.bfloat16)
    spectra = jnp.dot(
        tapered.reshape(channel_count * windows, length),
        table_values,
        preferred_element_type=jnp.float32,
    )
    real_part = spectra[:, :bins]
    imag_part = spectra[:, bins:]
    energy = real_part * real_part + imag_part * imag_part
    mean_energy = jnp.mean(energy, axis=-1, keepdims=True)
    inverse_scale = lax.rsqrt(energy + 0.25 * mean_energy + 1e-06)
    alive_rows = jnp.repeat((1 - dead_flags).astype(jnp.float32), windows)[:, None]
    whitened = (
        jnp.concatenate([real_part * inverse_scale, imag_part * inverse_scale], axis=1) * alive_rows
    )
    return whitened.astype(jnp.bfloat16).reshape(channel_count, windows, 2 * bins)


def correlate(receivers, sources, lag_weights):
    bins = receivers.shape[-1] // 2
    rec_values = receivers.astype(jnp.float32)
    src_values = sources.astype(jnp.float32)
    rec_re = rec_values[:, None, :, :bins]
    rec_im = rec_values[:, None, :, bins:]
    src_re = src_values[None, :, :, :bins]
    src_im = src_values[None, :, :, bins:]
    cross_re = rec_re * src_re + rec_im * src_im
    cross_im = rec_im * src_re - rec_re * src_im
    cross = jnp.concatenate([cross_re, cross_im], axis=-1).astype(jnp.bfloat16)
    result = jnp.einsum("rgwk,kl->wrgl", cross, lag_weights, preferred_element_type=jnp.float32)
    return result.astype(jnp.bfloat16)


def pick_group(source_count, rows_each):
    chosen = 1
    for candidate in range(1, source_count + 1):
        if source_count % candidate == 0 and candidate * rows_each <= 1024:
            chosen = candidate
    return chosen


def per_device(samples, dead_flags, pair_mask):
    block_size, local_windows, length = samples.shape
    table_values = forward_table(length, F)
    whitened = whiten(samples, dead_flags, table_values)
    subwin = local_windows * lax.axis_size("tm")
    lag_weights = lag_table(length, F, LAGS, 1.0 / math.sqrt(subwin * F))
    incoming = lax.all_gather(whitened, "chan", axis=0, tiled=True)
    source_count = incoming.shape[0]
    group_size = pick_group(source_count, block_size * local_windows)
    grouped = incoming.reshape(source_count // group_size, group_size, local_windows, 2 * F)

    def one_group(group_sources):
        return correlate(whitened, group_sources, lag_weights)[0]

    results = lax.map(one_group, grouped)
    placed = jnp.transpose(results, (1, 0, 2, 3)).reshape(block_size, source_count, LAGS)
    shares = lax.psum_scatter(
        placed.astype(jnp.float32).astype(jnp.bfloat16), "tm", scatter_dimension=1, tiled=True
    ).astype(jnp.float32)
    return shares * pair_mask.astype(jnp.float32)[..., None]


RADIX = 16
LANES = 128
ROWS = 8
MESH = pl.DeviceIdType.MESH


def bin_order(bins):
    share = bins // RADIX
    place = np.arange(bins)
    return place // share + 1 + RADIX * (place % share)


def split_tables(length, bins):
    depth, share = length // RADIX, bins // RADIX
    phases = share // math.gcd(share, LANES)
    steps, lanes = np.arange(depth)[:, None], np.arange(LANES)[None, :]
    table = []
    for phase in range(phases):
        angle = 2.0 * np.pi / depth * (steps * ((phase * LANES + lanes) % share) % depth)
        cos, sin = np.cos(angle), np.sin(angle)
        table.append(np.block([[cos, -sin], [sin, cos]]))
    turn = 2.0 * np.pi / length * (np.arange(1, RADIX + 1)[:, None] * np.arange(depth)[None, :] % length)
    return np.stack(table), np.stack([np.cos(turn), np.sin(turn)])


def folded_lags(lags):
    middle, over = lags // 2, lags - 2 * LANES
    at = np.arange(LANES)
    return np.concatenate([LANES + at - middle, np.where(at < over, LANES, 0) + LANES + at - middle])


def folded_lag_tables(length, order, lags, factor):
    angles = 2.0 * np.pi / length * np.mod(order[:, None] * folded_lags(lags)[None, :], length)
    return (np.stack([np.cos(angles), -np.sin(angles)]) * factor).astype(np.float32)


def folds(lags):
    middle = lags // 2
    return lags % 2 == 1 and 2 * LANES < lags < 3 * LANES and LANES <= middle + 1


def packing(block, length):
    width = block * length // ROWS
    tail = length - width
    return width, tail, width // tail if tail > 0 else 0


def packs(block, length):
    width, tail, chunks = packing(block, length)
    full = block < ROWS and block * length % (ROWS * LANES) == 0
    return full and tail % LANES == 0 and width % tail == 0 and (ROWS - block) * chunks == block


def stage_one(pieces):
    half = RADIX // 2
    sums = [pieces[a] + pieces[RADIX - a] for a in range(1, half)]
    diffs = [pieces[a] - pieces[RADIX - a] for a in range(1, half)]
    even = pieces[0] + pieces[half]
    odd = pieces[0] - pieces[half]

    def real(k):
        total = even if k % 2 == 0 else odd
        for a in range(1, half):
            total = total + sums[a - 1] * float(np.cos(2 * np.pi * a * k / RADIX))
        return total

    def imag(k):
        total = diffs[0] * float(-np.sin(2 * np.pi * k / RADIX))
        for a in range(2, half):
            total = total + diffs[a - 1] * float(-np.sin(2 * np.pi * a * k / RADIX))
        return total

    return [real(k) for k in range(half + 1)], [imag(k) for k in range(1, half)]


def twisted(pieces, turns):
    half = RADIX // 2
    reals, imags = stage_one(pieces)
    rows = []
    for k in range(1, RADIX + 1):
        low = min(k, RADIX - k)
        cos, sin, re = turns[1, k - 1 : k], turns[2, k - 1 : k], reals[low]
        if low == 0 or low == half:
            rows.append(jnp.concatenate([re * cos, -re * sin], axis=1))
            continue
        im = imags[low - 1] if k < half else -imags[low - 1]
        rows.append(jnp.concatenate([re * cos + im * sin, im * cos - re * sin], axis=1))
    return rows


def fused_kernel(
    sizes, samples_hbm, dead_hbm, mask_hbm, small_hbm, table_ref, lag_ref, out_ref, keep_ref,
    samples_ref, dead_ref, maskv, small, padded, packed, own, src, rec, recf, srcf, table, lagv,
    load_sem, send_sem, fwd_sem, slot_sem, half_sem, rec_sem, gate,
):
    chans, tms, block, group, bins = sizes
    me_c, me_t = lax.axis_index("chan"), lax.axis_index("tm")
    core = me_c % 2
    columns = chans // 2
    barrier = pltpu.get_barrier_semaphore()
    sibling = me_c + 1 - 2 * core
    loads = [
        pltpu.make_async_copy(samples_hbm, samples_ref, load_sem.at[0]),
        pltpu.make_async_copy(small_hbm, small, load_sem.at[0]),
        pltpu.make_async_copy(dead_hbm, dead_ref, load_sem.at[0]),
        pltpu.make_async_copy(table_ref, table, load_sem.at[1]),
        pltpu.make_async_copy(mask_hbm, maskv, load_sem.at[2]),
        pltpu.make_async_copy(lag_ref, lagv, load_sem.at[2]),
    ]
    for load in loads:
        load.start()

    half = group // 2
    chip = me_c // 2

    def split_of(t):
        return jnp.where(t == 0, 4, 2)

    part = (chip >= split_of(me_t)).astype(jnp.int32)
    for i in range(half // 2):
        for w in range(tms):
            from_chip = (me_t * group + core * half) // 2 + i

            @pl.when(jnp.logical_not(jnp.logical_and(from_chip == chip, w == me_t)))
            def _():
                pl.semaphore_signal(
                    barrier, inc=1, device_id=(2 * from_chip + part, w), device_id_type=MESH
                )

    for step in range(1, tms):
        pl.semaphore_signal(
            barrier, inc=1, device_id=(2 * chip, (me_t + step) % tms), device_id_type=MESH
        )
    pl.semaphore_signal(barrier, inc=1, device_id=(sibling, me_t), device_id_type=MESH)

    length = samples_ref.shape[-1]
    depth = length // RADIX
    for load in loads[:3]:
        load.wait()
    traces = samples_ref[...].astype(jnp.float32)
    traces = traces - jnp.mean(traces, axis=-1, keepdims=True)
    padded[block:, :] = jnp.zeros((ROWS - block, length), jnp.float32)
    for a in range(RADIX):
        lanes = slice(a * depth, (a + 1) * depth)
        padded[:block, lanes] = (traces[:, lanes] * small[0, a : a + 1]).astype(jnp.bfloat16).astype(jnp.float32)
    rows = twisted([padded[:, a * depth : (a + 1) * depth] for a in range(RADIX)], small)
    row = lax.broadcasted_iota(jnp.int32, (ROWS, 1), 0)
    alive = jnp.zeros((ROWS, 1), jnp.float32)
    for r in range(block):
        alive = jnp.where(row == r, (1 - dead_ref[r]).astype(jnp.float32), alive)
    loads[3].wait()
    share = bins // RADIX
    phases = table.shape[0]
    tiles = bins // LANES
    lane = lax.broadcasted_iota(jnp.int32, (1, LANES), 1)
    parts = [None] * tiles
    energy_sum = jnp.zeros((ROWS, LANES), jnp.float32)
    for phase in range(phases):
        members = []
        for tile in range(phase, tiles, phases):
            first, last = tile * LANES // share, (tile * LANES + LANES - 1) // share
            members += [(tile, r) for r in range(first, last + 1)]
        lhs = jnp.concatenate([rows[r] for _, r in members], axis=0).astype(jnp.bfloat16)
        spec = jnp.dot(lhs, table[phase], preferred_element_type=jnp.float32)
        for tile in range(phase, tiles, phases):
            re = im = None
            for index, (which, r) in enumerate(members):
                if which != tile:
                    continue
                now = spec[index * ROWS : (index + 1) * ROWS]
                begin = r * share - tile * LANES
                re = now[:, :LANES] if re is None else jnp.where(lane >= begin, now[:, :LANES], re)
                im = now[:, LANES:] if im is None else jnp.where(lane >= begin, now[:, LANES:], im)
            energy = re * re + im * im
            energy_sum = energy_sum + energy
            parts[tile] = (re, im, energy)
    width, tail, chunks = packing(block, 2 * bins)

    def pack(start, piece):
        if start < width:
            packed[:block, start : start + LANES] = piece[:block]
            return
        for r in range(block):
            first = (r % chunks) * tail + start - width
            packed[block + r // chunks : block + r // chunks + 1, first : first + LANES] = piece[r : r + 1]

    def unpack(values, store):
        store(slice(0, block), slice(0, width), values[:block])
        for r in range(block):
            first = (r % chunks) * tail
            store(
                slice(r, r + 1), slice(width, width + tail),
                values[block + r // chunks : block + r // chunks + 1, first : first + tail],
            )

    mean_energy = jnp.sum(energy_sum, axis=-1, keepdims=True) / bins
    for tile, (re, im, energy) in enumerate(parts):
        scale = lax.rsqrt(energy + 0.25 * mean_energy + 1e-06)
        pack(tile * LANES, re * scale * alive)
        pack(bins + tile * LANES, im * scale * alive)
    own[...] = packed[...].astype(jnp.bfloat16)

    to_t = me_c // group
    slot = me_c % group
    to_half, at = slot // half, slot % half
    keeps = jnp.logical_and(to_t == me_t, to_half == core)
    split = split_of(to_t)
    entered = jnp.where(core == 0, split, columns - split) + 1
    entered = entered - jnp.logical_and(to_t == me_t, part == core).astype(jnp.int32)

    def open_gate():
        pl.semaphore_signal(gate, inc=1, device_id=(sibling, me_t), device_id_type=MESH)

    mine = to_half * columns + at * tms + me_t

    def push(i):
        return pltpu.make_async_remote_copy(
            src_ref=own, dst_ref=src.at[mine], send_sem=send_sem, recv_sem=slot_sem.at[at],
            device_id=(2 * i + to_half, to_t), device_id_type=MESH,
        )

    def start_push(i):
        @pl.when(jnp.logical_not(jnp.logical_and(keeps, i == chip)))
        def _():
            push(i).start()

    def pair_copy(step):
        return pltpu.make_async_remote_copy(
            src_ref=own, dst_ref=rec.at[me_t], send_sem=send_sem, recv_sem=rec_sem,
            device_id=(me_c, (me_t + step) % tms), device_id_type=MESH,
        )

    rec[me_t] = own[...]

    @pl.when(keeps)
    def _():
        src[mine] = own[...]

    @pl.when(core == 0)
    def _():
        pl.semaphore_wait(barrier, entered + 2 * (tms - 1))
        open_gate()

    @pl.when(core == 1)
    def _():
        pl.semaphore_wait(gate, 1)

    @pl.loop(0, split)
    def _(i):
        start_push(i)

    for step in range(1, tms):
        pair_copy(step).start()

    @pl.when(core == 0)
    def _():
        pl.semaphore_wait(gate, 1)

    @pl.when(core == 1)
    def _():
        pl.semaphore_wait(barrier, entered)
        open_gate()

    @pl.loop(split, columns)
    def _(i):
        start_push(i)

    def landed(start, count, sem):
        blocks = src.at[pl.ds(start, count)]
        return pltpu.make_async_copy(blocks, blocks, sem)

    def forward(i):
        blocks = src.at[pl.ds(core * columns + i * tms, tms)]
        return pltpu.make_async_remote_copy(
            src_ref=blocks, dst_ref=blocks, send_sem=fwd_sem, recv_sem=half_sem,
            device_id=(sibling, me_t), device_id_type=MESH,
        )

    sources = half * block
    lags = out_ref.shape[-1]

    def correlate_half(h):
        for i in range(half):
            for w in range(tms):

                def store(rows, lanes, piece):
                    srcf[w, i * block + rows.start : i * block + rows.stop, lanes] = piece

                unpack(src[h * columns + i * tms + w].astype(jnp.float32), store)
        even = odd = None
        for first in range(0, bins // LANES, 2):
            parts_re, parts_im = [], []
            for tile in range(first, first + 2):
                lanes = slice(tile * LANES, (tile + 1) * LANES)
                lanes_im = slice(bins + tile * LANES, bins + (tile + 1) * LANES)
                rec_re = [recf[w, :, lanes] for w in range(tms)]
                rec_im = [recf[w, :, lanes_im] for w in range(tms)]
                src_re = [srcf[w, :, lanes] for w in range(tms)]
                src_im = [srcf[w, :, lanes_im] for w in range(tms)]
                rows_re, rows_im = [], []
                for r in range(block):
                    total_re = total_im = None
                    for w in range(tms):
                        a, c = rec_re[w][r : r + 1, :], rec_im[w][r : r + 1, :]
                        now_re = a * src_re[w] + c * src_im[w]
                        now_im = c * src_re[w] - a * src_im[w]
                        total_re = now_re if total_re is None else total_re + now_re
                        total_im = now_im if total_im is None else total_im + now_im
                    rows_re.append(total_re)
                    rows_im.append(total_im)
                parts_re.append(jnp.concatenate(rows_re, axis=0).astype(jnp.bfloat16))
                parts_im.append(jnp.concatenate(rows_im, axis=0).astype(jnp.bfloat16))
            depths = slice(first * LANES, (first + 2) * LANES)
            now_even = jnp.dot(
                jnp.concatenate(parts_re, axis=1), lagv[0, depths, :], preferred_element_type=jnp.float32
            )
            now_odd = jnp.dot(
                jnp.concatenate(parts_im, axis=1), lagv[1, depths, :], preferred_element_type=jnp.float32
            )
            even = now_even if even is None else even + now_even
            odd = now_odd if odd is None else odd + now_odd
        ahead = even + odd
        behind = even[:, LANES:] - odd[:, LANES:]
        over = lags - 2 * LANES
        lane = lax.broadcasted_iota(jnp.int32, behind.shape, 1)
        behind = jnp.take_along_axis(behind, (over - 1 - lane + LANES) % LANES, axis=1)
        for r in range(block):
            rows = slice(r * sources, (r + 1) * sources)
            to = pl.ds(pl.multiple_of(h * sources, sources), sources)
            out_ref[r, to, :LANES] = behind[rows]
            out_ref[r, to, LANES : 2 * LANES] = ahead[rows, :LANES]
            out_ref[r, to, 2 * LANES :] = ahead[rows, LANES : LANES + over]

    for i in range(half):
        holds = jnp.logical_and(keeps, at == i)

        @pl.when(jnp.logical_not(holds))
        def _():
            landed(core * columns + i * tms, tms, slot_sem.at[i]).wait()

        @pl.when(holds)
        def _():
            landed(core * columns + i * tms, tms - 1, slot_sem.at[i]).wait()

        forward(i).start()
    for load in loads[4:]:
        load.wait()
    keep_ref[...] = maskv[...].astype(jnp.float32)
    pltpu.make_async_copy(rec.at[pl.ds(0, tms - 1)], rec.at[pl.ds(0, tms - 1)], rec_sem).wait()

    for w in range(tms):

        def store_rec(rows, lanes, piece):
            recf[w, rows, lanes] = piece

        unpack(rec[w].astype(jnp.float32), store_rec)

    @pl.loop(0, 2)
    def _(turn):
        @pl.when(turn == 1)
        def _():
            landed((1 - core) * columns, columns, half_sem).wait()

        correlate_half((core + turn) % 2)

    @pl.when(jnp.logical_not(keeps))
    def _():
        landed(0, columns + tms - 1, send_sem).wait()

    @pl.when(keeps)
    def _():
        landed(0, columns + tms - 2, send_sem).wait()

    landed(0, columns, fwd_sem).wait()


def fused_device(chans, tms, samples, dead_flags, pair_mask):
    block, _, length = samples.shape
    sources = pair_mask.shape[1]
    group = sources // block
    table, turns = split_tables(length, F)
    lag_weights = folded_lag_tables(length, bin_order(F), LAGS, 1.0 / math.sqrt(tms * F))
    at = np.arange(length)
    taper = 0.5 - 0.5 * np.cos(2.0 * np.pi * (at + 0.5) / length)
    small = np.concatenate([taper.reshape(1, RADIX, length // RADIX), turns]).astype(np.float32)
    vmem, hbm = pl.BlockSpec(memory_space=pltpu.VMEM), pl.BlockSpec(memory_space=pltpu.HBM)
    sem = pltpu.SemaphoreType.DMA
    half = group // 2
    width = packing(block, 2 * F)[0]
    result, keep = pl.pallas_call(
        functools.partial(fused_kernel, (chans, tms, block, group, F)),
        out_shape=[
            pltpu.VMEM((block, sources, LAGS), jnp.float32),
            pltpu.VMEM((block, sources), jnp.float32),
        ],
        in_specs=[hbm] * 6,
        out_specs=[vmem] * 2,
        scratch_shapes=[
            pltpu.VMEM((block, length), jnp.bfloat16),
            pltpu.SMEM((block,), jnp.int32),
            pltpu.VMEM((block, sources), jnp.int32),
            pltpu.VMEM(small.shape, jnp.float32),
            pltpu.VMEM((ROWS, length), jnp.float32),
            pltpu.VMEM((ROWS, width), jnp.float32),
            pltpu.VMEM((ROWS, width), jnp.bfloat16),
            pltpu.VMEM((chans, ROWS, width), jnp.bfloat16),
            pltpu.VMEM((tms, ROWS, width), jnp.bfloat16),
            pltpu.VMEM((tms, block, 2 * F), jnp.float32),
            pltpu.VMEM((tms, half * block, 2 * F), jnp.float32),
            pltpu.VMEM(table.shape, jnp.bfloat16),
            pltpu.VMEM(lag_weights.shape, jnp.bfloat16),
            sem((3,)), sem, sem, sem((half,)), sem, sem, pltpu.SemaphoreType.REGULAR,
        ],
        compiler_params=pltpu.CompilerParams(
            collective_id=0, has_side_effects=True, vmem_limit_bytes=24 * 1024 * 1024
        ),
    )(
        *(
            pltpu.with_memory_space_constraint(operand, pltpu.HBM)
            for operand in (
                samples.reshape(block, length), dead_flags, pair_mask, jnp.asarray(small),
                jnp.asarray(table, jnp.bfloat16), jnp.asarray(lag_weights, jnp.bfloat16),
            )
        )
    )
    return result * keep[..., None]


def dispatch(chans, tms, samples, dead_flags, pair_mask):
    block, windows, length = samples.shape
    sources = pair_mask.shape[1]
    whole_blocks = sources % (4 * block) == 0 and chans % 4 == 0 and sources % 16 == 0 and block * chans == sources * tms
    aligned = length == RADIX * LANES and F % LANES == 0 and F % RADIX == 0 and windows == 1
    if whole_blocks and aligned and packs(block, 2 * F) and folds(LAGS):
        return fused_device(chans, tms, samples, dead_flags, pair_mask)
    return per_device(samples, dead_flags, pair_mask)


def solution(mesh):
    in_specs = (P("chan", "tm", None), P("chan"), P("chan", "tm"))
    out_specs = P("chan", "tm", None)
    chans, tms = mesh.shape["chan"], mesh.shape["tm"]
    return jax.shard_map(
        functools.partial(dispatch, chans, tms),
        mesh=mesh, in_specs=in_specs, out_specs=out_specs, check_vma=False,
    )
```

```python
import functools
import math

import jax
import jax.numpy as jnp
import numpy as np
from jax import lax
from jax.experimental import pallas as pl
from jax.experimental.pallas import tpu as pltpu
from jax.sharding import PartitionSpec as P

F = 768
LAGS = 301


def taper_window(length):
    sample_index = jnp.arange(length, dtype=jnp.float32)
    return 0.5 - 0.5 * jnp.cos(2.0 * math.pi * (sample_index + 0.5) / length)


def forward_table(length, bins):
    sample_index = jnp.arange(length, dtype=jnp.int32)
    frequency = jnp.arange(1, bins + 1, dtype=jnp.int32)
    phase_index = sample_index[:, None] * frequency[None, :] % length
    angles = 2.0 * math.pi / length * phase_index.astype(jnp.float32)
    return jnp.concatenate([jnp.cos(angles), -jnp.sin(angles)], axis=1).astype(jnp.bfloat16)


def lag_table(length, bins, lags, factor):
    frequency = jnp.arange(1, bins + 1, dtype=jnp.int32)
    shifts = jnp.arange(lags, dtype=jnp.int32) - (lags - 1) // 2
    phase_index = jnp.mod(frequency[:, None] * shifts[None, :], length)
    angles = 2.0 * math.pi / length * phase_index.astype(jnp.float32)
    table_values = jnp.concatenate([jnp.cos(angles), -jnp.sin(angles)], axis=0) * factor
    return table_values.astype(jnp.bfloat16)


def whiten(samples, dead_flags, table_values):
    channel_count, windows, length = samples.shape
    bins = table_values.shape[1] // 2
    traces = samples.astype(jnp.float32)
    traces = traces - jnp.mean(traces, axis=-1, keepdims=True)
    tapered = (traces * taper_window(length)).astype(jnp.bfloat16)
    spectra = jnp.dot(
        tapered.reshape(channel_count * windows, length),
        table_values,
        preferred_element_type=jnp.float32,
    )
    real_part = spectra[:, :bins]
    imag_part = spectra[:, bins:]
    energy = real_part * real_part + imag_part * imag_part
    mean_energy = jnp.mean(energy, axis=-1, keepdims=True)
    inverse_scale = lax.rsqrt(energy + 0.25 * mean_energy + 1e-06)
    alive_rows = jnp.repeat((1 - dead_flags).astype(jnp.float32), windows)[:, None]
    whitened = (
        jnp.concatenate([real_part * inverse_scale, imag_part * inverse_scale], axis=1) * alive_rows
    )
    return whitened.astype(jnp.bfloat16).reshape(channel_count, windows, 2 * bins)


def correlate(receivers, sources, lag_weights):
    bins = receivers.shape[-1] // 2
    rec_values = receivers.astype(jnp.float32)
    src_values = sources.astype(jnp.float32)
    rec_re = rec_values[:, None, :, :bins]
    rec_im = rec_values[:, None, :, bins:]
    src_re = src_values[None, :, :, :bins]
    src_im = src_values[None, :, :, bins:]
    cross_re = rec_re * src_re + rec_im * src_im
    cross_im = rec_im * src_re - rec_re * src_im
    cross = jnp.concatenate([cross_re, cross_im], axis=-1).astype(jnp.bfloat16)
    result = jnp.einsum("rgwk,kl->wrgl", cross, lag_weights, preferred_element_type=jnp.float32)
    return result.astype(jnp.bfloat16)


def pick_group(source_count, rows_each):
    chosen = 1
    for candidate in range(1, source_count + 1):
        if source_count % candidate == 0 and candidate * rows_each <= 1024:
            chosen = candidate
    return chosen


def per_device(samples, dead_flags, pair_mask):
    block_size, local_windows, length = samples.shape
    table_values = forward_table(length, F)
    whitened = whiten(samples, dead_flags, table_values)
    subwin = local_windows * lax.axis_size("tm")
    lag_weights = lag_table(length, F, LAGS, 1.0 / math.sqrt(subwin * F))
    incoming = lax.all_gather(whitened, "chan", axis=0, tiled=True)
    source_count = incoming.shape[0]
    group_size = pick_group(source_count, block_size * local_windows)
    grouped = incoming.reshape(source_count // group_size, group_size, local_windows, 2 * F)

    def one_group(group_sources):
        return correlate(whitened, group_sources, lag_weights)[0]

    results = lax.map(one_group, grouped)
    placed = jnp.transpose(results, (1, 0, 2, 3)).reshape(block_size, source_count, LAGS)
    shares = lax.psum_scatter(
        placed.astype(jnp.float32).astype(jnp.bfloat16), "tm", scatter_dimension=1, tiled=True
    ).astype(jnp.float32)
    return shares * pair_mask.astype(jnp.float32)[..., None]


RADIX = 16
LANES = 128
ROWS = 8
MESH = pl.DeviceIdType.MESH


def bin_order(bins):
    share = bins // RADIX
    place = np.arange(bins)
    return place // share + 1 + RADIX * (place % share)


def split_tables(length, bins):
    depth, share = length // RADIX, bins // RADIX
    phases = share // math.gcd(share, LANES)
    steps, lanes = np.arange(depth)[:, None], np.arange(LANES)[None, :]
    table = []
    for phase in range(phases):
        angle = 2.0 * np.pi / depth * (steps * ((phase * LANES + lanes) % share) % depth)
        cos, sin = np.cos(angle), np.sin(angle)
        table.append(np.block([[cos, -sin], [sin, cos]]))
    turn = 2.0 * np.pi / length * (np.arange(1, RADIX + 1)[:, None] * np.arange(depth)[None, :] % length)
    return np.stack(table), np.stack([np.cos(turn), np.sin(turn)])


def folded_lags(lags):
    middle, over = lags // 2, lags - 2 * LANES
    at = np.arange(LANES)
    return np.concatenate([LANES + at - middle, np.where(at < over, LANES, 0) + LANES + at - middle])


def folded_lag_tables(length, order, lags, factor):
    angles = 2.0 * np.pi / length * np.mod(order[:, None] * folded_lags(lags)[None, :], length)
    return (np.stack([np.cos(angles), -np.sin(angles)]) * factor).astype(np.float32)


def folds(lags):
    middle = lags // 2
    return lags % 2 == 1 and 2 * LANES < lags < 3 * LANES and LANES <= middle + 1


def packing(block, length):
    width = block * length // ROWS
    tail = length - width
    return width, tail, width // tail if tail > 0 else 0


def packs(block, length):
    width, tail, chunks = packing(block, length)
    full = block < ROWS and block * length % (ROWS * LANES) == 0
    return full and tail % LANES == 0 and width % tail == 0 and (ROWS - block) * chunks == block


def stage_one(pieces):
    half = RADIX // 2
    sums = [pieces[a] + pieces[RADIX - a] for a in range(1, half)]
    diffs = [pieces[a] - pieces[RADIX - a] for a in range(1, half)]
    even = pieces[0] + pieces[half]
    odd = pieces[0] - pieces[half]

    def real(k):
        total = even if k % 2 == 0 else odd
        for a in range(1, half):
            total = total + sums[a - 1] * float(np.cos(2 * np.pi * a * k / RADIX))
        return total

    def imag(k):
        total = diffs[0] * float(-np.sin(2 * np.pi * k / RADIX))
        for a in range(2, half):
            total = total + diffs[a - 1] * float(-np.sin(2 * np.pi * a * k / RADIX))
        return total

    return [real(k) for k in range(half + 1)], [imag(k) for k in range(1, half)]


def twisted(pieces, turns):
    half = RADIX // 2
    reals, imags = stage_one(pieces)
    rows = []
    for k in range(1, RADIX + 1):
        low = min(k, RADIX - k)
        cos, sin, re = turns[1, k - 1 : k], turns[2, k - 1 : k], reals[low]
        if low == 0 or low == half:
            rows.append(jnp.concatenate([re * cos, -re * sin], axis=1))
            continue
        im = imags[low - 1] if k < half else -imags[low - 1]
        rows.append(jnp.concatenate([re * cos + im * sin, im * cos - re * sin], axis=1))
    return rows


def correlate_sources(recf, srcf, lagv, lags, store):
    tms, block, bins = recf.shape[0], recf.shape[1], recf.shape[2] // 2
    sources = srcf.shape[1]
    even = odd = None
    for first in range(0, bins // LANES, 2):
        parts_re, parts_im = [], []
        for tile in range(first, first + 2):
            lanes = slice(tile * LANES, (tile + 1) * LANES)
            lanes_im = slice(bins + tile * LANES, bins + (tile + 1) * LANES)
            rec_re = [recf[w, :, lanes] for w in range(tms)]
            rec_im = [recf[w, :, lanes_im] for w in range(tms)]
            src_re = [srcf[w, :, lanes] for w in range(tms)]
            src_im = [srcf[w, :, lanes_im] for w in range(tms)]
            rows_re, rows_im = [], []
            for r in range(block):
                total_re = total_im = None
                for w in range(tms):
                    a, c = rec_re[w][r : r + 1, :], rec_im[w][r : r + 1, :]
                    now_re = a * src_re[w] + c * src_im[w]
                    now_im = c * src_re[w] - a * src_im[w]
                    total_re = now_re if total_re is None else total_re + now_re
                    total_im = now_im if total_im is None else total_im + now_im
                rows_re.append(total_re)
                rows_im.append(total_im)
            parts_re.append(jnp.concatenate(rows_re, axis=0).astype(jnp.bfloat16))
            parts_im.append(jnp.concatenate(rows_im, axis=0).astype(jnp.bfloat16))
        depths = slice(first * LANES, (first + 2) * LANES)
        now_even = jnp.dot(
            jnp.concatenate(parts_re, axis=1), lagv[0, depths, :], preferred_element_type=jnp.float32
        )
        now_odd = jnp.dot(
            jnp.concatenate(parts_im, axis=1), lagv[1, depths, :], preferred_element_type=jnp.float32
        )
        even = now_even if even is None else even + now_even
        odd = now_odd if odd is None else odd + now_odd
    ahead = even + odd
    behind = even[:, LANES:] - odd[:, LANES:]
    over = lags - 2 * LANES
    lane = lax.broadcasted_iota(jnp.int32, behind.shape, 1)
    behind = jnp.take_along_axis(behind, (over - 1 - lane + LANES) % LANES, axis=1)
    for r in range(block):
        rows = slice(r * sources, (r + 1) * sources)
        store(r, 0, behind[rows])
        store(r, 1, ahead[rows, :LANES])
        store(r, 2, ahead[rows, LANES : LANES + over])


def finish_kernel(first_ref, srcf, recf, lagv, kept, out_ref):
    other = 1 - lax.axis_index("chan") % 2
    block, sources, lags = first_ref.shape
    begin = pl.multiple_of((1 - other) * sources, sources)
    place = pl.ds(pl.multiple_of(other * sources, sources), sources)

    def store(r, tile, values):
        lanes = slice(tile * LANES, tile * LANES + values.shape[1])
        out_ref[r, place, lanes] = values * kept[r, place, : values.shape[1]]

    correlate_sources(recf, srcf, lagv, lags, store)
    for r in range(block):
        out_ref[r, pl.ds(begin, sources), :] = first_ref[r]


def push_orders(columns):
    near, far = list(range(columns // 2)), list(range(columns // 2, columns))
    return [near + far[0::2] + far[1::2], near[0::2] + near[1::2] + far]


def fused_kernel(
    sizes, samples_hbm, dead_hbm, mask_hbm, small_hbm, table_ref, lag_ref,
    first_ref, srcf, recf, lagv, kept,
    samples_ref, dead_ref, maskv, small, padded, packed, own, src, rec, table,
    load_sem, send_sem, fwd_sem, slot_sem, half_sem, rec_sem, gate,
):
    chans, tms, block, group, bins = sizes
    me_c, me_t = lax.axis_index("chan"), lax.axis_index("tm")
    core = me_c % 2
    columns = chans // 2
    barrier = pltpu.get_barrier_semaphore()
    sibling = me_c + 1 - 2 * core
    half = group // 2
    chip = me_c // 2
    orders = push_orders(columns)
    splits = [columns // 2 + 1, columns // 4]

    def choose(t, values):
        return jnp.where(t == 0, values[0], values[1])

    def is_late(t, at):
        late = [functools.reduce(jnp.logical_or, [at == i for i in o[n:]]) for o, n in zip(orders, splits)]
        return jnp.where(t == 0, late[0].astype(jnp.int32), late[1].astype(jnp.int32))

    part = is_late(me_t, chip)
    for i in range(half // 2):
        for w in range(tms):
            from_chip = (me_t * group + core * half) // 2 + i

            @pl.when(jnp.logical_not(jnp.logical_and(from_chip == chip, w == me_t)))
            def _():
                pl.semaphore_signal(
                    barrier, inc=1, device_id=(2 * from_chip + part, w), device_id_type=MESH
                )

    for step in range(1, tms):
        pl.semaphore_signal(
            barrier, inc=1, device_id=(2 * chip, (me_t + step) % tms), device_id_type=MESH
        )
    pl.semaphore_signal(barrier, inc=1, device_id=(sibling, me_t), device_id_type=MESH)

    length = samples_ref.shape[-1]
    depth = length // RADIX
    loads = [
        pltpu.make_async_copy(samples_hbm, samples_ref, load_sem.at[0]),
        pltpu.make_async_copy(small_hbm, small, load_sem.at[0]),
        pltpu.make_async_copy(dead_hbm, dead_ref, load_sem.at[0]),
        pltpu.make_async_copy(table_ref, table, load_sem.at[1]),
        pltpu.make_async_copy(mask_hbm, maskv, load_sem.at[2]),
        pltpu.make_async_copy(lag_ref, lagv, load_sem.at[2]),
    ]
    for load in loads:
        load.start()

    for load in loads[:3]:
        load.wait()
    traces = samples_ref[...].astype(jnp.float32)
    traces = traces - jnp.mean(traces, axis=-1, keepdims=True)
    padded[block:, :] = jnp.zeros((ROWS - block, length), jnp.float32)
    for a in range(RADIX):
        lanes = slice(a * depth, (a + 1) * depth)
        padded[:block, lanes] = (traces[:, lanes] * small[0, a : a + 1]).astype(jnp.bfloat16).astype(jnp.float32)
    rows = twisted([padded[:, a * depth : (a + 1) * depth] for a in range(RADIX)], small)
    row = lax.broadcasted_iota(jnp.int32, (ROWS, 1), 0)
    alive = jnp.zeros((ROWS, 1), jnp.float32)
    for r in range(block):
        alive = jnp.where(row == r, (1 - dead_ref[r]).astype(jnp.float32), alive)
    loads[3].wait()
    share = bins // RADIX
    phases = table.shape[0]
    tiles = bins // LANES
    lane = lax.broadcasted_iota(jnp.int32, (1, LANES), 1)
    parts = [None] * tiles
    energy_sum = jnp.zeros((ROWS, LANES), jnp.float32)
    for phase in range(phases):
        members = []
        for tile in range(phase, tiles, phases):
            first, last = tile * LANES // share, (tile * LANES + LANES - 1) // share
            members += [(tile, r) for r in range(first, last + 1)]
        lhs = jnp.concatenate([rows[r] for _, r in members], axis=0).astype(jnp.bfloat16)
        spec = jnp.dot(lhs, table[phase], preferred_element_type=jnp.float32)
        for tile in range(phase, tiles, phases):
            re = im = None
            for index, (which, r) in enumerate(members):
                if which != tile:
                    continue
                now = spec[index * ROWS : (index + 1) * ROWS]
                begin = r * share - tile * LANES
                re = now[:, :LANES] if re is None else jnp.where(lane >= begin, now[:, :LANES], re)
                im = now[:, LANES:] if im is None else jnp.where(lane >= begin, now[:, LANES:], im)
            energy = re * re + im * im
            energy_sum = energy_sum + energy
            parts[tile] = (re, im, energy)
    width, tail, chunks = packing(block, 2 * bins)

    def pack(start, piece):
        if start < width:
            packed[:block, start : start + LANES] = piece[:block]
            return
        for r in range(block):
            first = (r % chunks) * tail + start - width
            packed[block + r // chunks : block + r // chunks + 1, first : first + LANES] = piece[r : r + 1]

    def unpack(values, store):
        store(slice(0, block), slice(0, width), values[:block])
        for r in range(block):
            first = (r % chunks) * tail
            store(
                slice(r, r + 1), slice(width, width + tail),
                values[block + r // chunks : block + r // chunks + 1, first : first + tail],
            )

    mean_energy = jnp.sum(energy_sum, axis=-1, keepdims=True) / bins
    for tile, (re, im, energy) in enumerate(parts):
        scale = lax.rsqrt(energy + 0.25 * mean_energy + 1e-06)
        pack(tile * LANES, re * scale * alive)
        pack(bins + tile * LANES, im * scale * alive)
    own[...] = packed[...].astype(jnp.bfloat16)

    to_t = me_c // group
    slot = me_c % group
    to_half, at = slot // half, slot % half
    keeps = jnp.logical_and(to_t == me_t, to_half == core)
    split = choose(to_t, splits)
    entered = jnp.where(core == 0, split, columns - split) + 1 - jnp.logical_and(to_t == me_t, part == core).astype(jnp.int32)

    def open_gate():
        pl.semaphore_signal(gate, inc=1, device_id=(sibling, me_t), device_id_type=MESH)

    mine = to_half * columns + at * tms + me_t

    def push(i):
        return pltpu.make_async_remote_copy(
            src_ref=own, dst_ref=src.at[mine], send_sem=send_sem, recv_sem=slot_sem.at[at],
            device_id=(2 * i + to_half, to_t), device_id_type=MESH,
        )

    def start_push(i):
        @pl.when(jnp.logical_not(jnp.logical_and(keeps, i == chip)))
        def _():
            push(i).start()

    def pair_copy(step):
        return pltpu.make_async_remote_copy(
            src_ref=own, dst_ref=rec.at[me_t], send_sem=send_sem, recv_sem=rec_sem,
            device_id=(me_c, (me_t + step) % tms), device_id_type=MESH,
        )

    rec[me_t] = own[...]

    @pl.when(keeps)
    def _():
        src[mine] = own[...]

    @pl.when(core == 0)
    def _():
        pl.semaphore_wait(barrier, entered + 2 * (tms - 1))
        open_gate()

    @pl.when(core == 1)
    def _():
        pl.semaphore_wait(gate, 1)

    for q in range(max(splits)):
        @pl.when(q < split)
        def _():
            start_push(choose(to_t, [o[q] for o in orders]))

    for step in range(1, tms):
        pair_copy(step).start()

    @pl.when(core == 0)
    def _():
        pl.semaphore_wait(gate, 1)

    @pl.when(core == 1)
    def _():
        pl.semaphore_wait(barrier, entered)
        open_gate()

    for q in range(min(splits), columns):
        @pl.when(q >= split)
        def _():
            start_push(choose(to_t, [o[q] for o in orders]))


    def landed(start, count, sem):
        blocks = src.at[pl.ds(start, count)]
        return pltpu.make_async_copy(blocks, blocks, sem)

    def forward(i):
        blocks = src.at[pl.ds(core * columns + i * tms, tms)]
        return pltpu.make_async_remote_copy(
            src_ref=blocks, dst_ref=blocks, send_sem=fwd_sem, recv_sem=half_sem,
            device_id=(sibling, me_t), device_id_type=MESH,
        )

    sources = half * block

    def unpack_half(h):
        for i in range(half):
            for w in range(tms):

                def store(rows, lanes, piece):
                    srcf[w, i * block + rows.start : i * block + rows.stop, lanes] = piece

                unpack(src[h * columns + i * tms + w].astype(jnp.float32), store)

    for i in range(half):
        holds = jnp.logical_and(keeps, at == i)

        @pl.when(jnp.logical_not(holds))
        def _():
            landed(core * columns + i * tms, tms, slot_sem.at[i]).wait()

        @pl.when(holds)
        def _():
            landed(core * columns + i * tms, tms - 1, slot_sem.at[i]).wait()

        forward(i).start()
    for load in loads[4:]:
        load.wait()
    keep = maskv[...].astype(jnp.float32)
    count = keep.shape[1]
    diagonal = lax.broadcasted_iota(jnp.int32, (count, count), 0) == lax.broadcasted_iota(jnp.int32, (count, count), 1)
    for r in range(block):
        column = jnp.sum(jnp.where(diagonal, keep[r : r + 1, :], 0.0), axis=1, keepdims=True)
        kept[r] = jnp.broadcast_to(column, (count, LANES))
    pltpu.make_async_copy(rec.at[pl.ds(0, tms - 1)], rec.at[pl.ds(0, tms - 1)], rec_sem).wait()

    for w in range(tms):

        def store_rec(rows, lanes, piece):
            recf[w, rows, lanes] = piece

        unpack(rec[w].astype(jnp.float32), store_rec)

    def store(r, tile, values):
        lanes = slice(tile * LANES, tile * LANES + values.shape[1])
        rows = pl.ds(pl.multiple_of(core * sources, sources), sources)
        first_ref[r, :, lanes] = values * kept[r, rows, : values.shape[1]]

    unpack_half(core)
    correlate_sources(recf, srcf, lagv, first_ref.shape[-1], store)
    landed((1 - core) * columns, columns, half_sem).wait()
    unpack_half(1 - core)

    @pl.when(jnp.logical_not(keeps))
    def _():
        landed(0, columns + tms - 1, send_sem).wait()

    @pl.when(keeps)
    def _():
        landed(0, columns + tms - 2, send_sem).wait()

    landed(0, columns, fwd_sem).wait()


def fused_device(chans, tms, samples, dead_flags, pair_mask):
    block, _, length = samples.shape
    sources = pair_mask.shape[1]
    group = sources // block
    table, turns = split_tables(length, F)
    lag_weights = folded_lag_tables(length, bin_order(F), LAGS, 1.0 / math.sqrt(tms * F))
    at = np.arange(length)
    taper = 0.5 - 0.5 * np.cos(2.0 * np.pi * (at + 0.5) / length)
    small = np.concatenate([taper.reshape(1, RADIX, length // RADIX), turns]).astype(np.float32)
    vmem, hbm = pl.BlockSpec(memory_space=pltpu.VMEM), pl.BlockSpec(memory_space=pltpu.HBM)
    sem = pltpu.SemaphoreType.DMA
    half = group // 2
    width = packing(block, 2 * F)[0]
    stage = pl.pallas_call(
        functools.partial(fused_kernel, (chans, tms, block, group, F)),
        out_shape=[
            pltpu.VMEM((block, half * block, LAGS), jnp.float32),
            pltpu.VMEM((tms, half * block, 2 * F), jnp.float32),
            pltpu.VMEM((tms, block, 2 * F), jnp.float32),
            pltpu.VMEM(lag_weights.shape, jnp.bfloat16),
            pltpu.VMEM((block, sources, LANES), jnp.float32),
        ],
        in_specs=[hbm] * 6,
        out_specs=[vmem] * 5,
        scratch_shapes=[
            pltpu.VMEM((block, length), jnp.bfloat16),
            pltpu.SMEM((block,), jnp.int32),
            pltpu.VMEM((block, sources), jnp.int32),
            pltpu.VMEM(small.shape, jnp.float32),
            pltpu.VMEM((ROWS, length), jnp.float32),
            pltpu.VMEM((ROWS, width), jnp.float32),
            pltpu.VMEM((ROWS, width), jnp.bfloat16),
            pltpu.VMEM((chans, ROWS, width), jnp.bfloat16),
            pltpu.VMEM((tms, ROWS, width), jnp.bfloat16),
            pltpu.VMEM(table.shape, jnp.bfloat16),
            sem((3,)), sem, sem, sem((half,)), sem, sem, pltpu.SemaphoreType.REGULAR,
        ],
        compiler_params=pltpu.CompilerParams(
            collective_id=0, has_side_effects=True, vmem_limit_bytes=24 * 1024 * 1024
        ),
    )(
        *(
            pltpu.with_memory_space_constraint(operand, pltpu.HBM)
            for operand in (
                samples.reshape(block, length), dead_flags, pair_mask, jnp.asarray(small),
                jnp.asarray(table, jnp.bfloat16), jnp.asarray(lag_weights, jnp.bfloat16),
            )
        )
    )
    return pl.pallas_call(
        finish_kernel,
        out_shape=jax.ShapeDtypeStruct((block, sources, LAGS), jnp.float32),
        in_specs=[vmem] * 5,
        out_specs=vmem,
        compiler_params=pltpu.CompilerParams(vmem_limit_bytes=16 * 1024 * 1024),
    )(*stage)


def dispatch(chans, tms, samples, dead_flags, pair_mask):
    block, windows, length = samples.shape
    sources = pair_mask.shape[1]
    whole_blocks = sources % (4 * block) == 0 and chans % 4 == 0 and sources % 16 == 0 and block * chans == sources * tms
    aligned = length == RADIX * LANES and F % LANES == 0 and F % RADIX == 0 and windows == 1
    if whole_blocks and aligned and packs(block, 2 * F) and folds(LAGS):
        return fused_device(chans, tms, samples, dead_flags, pair_mask)
    return per_device(samples, dead_flags, pair_mask)


def solution(mesh):
    in_specs = (P("chan", "tm", None), P("chan"), P("chan", "tm"))
    out_specs = P("chan", "tm", None)
    chans, tms = mesh.shape["chan"], mesh.shape["tm"]
    return jax.shard_map(
        functools.partial(dispatch, chans, tms),
        mesh=mesh, in_specs=in_specs, out_specs=out_specs, check_vma=False,
    )
```

```python
import functools
import math

import jax
import jax.numpy as jnp
import numpy as np
from jax import lax
from jax.experimental import pallas as pl
from jax.experimental.pallas import tpu as pltpu
from jax.sharding import PartitionSpec as P

F = 768
LAGS = 301


def taper_window(length):
    sample_index = jnp.arange(length, dtype=jnp.float32)
    return 0.5 - 0.5 * jnp.cos(2.0 * math.pi * (sample_index + 0.5) / length)


def forward_table(length, bins):
    sample_index = jnp.arange(length, dtype=jnp.int32)
    frequency = jnp.arange(1, bins + 1, dtype=jnp.int32)
    phase_index = sample_index[:, None] * frequency[None, :] % length
    angles = 2.0 * math.pi / length * phase_index.astype(jnp.float32)
    return jnp.concatenate([jnp.cos(angles), -jnp.sin(angles)], axis=1).astype(jnp.bfloat16)


def lag_table(length, bins, lags, factor):
    frequency = jnp.arange(1, bins + 1, dtype=jnp.int32)
    shifts = jnp.arange(lags, dtype=jnp.int32) - (lags - 1) // 2
    phase_index = jnp.mod(frequency[:, None] * shifts[None, :], length)
    angles = 2.0 * math.pi / length * phase_index.astype(jnp.float32)
    table_values = jnp.concatenate([jnp.cos(angles), -jnp.sin(angles)], axis=0) * factor
    return table_values.astype(jnp.bfloat16)


def whiten(samples, dead_flags, table_values):
    channel_count, windows, length = samples.shape
    bins = table_values.shape[1] // 2
    traces = samples.astype(jnp.float32)
    traces = traces - jnp.mean(traces, axis=-1, keepdims=True)
    tapered = (traces * taper_window(length)).astype(jnp.bfloat16)
    spectra = jnp.dot(
        tapered.reshape(channel_count * windows, length),
        table_values,
        preferred_element_type=jnp.float32,
    )
    real_part = spectra[:, :bins]
    imag_part = spectra[:, bins:]
    energy = real_part * real_part + imag_part * imag_part
    mean_energy = jnp.mean(energy, axis=-1, keepdims=True)
    inverse_scale = lax.rsqrt(energy + 0.25 * mean_energy + 1e-06)
    alive_rows = jnp.repeat((1 - dead_flags).astype(jnp.float32), windows)[:, None]
    whitened = (
        jnp.concatenate([real_part * inverse_scale, imag_part * inverse_scale], axis=1) * alive_rows
    )
    return whitened.astype(jnp.bfloat16).reshape(channel_count, windows, 2 * bins)


def correlate(receivers, sources, lag_weights):
    bins = receivers.shape[-1] // 2
    rec_values = receivers.astype(jnp.float32)
    src_values = sources.astype(jnp.float32)
    rec_re = rec_values[:, None, :, :bins]
    rec_im = rec_values[:, None, :, bins:]
    src_re = src_values[None, :, :, :bins]
    src_im = src_values[None, :, :, bins:]
    cross_re = rec_re * src_re + rec_im * src_im
    cross_im = rec_im * src_re - rec_re * src_im
    cross = jnp.concatenate([cross_re, cross_im], axis=-1).astype(jnp.bfloat16)
    result = jnp.einsum("rgwk,kl->wrgl", cross, lag_weights, preferred_element_type=jnp.float32)
    return result.astype(jnp.bfloat16)


def pick_group(source_count, rows_each):
    chosen = 1
    for candidate in range(1, source_count + 1):
        if source_count % candidate == 0 and candidate * rows_each <= 1024:
            chosen = candidate
    return chosen


def per_device(samples, dead_flags, pair_mask):
    block_size, local_windows, length = samples.shape
    table_values = forward_table(length, F)
    whitened = whiten(samples, dead_flags, table_values)
    subwin = local_windows * lax.axis_size("tm")
    lag_weights = lag_table(length, F, LAGS, 1.0 / math.sqrt(subwin * F))
    incoming = lax.all_gather(whitened, "chan", axis=0, tiled=True)
    source_count = incoming.shape[0]
    group_size = pick_group(source_count, block_size * local_windows)
    grouped = incoming.reshape(source_count // group_size, group_size, local_windows, 2 * F)

    def one_group(group_sources):
        return correlate(whitened, group_sources, lag_weights)[0]

    results = lax.map(one_group, grouped)
    placed = jnp.transpose(results, (1, 0, 2, 3)).reshape(block_size, source_count, LAGS)
    shares = lax.psum_scatter(
        placed.astype(jnp.float32).astype(jnp.bfloat16), "tm", scatter_dimension=1, tiled=True
    ).astype(jnp.float32)
    return shares * pair_mask.astype(jnp.float32)[..., None]


RADIX = 16
LANES = 128
ROWS = 8
MESH = pl.DeviceIdType.MESH


def bin_order(bins):
    share = bins // RADIX
    place = np.arange(bins)
    return place // share + 1 + RADIX * (place % share)


def split_tables(length, bins):
    depth, share = length // RADIX, bins // RADIX
    phases = share // math.gcd(share, LANES)
    steps, lanes = np.arange(depth)[:, None], np.arange(LANES)[None, :]
    table = []
    for phase in range(phases):
        angle = 2.0 * np.pi / depth * (steps * ((phase * LANES + lanes) % share) % depth)
        cos, sin = np.cos(angle), np.sin(angle)
        table.append(np.block([[cos, -sin], [sin, cos]]))
    turn = 2.0 * np.pi / length * (np.arange(1, RADIX + 1)[:, None] * np.arange(depth)[None, :] % length)
    return np.stack(table), np.stack([np.cos(turn), np.sin(turn)])


def folded_lags(lags):
    middle, over = lags // 2, lags - 2 * LANES
    at = np.arange(LANES)
    return np.concatenate([LANES + at - middle, np.where(at < over, LANES, 0) + LANES + at - middle])


def folded_lag_tables(length, order, lags, factor):
    angles = 2.0 * np.pi / length * np.mod(order[:, None] * folded_lags(lags)[None, :], length)
    return (np.stack([np.cos(angles), -np.sin(angles)]) * factor).astype(np.float32)


def folds(lags):
    middle = lags // 2
    return lags % 2 == 1 and 2 * LANES < lags < 3 * LANES and LANES <= middle + 1


def packing(block, length):
    width = block * length // ROWS
    tail = length - width
    return width, tail, width // tail if tail > 0 else 0


def packs(block, length):
    width, tail, chunks = packing(block, length)
    full = block < ROWS and block * length % (ROWS * LANES) == 0
    return full and tail % LANES == 0 and width % tail == 0 and (ROWS - block) * chunks == block


def stage_one(pieces):
    half = RADIX // 2
    sums = [pieces[a] + pieces[RADIX - a] for a in range(1, half)]
    diffs = [pieces[a] - pieces[RADIX - a] for a in range(1, half)]
    even = pieces[0] + pieces[half]
    odd = pieces[0] - pieces[half]

    def real(k):
        total = even if k % 2 == 0 else odd
        for a in range(1, half):
            total = total + sums[a - 1] * float(np.cos(2 * np.pi * a * k / RADIX))
        return total

    def imag(k):
        total = diffs[0] * float(-np.sin(2 * np.pi * k / RADIX))
        for a in range(2, half):
            total = total + diffs[a - 1] * float(-np.sin(2 * np.pi * a * k / RADIX))
        return total

    return [real(k) for k in range(half + 1)], [imag(k) for k in range(1, half)]


def twisted(pieces, turns):
    half = RADIX // 2
    reals, imags = stage_one(pieces)
    rows = []
    for k in range(1, RADIX + 1):
        low = min(k, RADIX - k)
        cos, sin, re = turns[1, k - 1 : k], turns[2, k - 1 : k], reals[low]
        if low == 0 or low == half:
            rows.append(jnp.concatenate([re * cos, -re * sin], axis=1))
            continue
        im = imags[low - 1] if k < half else -imags[low - 1]
        rows.append(jnp.concatenate([re * cos + im * sin, im * cos - re * sin], axis=1))
    return rows


def correlate_sources(recf, srcf, lagv, lags, store):
    tms, block, bins = recf.shape[0], recf.shape[1], recf.shape[2] // 2
    sources = srcf.shape[1]
    even = odd = None
    for first in range(0, bins // LANES, 2):
        parts_re, parts_im = [], []
        for tile in range(first, first + 2):
            lanes = slice(tile * LANES, (tile + 1) * LANES)
            lanes_im = slice(bins + tile * LANES, bins + (tile + 1) * LANES)
            rec_re = [recf[w, :, lanes] for w in range(tms)]
            rec_im = [recf[w, :, lanes_im] for w in range(tms)]
            src_re = [srcf[w, :, lanes] for w in range(tms)]
            src_im = [srcf[w, :, lanes_im] for w in range(tms)]
            rows_re, rows_im = [], []
            for r in range(block):
                total_re = total_im = None
                for w in range(tms):
                    a, c = rec_re[w][r : r + 1, :], rec_im[w][r : r + 1, :]
                    now_re = a * src_re[w] + c * src_im[w]
                    now_im = c * src_re[w] - a * src_im[w]
                    total_re = now_re if total_re is None else total_re + now_re
                    total_im = now_im if total_im is None else total_im + now_im
                rows_re.append(total_re)
                rows_im.append(total_im)
            parts_re.append(jnp.concatenate(rows_re, axis=0).astype(jnp.bfloat16))
            parts_im.append(jnp.concatenate(rows_im, axis=0).astype(jnp.bfloat16))
        depths = slice(first * LANES, (first + 2) * LANES)
        now_even = jnp.dot(
            jnp.concatenate(parts_re, axis=1), lagv[0, depths, :], preferred_element_type=jnp.float32
        )
        now_odd = jnp.dot(
            jnp.concatenate(parts_im, axis=1), lagv[1, depths, :], preferred_element_type=jnp.float32
        )
        even = now_even if even is None else even + now_even
        odd = now_odd if odd is None else odd + now_odd
    ahead = even + odd
    behind = even[:, LANES:] - odd[:, LANES:]
    over = lags - 2 * LANES
    lane = lax.broadcasted_iota(jnp.int32, behind.shape, 1)
    behind = jnp.take_along_axis(behind, (over - 1 - lane + LANES) % LANES, axis=1)
    for r in range(block):
        rows = slice(r * sources, (r + 1) * sources)
        store(r, 0, behind[rows])
        store(r, 1, ahead[rows, :LANES])
        store(r, 2, ahead[rows, LANES : LANES + over])


def finish_kernel(first_ref, srcf, recf, lagv, kept, out_ref):
    other = 1 - lax.axis_index("chan") % 2
    block, sources, lags = first_ref.shape
    begin = pl.multiple_of((1 - other) * sources, sources)
    place = pl.ds(pl.multiple_of(other * sources, sources), sources)

    def store(r, tile, values):
        lanes = slice(tile * LANES, tile * LANES + values.shape[1])
        out_ref[r, place, lanes] = values * kept[r, place, : values.shape[1]]

    correlate_sources(recf, srcf, lagv, lags, store)
    for r in range(block):
        out_ref[r, pl.ds(begin, sources), :] = first_ref[r]


def push_orders(columns):
    near, far = list(range(columns // 2)), list(range(columns // 2, columns))
    return [near + far[0::2] + far[1::2], near + far]


def fused_kernel(
    sizes, samples_hbm, dead_hbm, mask_hbm, small_hbm, table_ref, lag_ref,
    first_ref, srcf, recf, lagv, kept,
    samples_ref, dead_ref, maskv, small, padded, packed, own, src, rec, table,
    load_sem, send_sem, fwd_sem, slot_sem, half_sem, rec_sem, gate, ready,
):
    chans, tms, block, group, bins = sizes
    me_c, me_t = lax.axis_index("chan"), lax.axis_index("tm")
    core = me_c % 2
    columns = chans // 2
    barrier = pltpu.get_barrier_semaphore()
    sibling = me_c + 1 - 2 * core
    half = group // 2
    chip = me_c // 2
    orders = push_orders(columns)
    splits = [columns // 2 + 1, 1]

    def choose(t, values):
        return jnp.where(t == 0, values[0], values[1])

    def is_late(t, at):
        late = [functools.reduce(jnp.logical_or, [at == i for i in o[n:]]) for o, n in zip(orders, splits)]
        return jnp.where(t == 0, late[0].astype(jnp.int32), late[1].astype(jnp.int32))

    part = is_late(me_t, chip)
    home_late = jnp.logical_and(me_t == 1, chip >= columns // 2)
    told_later = jnp.logical_and(home_late, core == 0)
    for i in range(half // 2):
        for w in range(tms):
            from_chip = (me_t * group + core * half) // 2 + i
            own_chip = jnp.logical_and(from_chip == chip, w == me_t)

            @pl.when(jnp.logical_not(jnp.logical_or(own_chip, told_later)))
            def _():
                pl.semaphore_signal(
                    barrier, inc=1, device_id=(2 * from_chip + part, w), device_id_type=MESH
                )

    for step in range(1, tms):
        pl.semaphore_signal(
            barrier, inc=1, device_id=(2 * chip, (me_t + step) % tms), device_id_type=MESH
        )
    pl.semaphore_signal(barrier, inc=1, device_id=(sibling, me_t), device_id_type=MESH)
    to_t = me_c // group
    slot = me_c % group
    to_half, at = slot // half, slot % half
    inner = jnp.logical_and(to_t == 1, to_half == 0)
    for i in range(columns // 2, columns):

        @pl.when(inner & (core == 0) & jnp.logical_not((me_t == 1) & (chip == i)))
        def _():
            pl.semaphore_signal(barrier, inc=1, device_id=(2 * i + 1, 1), device_id_type=MESH)


    length = samples_ref.shape[-1]
    depth = length // RADIX
    loads = [
        pltpu.make_async_copy(samples_hbm, samples_ref, load_sem.at[0]),
        pltpu.make_async_copy(small_hbm, small, load_sem.at[0]),
        pltpu.make_async_copy(dead_hbm, dead_ref, load_sem.at[0]),
        pltpu.make_async_copy(table_ref, table, load_sem.at[1]),
        pltpu.make_async_copy(mask_hbm, maskv, load_sem.at[2]),
        pltpu.make_async_copy(lag_ref, lagv, load_sem.at[2]),
    ]
    for load in loads:
        load.start()

    for load in loads[:3]:
        load.wait()
    traces = samples_ref[...].astype(jnp.float32)
    traces = traces - jnp.mean(traces, axis=-1, keepdims=True)
    padded[block:, :] = jnp.zeros((ROWS - block, length), jnp.float32)
    for a in range(RADIX):
        lanes = slice(a * depth, (a + 1) * depth)
        padded[:block, lanes] = (traces[:, lanes] * small[0, a : a + 1]).astype(jnp.bfloat16).astype(jnp.float32)
    rows = twisted([padded[:, a * depth : (a + 1) * depth] for a in range(RADIX)], small)
    row = lax.broadcasted_iota(jnp.int32, (ROWS, 1), 0)
    alive = jnp.zeros((ROWS, 1), jnp.float32)
    for r in range(block):
        alive = jnp.where(row == r, (1 - dead_ref[r]).astype(jnp.float32), alive)
    loads[3].wait()
    share = bins // RADIX
    phases = table.shape[0]
    tiles = bins // LANES
    lane = lax.broadcasted_iota(jnp.int32, (1, LANES), 1)
    parts = [None] * tiles
    energy_sum = jnp.zeros((ROWS, LANES), jnp.float32)
    for phase in range(phases):
        members = []
        for tile in range(phase, tiles, phases):
            first, last = tile * LANES // share, (tile * LANES + LANES - 1) // share
            members += [(tile, r) for r in range(first, last + 1)]
        lhs = jnp.concatenate([rows[r] for _, r in members], axis=0).astype(jnp.bfloat16)
        spec = jnp.dot(lhs, table[phase], preferred_element_type=jnp.float32)
        for tile in range(phase, tiles, phases):
            re = im = None
            for index, (which, r) in enumerate(members):
                if which != tile:
                    continue
                now = spec[index * ROWS : (index + 1) * ROWS]
                begin = r * share - tile * LANES
                re = now[:, :LANES] if re is None else jnp.where(lane >= begin, now[:, :LANES], re)
                im = now[:, LANES:] if im is None else jnp.where(lane >= begin, now[:, LANES:], im)
            energy = re * re + im * im
            energy_sum = energy_sum + energy
            parts[tile] = (re, im, energy)
    width, tail, chunks = packing(block, 2 * bins)

    def pack(start, piece):
        if start < width:
            packed[:block, start : start + LANES] = piece[:block]
            return
        for r in range(block):
            first = (r % chunks) * tail + start - width
            packed[block + r // chunks : block + r // chunks + 1, first : first + LANES] = piece[r : r + 1]

    def unpack(values, store):
        store(slice(0, block), slice(0, width), values[:block])
        for r in range(block):
            first = (r % chunks) * tail
            store(
                slice(r, r + 1), slice(width, width + tail),
                values[block + r // chunks : block + r // chunks + 1, first : first + tail],
            )

    mean_energy = jnp.sum(energy_sum, axis=-1, keepdims=True) / bins
    for tile, (re, im, energy) in enumerate(parts):
        scale = lax.rsqrt(energy + 0.25 * mean_energy + 1e-06)
        pack(tile * LANES, re * scale * alive)
        pack(bins + tile * LANES, im * scale * alive)
    own[...] = packed[...].astype(jnp.bfloat16)

    keeps = jnp.logical_and(to_t == me_t, to_half == core)
    split = choose(to_t, splits)
    until = jnp.where(inner, columns // 2, columns)
    in_part = jnp.logical_and(to_t == me_t, jnp.logical_and(part == core, jnp.logical_not(jnp.logical_and(inner, core == 1))))
    entered = jnp.where(core == 0, split + 2 * (tms - 1), until - split) + 1 - in_part.astype(jnp.int32)
    greeted = half // 2 * tms - inner.astype(jnp.int32)
    entered = entered + jnp.where(jnp.logical_and(home_late, core == 1), greeted, 0)

    def open_gate():
        pl.semaphore_signal(gate, inc=1, device_id=(sibling, me_t), device_id_type=MESH)

    mine = to_half * columns + at * tms + me_t

    def push(i):
        return pltpu.make_async_remote_copy(
            src_ref=own, dst_ref=src.at[mine], send_sem=send_sem, recv_sem=slot_sem.at[at],
            device_id=(2 * i + to_half, to_t), device_id_type=MESH,
        )

    def start_push(i):
        @pl.when(jnp.logical_not(jnp.logical_and(keeps, i == chip)))
        def _():
            push(i).start()

    def pair_copy(step):
        return pltpu.make_async_remote_copy(
            src_ref=own, dst_ref=rec.at[me_t], send_sem=send_sem, recv_sem=rec_sem,
            device_id=(me_c, (me_t + step) % tms), device_id_type=MESH,
        )

    rec[me_t] = own[...]

    @pl.when(keeps)
    def _():
        src[mine] = own[...]

    @pl.when(core == 0)
    def _():
        pl.semaphore_wait(barrier, entered)
        open_gate()

    @pl.when(core == 1)
    def _():
        pl.semaphore_wait(gate, 1)

    for q in range(max(splits)):
        @pl.when(q < split)
        def _():
            start_push(choose(to_t, [o[q] for o in orders]))

    for step in range(1, tms):
        pair_copy(step).start()

    @pl.when(core == 0)
    def _():
        pl.semaphore_wait(gate, 1)

    @pl.when(core == 1)
    def _():
        pl.semaphore_wait(barrier, entered)
        open_gate()

    for q in range(min(splits), columns):

        @pl.when(jnp.logical_and(q >= split, q < until))
        def _():
            start_push(choose(to_t, [o[q] for o in orders]))

    for i in range(half // 2):
        for w in range(tms):
            to_chip = group // 2 + i

            @pl.when(home_late & (core == 1) & jnp.logical_not((to_chip == chip) & (w == me_t)))
            def _():
                pl.semaphore_signal(ready, inc=1, device_id=(2 * to_chip, w), device_id_type=MESH)

    @pl.when(jnp.logical_and(inner, core == 0))
    def _():
        pl.semaphore_wait(ready, columns // 2 - (me_t == 1).astype(jnp.int32))
        open_gate()

    @pl.when(jnp.logical_and(inner, core == 1))
    def _():
        pl.semaphore_wait(gate, 1)

    for i in range(columns // 2, columns):

        @pl.when(inner)
        def _():
            start_push(i)

    def landed(start, count, sem):
        blocks = src.at[pl.ds(start, count)]
        return pltpu.make_async_copy(blocks, blocks, sem)

    def forward(i):
        blocks = src.at[pl.ds(core * columns + i * tms, tms)]
        return pltpu.make_async_remote_copy(
            src_ref=blocks, dst_ref=blocks, send_sem=fwd_sem, recv_sem=half_sem,
            device_id=(sibling, me_t), device_id_type=MESH,
        )

    sources = half * block

    def unpack_half(h):
        for i in range(half):
            for w in range(tms):

                def store(rows, lanes, piece):
                    srcf[w, i * block + rows.start : i * block + rows.stop, lanes] = piece

                unpack(src[h * columns + i * tms + w].astype(jnp.float32), store)

    for i in range(half):
        holds = jnp.logical_and(keeps, at == i)

        @pl.when(jnp.logical_not(holds))
        def _():
            landed(core * columns + i * tms, tms, slot_sem.at[i]).wait()

        @pl.when(holds)
        def _():
            landed(core * columns + i * tms, tms - 1, slot_sem.at[i]).wait()

        forward(i).start()
    for load in loads[4:]:
        load.wait()
    keep = maskv[...].astype(jnp.float32)
    count = keep.shape[1]
    diagonal = lax.broadcasted_iota(jnp.int32, (count, count), 0) == lax.broadcasted_iota(jnp.int32, (count, count), 1)
    for r in range(block):
        column = jnp.sum(jnp.where(diagonal, keep[r : r + 1, :], 0.0), axis=1, keepdims=True)
        kept[r] = jnp.broadcast_to(column, (count, LANES))
    pltpu.make_async_copy(rec.at[pl.ds(0, tms - 1)], rec.at[pl.ds(0, tms - 1)], rec_sem).wait()

    for w in range(tms):

        def store_rec(rows, lanes, piece):
            recf[w, rows, lanes] = piece

        unpack(rec[w].astype(jnp.float32), store_rec)

    def store(r, tile, values):
        lanes = slice(tile * LANES, tile * LANES + values.shape[1])
        rows = pl.ds(pl.multiple_of(core * sources, sources), sources)
        first_ref[r, :, lanes] = values * kept[r, rows, : values.shape[1]]

    unpack_half(core)
    correlate_sources(recf, srcf, lagv, first_ref.shape[-1], store)
    landed((1 - core) * columns, columns, half_sem).wait()
    unpack_half(1 - core)

    @pl.when(jnp.logical_not(keeps))
    def _():
        landed(0, columns + tms - 1, send_sem).wait()

    @pl.when(keeps)
    def _():
        landed(0, columns + tms - 2, send_sem).wait()

    landed(0, columns, fwd_sem).wait()


def fused_device(chans, tms, samples, dead_flags, pair_mask):
    block, _, length = samples.shape
    sources = pair_mask.shape[1]
    group = sources // block
    table, turns = split_tables(length, F)
    lag_weights = folded_lag_tables(length, bin_order(F), LAGS, 1.0 / math.sqrt(tms * F))
    at = np.arange(length)
    taper = 0.5 - 0.5 * np.cos(2.0 * np.pi * (at + 0.5) / length)
    small = np.concatenate([taper.reshape(1, RADIX, length // RADIX), turns]).astype(np.float32)
    vmem, hbm = pl.BlockSpec(memory_space=pltpu.VMEM), pl.BlockSpec(memory_space=pltpu.HBM)
    sem = pltpu.SemaphoreType.DMA
    half = group // 2
    width = packing(block, 2 * F)[0]
    stage = pl.pallas_call(
        functools.partial(fused_kernel, (chans, tms, block, group, F)),
        out_shape=[
            pltpu.VMEM((block, half * block, LAGS), jnp.float32),
            pltpu.VMEM((tms, half * block, 2 * F), jnp.float32),
            pltpu.VMEM((tms, block, 2 * F), jnp.float32),
            pltpu.VMEM(lag_weights.shape, jnp.bfloat16),
            pltpu.VMEM((block, sources, LANES), jnp.float32),
        ],
        in_specs=[hbm] * 6,
        out_specs=[vmem] * 5,
        scratch_shapes=[
            pltpu.VMEM((block, length), jnp.bfloat16),
            pltpu.SMEM((block,), jnp.int32),
            pltpu.VMEM((block, sources), jnp.int32),
            pltpu.VMEM(small.shape, jnp.float32),
            pltpu.VMEM((ROWS, length), jnp.float32),
            pltpu.VMEM((ROWS, width), jnp.float32),
            pltpu.VMEM((ROWS, width), jnp.bfloat16),
            pltpu.VMEM((chans, ROWS, width), jnp.bfloat16),
            pltpu.VMEM((tms, ROWS, width), jnp.bfloat16),
            pltpu.VMEM(table.shape, jnp.bfloat16),
            sem((3,)), sem, sem, sem((half,)), sem, sem, pltpu.SemaphoreType.REGULAR, pltpu.SemaphoreType.REGULAR,
        ],
        compiler_params=pltpu.CompilerParams(
            collective_id=0, has_side_effects=True, vmem_limit_bytes=24 * 1024 * 1024
        ),
    )(
        *(
            pltpu.with_memory_space_constraint(operand, pltpu.HBM)
            for operand in (
                samples.reshape(block, length), dead_flags, pair_mask, jnp.asarray(small),
                jnp.asarray(table, jnp.bfloat16), jnp.asarray(lag_weights, jnp.bfloat16),
            )
        )
    )
    return pl.pallas_call(
        finish_kernel,
        out_shape=jax.ShapeDtypeStruct((block, sources, LAGS), jnp.float32),
        in_specs=[vmem] * 5,
        out_specs=vmem,
        compiler_params=pltpu.CompilerParams(vmem_limit_bytes=16 * 1024 * 1024),
    )(*stage)


def dispatch(chans, tms, samples, dead_flags, pair_mask):
    block, windows, length = samples.shape
    sources = pair_mask.shape[1]
    whole_blocks = sources % (4 * block) == 0 and chans % 8 == 0 and tms == 2 and sources % 16 == 0 and block * chans == sources * tms
    aligned = length == RADIX * LANES and F % LANES == 0 and F % RADIX == 0 and windows == 1
    if whole_blocks and aligned and packs(block, 2 * F) and folds(LAGS):
        return fused_device(chans, tms, samples, dead_flags, pair_mask)
    return per_device(samples, dead_flags, pair_mask)


def solution(mesh):
    in_specs = (P("chan", "tm", None), P("chan"), P("chan", "tm"))
    out_specs = P("chan", "tm", None)
    chans, tms = mesh.shape["chan"], mesh.shape["tm"]
    return jax.shard_map(
        functools.partial(dispatch, chans, tms),
        mesh=mesh, in_specs=in_specs, out_specs=out_specs, check_vma=False,
    )
```

```python
import functools
import math

import jax
import jax.numpy as jnp
import numpy as np
from jax import lax
from jax.experimental import pallas as pl
from jax.experimental.pallas import tpu as pltpu
from jax.sharding import PartitionSpec as P

F = 768
LAGS = 301


def taper_window(length):
    sample_index = jnp.arange(length, dtype=jnp.float32)
    return 0.5 - 0.5 * jnp.cos(2.0 * math.pi * (sample_index + 0.5) / length)


def forward_table(length, bins):
    sample_index = jnp.arange(length, dtype=jnp.int32)
    frequency = jnp.arange(1, bins + 1, dtype=jnp.int32)
    phase_index = sample_index[:, None] * frequency[None, :] % length
    angles = 2.0 * math.pi / length * phase_index.astype(jnp.float32)
    return jnp.concatenate([jnp.cos(angles), -jnp.sin(angles)], axis=1).astype(jnp.bfloat16)


def lag_table(length, bins, lags, factor):
    frequency = jnp.arange(1, bins + 1, dtype=jnp.int32)
    shifts = jnp.arange(lags, dtype=jnp.int32) - (lags - 1) // 2
    phase_index = jnp.mod(frequency[:, None] * shifts[None, :], length)
    angles = 2.0 * math.pi / length * phase_index.astype(jnp.float32)
    table_values = jnp.concatenate([jnp.cos(angles), -jnp.sin(angles)], axis=0) * factor
    return table_values.astype(jnp.bfloat16)


def whiten(samples, dead_flags, table_values):
    channel_count, windows, length = samples.shape
    bins = table_values.shape[1] // 2
    traces = samples.astype(jnp.float32)
    traces = traces - jnp.mean(traces, axis=-1, keepdims=True)
    tapered = (traces * taper_window(length)).astype(jnp.bfloat16)
    spectra = jnp.dot(
        tapered.reshape(channel_count * windows, length),
        table_values,
        preferred_element_type=jnp.float32,
    )
    real_part = spectra[:, :bins]
    imag_part = spectra[:, bins:]
    energy = real_part * real_part + imag_part * imag_part
    mean_energy = jnp.mean(energy, axis=-1, keepdims=True)
    inverse_scale = lax.rsqrt(energy + 0.25 * mean_energy + 1e-06)
    alive_rows = jnp.repeat((1 - dead_flags).astype(jnp.float32), windows)[:, None]
    whitened = (
        jnp.concatenate([real_part * inverse_scale, imag_part * inverse_scale], axis=1) * alive_rows
    )
    return whitened.astype(jnp.bfloat16).reshape(channel_count, windows, 2 * bins)


def correlate(receivers, sources, lag_weights):
    bins = receivers.shape[-1] // 2
    rec_values = receivers.astype(jnp.float32)
    src_values = sources.astype(jnp.float32)
    rec_re = rec_values[:, None, :, :bins]
    rec_im = rec_values[:, None, :, bins:]
    src_re = src_values[None, :, :, :bins]
    src_im = src_values[None, :, :, bins:]
    cross_re = rec_re * src_re + rec_im * src_im
    cross_im = rec_im * src_re - rec_re * src_im
    cross = jnp.concatenate([cross_re, cross_im], axis=-1).astype(jnp.bfloat16)
    result = jnp.einsum("rgwk,kl->wrgl", cross, lag_weights, preferred_element_type=jnp.float32)
    return result.astype(jnp.bfloat16)


def pick_group(source_count, rows_each):
    chosen = 1
    for candidate in range(1, source_count + 1):
        if source_count % candidate == 0 and candidate * rows_each <= 1024:
            chosen = candidate
    return chosen


def per_device(samples, dead_flags, pair_mask):
    block_size, local_windows, length = samples.shape
    table_values = forward_table(length, F)
    whitened = whiten(samples, dead_flags, table_values)
    subwin = local_windows * lax.axis_size("tm")
    lag_weights = lag_table(length, F, LAGS, 1.0 / math.sqrt(subwin * F))
    incoming = lax.all_gather(whitened, "chan", axis=0, tiled=True)
    source_count = incoming.shape[0]
    group_size = pick_group(source_count, block_size * local_windows)
    grouped = incoming.reshape(source_count // group_size, group_size, local_windows, 2 * F)

    def one_group(group_sources):
        return correlate(whitened, group_sources, lag_weights)[0]

    results = lax.map(one_group, grouped)
    placed = jnp.transpose(results, (1, 0, 2, 3)).reshape(block_size, source_count, LAGS)
    shares = lax.psum_scatter(
        placed.astype(jnp.float32).astype(jnp.bfloat16), "tm", scatter_dimension=1, tiled=True
    ).astype(jnp.float32)
    return shares * pair_mask.astype(jnp.float32)[..., None]


RADIX = 16
LANES = 128
ROWS = 8
MESH = pl.DeviceIdType.MESH


def bin_order(bins):
    share = bins // RADIX
    place = np.arange(bins)
    return place // share + 1 + RADIX * (place % share)


def split_tables(length, bins):
    depth, share = length // RADIX, bins // RADIX
    phases = share // math.gcd(share, LANES)
    steps, lanes = np.arange(depth)[:, None], np.arange(LANES)[None, :]
    table = []
    for phase in range(phases):
        angle = 2.0 * np.pi / depth * (steps * ((phase * LANES + lanes) % share) % depth)
        cos, sin = np.cos(angle), np.sin(angle)
        table.append(np.block([[cos, -sin], [sin, cos]]))
    turn = 2.0 * np.pi / length * (np.arange(1, RADIX + 1)[:, None] * np.arange(depth)[None, :] % length)
    return np.stack(table), np.stack([np.cos(turn), np.sin(turn)])


def folded_lags(lags):
    middle, over = lags // 2, lags - 2 * LANES
    at = np.arange(LANES)
    return np.concatenate([LANES + at - middle, np.where(at < over, LANES, 0) + LANES + at - middle])


def folded_lag_tables(length, order, lags, factor):
    angles = 2.0 * np.pi / length * np.mod(order[:, None] * folded_lags(lags)[None, :], length)
    return (np.stack([np.cos(angles), -np.sin(angles)]) * factor).astype(np.float32)


def folds(lags):
    middle = lags // 2
    return lags % 2 == 1 and 2 * LANES < lags < 3 * LANES and LANES <= middle + 1


def packing(block, length):
    width = block * length // ROWS
    tail = length - width
    return width, tail, width // tail if tail > 0 else 0


def packs(block, length):
    width, tail, chunks = packing(block, length)
    full = block < ROWS and block * length % (ROWS * LANES) == 0
    return full and tail % LANES == 0 and width % tail == 0 and (ROWS - block) * chunks == block


def stage_one(pieces):
    half = RADIX // 2
    sums = [pieces[a] + pieces[RADIX - a] for a in range(1, half)]
    diffs = [pieces[a] - pieces[RADIX - a] for a in range(1, half)]
    even = pieces[0] + pieces[half]
    odd = pieces[0] - pieces[half]

    def real(k):
        total = even if k % 2 == 0 else odd
        for a in range(1, half):
            total = total + sums[a - 1] * float(np.cos(2 * np.pi * a * k / RADIX))
        return total

    def imag(k):
        total = diffs[0] * float(-np.sin(2 * np.pi * k / RADIX))
        for a in range(2, half):
            total = total + diffs[a - 1] * float(-np.sin(2 * np.pi * a * k / RADIX))
        return total

    return [real(k) for k in range(half + 1)], [imag(k) for k in range(1, half)]


def twisted(pieces, turns):
    half = RADIX // 2
    reals, imags = stage_one(pieces)
    rows = []
    for k in range(1, RADIX + 1):
        low = min(k, RADIX - k)
        cos, sin, re = turns[1, k - 1 : k], turns[2, k - 1 : k], reals[low]
        if low == 0 or low == half:
            rows.append(jnp.concatenate([re * cos, -re * sin], axis=1))
            continue
        im = imags[low - 1] if k < half else -imags[low - 1]
        rows.append(jnp.concatenate([re * cos + im * sin, im * cos - re * sin], axis=1))
    return rows


def correlate_sources(recf, srcf, lagv, lags, store):
    tms, block, bins = recf.shape[0], recf.shape[1], recf.shape[2] // 2
    sources = srcf.shape[1]
    even = odd = None
    for first in range(0, bins // LANES, 2):
        parts_re, parts_im = [], []
        for tile in range(first, first + 2):
            lanes = slice(tile * LANES, (tile + 1) * LANES)
            lanes_im = slice(bins + tile * LANES, bins + (tile + 1) * LANES)
            rec_re = [recf[w, :, lanes] for w in range(tms)]
            rec_im = [recf[w, :, lanes_im] for w in range(tms)]
            src_re = [srcf[w, :, lanes] for w in range(tms)]
            src_im = [srcf[w, :, lanes_im] for w in range(tms)]
            rows_re, rows_im = [], []
            for r in range(block):
                total_re = total_im = None
                for w in range(tms):
                    a, c = rec_re[w][r : r + 1, :], rec_im[w][r : r + 1, :]
                    now_re = a * src_re[w] + c * src_im[w]
                    now_im = c * src_re[w] - a * src_im[w]
                    total_re = now_re if total_re is None else total_re + now_re
                    total_im = now_im if total_im is None else total_im + now_im
                rows_re.append(total_re)
                rows_im.append(total_im)
            parts_re.append(jnp.concatenate(rows_re, axis=0).astype(jnp.bfloat16))
            parts_im.append(jnp.concatenate(rows_im, axis=0).astype(jnp.bfloat16))
        depths = slice(first * LANES, (first + 2) * LANES)
        now_even = jnp.dot(
            jnp.concatenate(parts_re, axis=1), lagv[0, depths, :], preferred_element_type=jnp.float32
        )
        now_odd = jnp.dot(
            jnp.concatenate(parts_im, axis=1), lagv[1, depths, :], preferred_element_type=jnp.float32
        )
        even = now_even if even is None else even + now_even
        odd = now_odd if odd is None else odd + now_odd
    ahead = even + odd
    behind = even[:, LANES:] - odd[:, LANES:]
    over = lags - 2 * LANES
    lane = lax.broadcasted_iota(jnp.int32, behind.shape, 1)
    behind = jnp.take_along_axis(behind, (over - 1 - lane + LANES) % LANES, axis=1)
    for r in range(block):
        rows = slice(r * sources, (r + 1) * sources)
        store(r, 0, behind[rows])
        store(r, 1, ahead[rows, :LANES])
        store(r, 2, ahead[rows, LANES : LANES + over])


def finish_kernel(first_ref, srcf, recf, lagv, kept, out_ref):
    other = 1 - lax.axis_index("chan") % 2
    block, sources, lags = first_ref.shape
    begin = pl.multiple_of((1 - other) * sources, sources)
    place = pl.ds(pl.multiple_of(other * sources, sources), sources)

    def store(r, tile, values):
        lanes = slice(tile * LANES, tile * LANES + values.shape[1])
        out_ref[r, place, lanes] = values * kept[r, place, : values.shape[1]]

    correlate_sources(recf, srcf, lagv, lags, store)
    for r in range(block):
        out_ref[r, pl.ds(begin, sources), :] = first_ref[r]


def push_orders(columns):
    near, far = list(range(columns // 2)), list(range(columns // 2, columns))
    return [near + far[0::2] + far[1::2], near + far]


def fused_kernel(
    sizes, samples_hbm, dead_hbm, mask_hbm, small_hbm, table_ref, lag_ref,
    first_ref, srcf, recf, lagv, kept,
    samples_ref, dead_ref, maskv, small, padded, packed, own, src, rec, table,
    load_sem, send_sem, fwd_sem, slot_sem, half_sem, rec_sem, gate, ready,
):
    chans, tms, block, group, bins = sizes
    me_c, me_t = lax.axis_index("chan"), lax.axis_index("tm")
    core = me_c % 2
    columns = chans // 2
    barrier = pltpu.get_barrier_semaphore()
    sibling = me_c + 1 - 2 * core
    half = group // 2
    chip = me_c // 2
    orders = push_orders(columns)
    splits = [columns // 2 + 1, 1]

    def choose(t, values):
        return jnp.where(t == 0, values[0], values[1])

    def is_late(t, at):
        late = [functools.reduce(jnp.logical_or, [at == i for i in o[n:]]) for o, n in zip(orders, splits)]
        return jnp.where(t == 0, late[0].astype(jnp.int32), late[1].astype(jnp.int32))

    part = is_late(me_t, chip)
    home_late = jnp.logical_and(me_t == 1, chip >= columns // 2)
    told_later = jnp.logical_and(home_late, core == 0)
    for i in range(half // 2):
        for w in range(tms):
            from_chip = (me_t * group + core * half) // 2 + i
            own_chip = jnp.logical_and(from_chip == chip, w == me_t)

            @pl.when(jnp.logical_not(jnp.logical_or(own_chip, told_later)))
            def _():
                pl.semaphore_signal(
                    barrier, inc=1, device_id=(2 * from_chip + part, w), device_id_type=MESH
                )

    for step in range(1, tms):
        pl.semaphore_signal(
            barrier, inc=1, device_id=(2 * chip, (me_t + step) % tms), device_id_type=MESH
        )
    pl.semaphore_signal(barrier, inc=1, device_id=(sibling, me_t), device_id_type=MESH)
    to_t = me_c // group
    slot = me_c % group
    to_half, at = slot // half, slot % half
    inner = jnp.logical_and(to_t == 1, to_half == 0)
    for i in range(columns // 2, columns):

        @pl.when(inner & (core == 0) & jnp.logical_not((me_t == 1) & (chip == i)))
        def _():
            pl.semaphore_signal(barrier, inc=1, device_id=(2 * i + 1, 1), device_id_type=MESH)


    length = samples_ref.shape[-1]
    depth = length // RADIX
    loads = [
        pltpu.make_async_copy(samples_hbm, samples_ref, load_sem.at[0]),
        pltpu.make_async_copy(small_hbm, small, load_sem.at[0]),
        pltpu.make_async_copy(dead_hbm, dead_ref, load_sem.at[0]),
        pltpu.make_async_copy(table_ref, table, load_sem.at[1]),
        pltpu.make_async_copy(mask_hbm, maskv, load_sem.at[2]),
        pltpu.make_async_copy(lag_ref, lagv, load_sem.at[2]),
    ]
    for load in loads:
        load.start()

    for load in loads[:3]:
        load.wait()
    traces = samples_ref[...].astype(jnp.float32)
    traces = traces - jnp.mean(traces, axis=-1, keepdims=True)
    padded[block:, :] = jnp.zeros((ROWS - block, length), jnp.float32)
    for a in range(RADIX):
        lanes = slice(a * depth, (a + 1) * depth)
        padded[:block, lanes] = (traces[:, lanes] * small[0, a : a + 1]).astype(jnp.bfloat16).astype(jnp.float32)
    rows = twisted([padded[:, a * depth : (a + 1) * depth] for a in range(RADIX)], small)
    row = lax.broadcasted_iota(jnp.int32, (ROWS, 1), 0)
    alive = jnp.zeros((ROWS, 1), jnp.float32)
    for r in range(block):
        alive = jnp.where(row == r, (1 - dead_ref[r]).astype(jnp.float32), alive)
    loads[3].wait()
    share = bins // RADIX
    phases = table.shape[0]
    tiles = bins // LANES
    lane = lax.broadcasted_iota(jnp.int32, (1, LANES), 1)
    parts = [None] * tiles
    energy_sum = jnp.zeros((ROWS, LANES), jnp.float32)
    for phase in range(phases):
        members = []
        for tile in range(phase, tiles, phases):
            first, last = tile * LANES // share, (tile * LANES + LANES - 1) // share
            members += [(tile, r) for r in range(first, last + 1)]
        lhs = jnp.concatenate([rows[r] for _, r in members], axis=0).astype(jnp.bfloat16)
        spec = jnp.dot(lhs, table[phase], preferred_element_type=jnp.float32)
        for tile in range(phase, tiles, phases):
            re = im = None
            for index, (which, r) in enumerate(members):
                if which != tile:
                    continue
                now = spec[index * ROWS : (index + 1) * ROWS]
                begin = r * share - tile * LANES
                re = now[:, :LANES] if re is None else jnp.where(lane >= begin, now[:, :LANES], re)
                im = now[:, LANES:] if im is None else jnp.where(lane >= begin, now[:, LANES:], im)
            energy = re * re + im * im
            energy_sum = energy_sum + energy
            parts[tile] = (re, im, energy)
    width, tail, chunks = packing(block, 2 * bins)

    def pack(start, piece):
        if start < width:
            packed[:block, start : start + LANES] = piece[:block]
            return
        for r in range(block):
            first = (r % chunks) * tail + start - width
            packed[block + r // chunks : block + r // chunks + 1, first : first + LANES] = piece[r : r + 1]

    def unpack(values, store):
        store(slice(0, block), slice(0, width), values[:block])
        for r in range(block):
            first = (r % chunks) * tail
            store(
                slice(r, r + 1), slice(width, width + tail),
                values[block + r // chunks : block + r // chunks + 1, first : first + tail],
            )

    mean_energy = jnp.sum(energy_sum, axis=-1, keepdims=True) / bins
    for tile, (re, im, energy) in enumerate(parts):
        scale = lax.rsqrt(energy + 0.25 * mean_energy + 1e-06)
        pack(tile * LANES, re * scale * alive)
        pack(bins + tile * LANES, im * scale * alive)
    own[...] = packed[...].astype(jnp.bfloat16)

    keeps = jnp.logical_and(to_t == me_t, to_half == core)
    split = choose(to_t, splits)
    until = jnp.where(inner, columns // 2, columns)
    in_part = jnp.logical_and(to_t == me_t, jnp.logical_and(part == core, jnp.logical_not(jnp.logical_and(inner, core == 1))))
    entered = jnp.where(core == 0, split + 2 * (tms - 1), until - split) + 1 - in_part.astype(jnp.int32)
    greeted = half // 2 * tms - inner.astype(jnp.int32)
    entered = entered + jnp.where(jnp.logical_and(home_late, core == 1), greeted, 0)

    def open_gate():
        pl.semaphore_signal(gate, inc=1, device_id=(sibling, me_t), device_id_type=MESH)

    mine = to_half * columns + at * tms + me_t

    def push(i):
        return pltpu.make_async_remote_copy(
            src_ref=own, dst_ref=src.at[mine], send_sem=send_sem, recv_sem=slot_sem.at[at],
            device_id=(2 * i + to_half, to_t), device_id_type=MESH,
        )

    def start_push(i):
        @pl.when(jnp.logical_not(jnp.logical_and(keeps, i == chip)))
        def _():
            push(i).start()

    def pair_copy(step):
        return pltpu.make_async_remote_copy(
            src_ref=own, dst_ref=rec.at[me_t], send_sem=send_sem, recv_sem=rec_sem,
            device_id=(me_c, (me_t + step) % tms), device_id_type=MESH,
        )

    rec[me_t] = own[...]

    @pl.when(keeps)
    def _():
        src[mine] = own[...]

    @pl.when(core == 0)
    def _():
        pl.semaphore_wait(barrier, entered)
        open_gate()

    @pl.when(core == 1)
    def _():
        pl.semaphore_wait(gate, 1)

    for q in range(max(splits)):
        @pl.when(q < split)
        def _():
            start_push(choose(to_t, [o[q] for o in orders]))

    for step in range(1, tms):
        pair_copy(step).start()

    @pl.when(core == 0)
    def _():
        pl.semaphore_wait(gate, 1)

    @pl.when(core == 1)
    def _():
        pl.semaphore_wait(barrier, entered)
        open_gate()

    for q in range(min(splits), columns):

        @pl.when(jnp.logical_and(q >= split, q < until))
        def _():
            start_push(choose(to_t, [o[q] for o in orders]))

    for i in range(half // 2):
        for w in range(tms):
            to_chip = group // 2 + i

            @pl.when(home_late & (core == 1) & jnp.logical_not((to_chip == chip) & (w == me_t)))
            def _():
                pl.semaphore_signal(ready, inc=1, device_id=(2 * to_chip, w), device_id_type=MESH)

    @pl.when(jnp.logical_and(inner, core == 0))
    def _():
        pl.semaphore_wait(ready, columns // 2 - (me_t == 1).astype(jnp.int32))
        open_gate()

    @pl.when(jnp.logical_and(inner, core == 1))
    def _():
        pl.semaphore_wait(gate, 1)

    for i in range(columns // 2, columns):

        @pl.when(inner)
        def _():
            start_push(i)

    def landed(start, count, sem):
        blocks = src.at[pl.ds(start, count)]
        return pltpu.make_async_copy(blocks, blocks, sem)

    def forward(i):
        blocks = src.at[pl.ds(core * columns + i * tms, tms)]
        return pltpu.make_async_remote_copy(
            src_ref=blocks, dst_ref=blocks, send_sem=fwd_sem, recv_sem=half_sem.at[i],
            device_id=(sibling, me_t), device_id_type=MESH,
        )

    sources = half * block

    def unpack_half(h, wait=False):
        for i in range(half):
            if wait:
                landed(h * columns + i * tms, tms, half_sem.at[i]).wait()
            for w in range(tms):

                def store(rows, lanes, piece):
                    srcf[w, i * block + rows.start : i * block + rows.stop, lanes] = piece

                unpack(src[h * columns + i * tms + w].astype(jnp.float32), store)

    for i in range(half):
        holds = jnp.logical_and(keeps, at == i)

        @pl.when(jnp.logical_not(holds))
        def _():
            landed(core * columns + i * tms, tms, slot_sem.at[i]).wait()

        @pl.when(holds)
        def _():
            landed(core * columns + i * tms, tms - 1, slot_sem.at[i]).wait()

        forward(i).start()
    for load in loads[4:]:
        load.wait()
    keep = maskv[...].astype(jnp.float32)
    count = keep.shape[1]
    diagonal = lax.broadcasted_iota(jnp.int32, (count, count), 0) == lax.broadcasted_iota(jnp.int32, (count, count), 1)
    for r in range(block):
        column = jnp.sum(jnp.where(diagonal, keep[r : r + 1, :], 0.0), axis=1, keepdims=True)
        kept[r] = jnp.broadcast_to(column, (count, LANES))
    pltpu.make_async_copy(rec.at[pl.ds(0, tms - 1)], rec.at[pl.ds(0, tms - 1)], rec_sem).wait()

    for w in range(tms):

        def store_rec(rows, lanes, piece):
            recf[w, rows, lanes] = piece

        unpack(rec[w].astype(jnp.float32), store_rec)

    def store(r, tile, values):
        lanes = slice(tile * LANES, tile * LANES + values.shape[1])
        rows = pl.ds(pl.multiple_of(core * sources, sources), sources)
        first_ref[r, :, lanes] = values * kept[r, rows, : values.shape[1]]

    unpack_half(core)
    correlate_sources(recf, srcf, lagv, first_ref.shape[-1], store)
    @pl.when(jnp.logical_not(keeps))
    def _():
        landed(0, columns + tms - 1, send_sem).wait()

    @pl.when(keeps)
    def _():
        landed(0, columns + tms - 2, send_sem).wait()

    landed(0, columns, fwd_sem).wait()

    unpack_half(1 - core, wait=True)


def fused_device(chans, tms, samples, dead_flags, pair_mask):
    block, _, length = samples.shape
    sources = pair_mask.shape[1]
    group = sources // block
    table, turns = split_tables(length, F)
    lag_weights = folded_lag_tables(length, bin_order(F), LAGS, 1.0 / math.sqrt(tms * F))
    at = np.arange(length)
    taper = 0.5 - 0.5 * np.cos(2.0 * np.pi * (at + 0.5) / length)
    small = np.concatenate([taper.reshape(1, RADIX, length // RADIX), turns]).astype(np.float32)
    vmem, hbm = pl.BlockSpec(memory_space=pltpu.VMEM), pl.BlockSpec(memory_space=pltpu.HBM)
    sem = pltpu.SemaphoreType.DMA
    half = group // 2
    width = packing(block, 2 * F)[0]
    stage = pl.pallas_call(
        functools.partial(fused_kernel, (chans, tms, block, group, F)),
        out_shape=[
            pltpu.VMEM((block, half * block, LAGS), jnp.float32),
            pltpu.VMEM((tms, half * block, 2 * F), jnp.float32),
            pltpu.VMEM((tms, block, 2 * F), jnp.float32),
            pltpu.VMEM(lag_weights.shape, jnp.bfloat16),
            pltpu.VMEM((block, sources, LANES), jnp.float32),
        ],
        in_specs=[hbm] * 6,
        out_specs=[vmem] * 5,
        scratch_shapes=[
            pltpu.VMEM((block, length), jnp.bfloat16),
            pltpu.SMEM((block,), jnp.int32),
            pltpu.VMEM((block, sources), jnp.int32),
            pltpu.VMEM(small.shape, jnp.float32),
            pltpu.VMEM((ROWS, length), jnp.float32),
            pltpu.VMEM((ROWS, width), jnp.float32),
            pltpu.VMEM((ROWS, width), jnp.bfloat16),
            pltpu.VMEM((chans, ROWS, width), jnp.bfloat16),
            pltpu.VMEM((tms, ROWS, width), jnp.bfloat16),
            pltpu.VMEM(table.shape, jnp.bfloat16),
            sem((3,)), sem, sem, sem((half,)), sem((half,)), sem, pltpu.SemaphoreType.REGULAR, pltpu.SemaphoreType.REGULAR,
        ],
        compiler_params=pltpu.CompilerParams(
            collective_id=0, has_side_effects=True, vmem_limit_bytes=24 * 1024 * 1024
        ),
    )(
        *(
            pltpu.with_memory_space_constraint(operand, pltpu.HBM)
            for operand in (
                samples.reshape(block, length), dead_flags, pair_mask, jnp.asarray(small),
                jnp.asarray(table, jnp.bfloat16), jnp.asarray(lag_weights, jnp.bfloat16),
            )
        )
    )
    return pl.pallas_call(
        finish_kernel,
        out_shape=jax.ShapeDtypeStruct((block, sources, LAGS), jnp.float32),
        in_specs=[vmem] * 5,
        out_specs=vmem,
        compiler_params=pltpu.CompilerParams(vmem_limit_bytes=16 * 1024 * 1024),
    )(*stage)


def dispatch(chans, tms, samples, dead_flags, pair_mask):
    block, windows, length = samples.shape
    sources = pair_mask.shape[1]
    whole_blocks = sources % (4 * block) == 0 and chans % 8 == 0 and tms == 2 and sources % 16 == 0 and block * chans == sources * tms
    aligned = length == RADIX * LANES and F % LANES == 0 and F % RADIX == 0 and windows == 1
    if whole_blocks and aligned and packs(block, 2 * F) and folds(LAGS):
        return fused_device(chans, tms, samples, dead_flags, pair_mask)
    return per_device(samples, dead_flags, pair_mask)


def solution(mesh):
    in_specs = (P("chan", "tm", None), P("chan"), P("chan", "tm"))
    out_specs = P("chan", "tm", None)
    chans, tms = mesh.shape["chan"], mesh.shape["tm"]
    return jax.shard_map(
        functools.partial(dispatch, chans, tms),
        mesh=mesh, in_specs=in_specs, out_specs=out_specs, check_vma=False,
    )
```

```python
import functools
import math

import jax
import jax.numpy as jnp
import numpy as np
from jax import lax
from jax.experimental import pallas as pl
from jax.experimental.pallas import tpu as pltpu
from jax.sharding import PartitionSpec as P

F = 768
LAGS = 301


def taper_window(length):
    sample_index = jnp.arange(length, dtype=jnp.float32)
    return 0.5 - 0.5 * jnp.cos(2.0 * math.pi * (sample_index + 0.5) / length)


def forward_table(length, bins):
    sample_index = jnp.arange(length, dtype=jnp.int32)
    frequency = jnp.arange(1, bins + 1, dtype=jnp.int32)
    phase_index = sample_index[:, None] * frequency[None, :] % length
    angles = 2.0 * math.pi / length * phase_index.astype(jnp.float32)
    return jnp.concatenate([jnp.cos(angles), -jnp.sin(angles)], axis=1).astype(jnp.bfloat16)


def lag_table(length, bins, lags, factor):
    frequency = jnp.arange(1, bins + 1, dtype=jnp.int32)
    shifts = jnp.arange(lags, dtype=jnp.int32) - (lags - 1) // 2
    phase_index = jnp.mod(frequency[:, None] * shifts[None, :], length)
    angles = 2.0 * math.pi / length * phase_index.astype(jnp.float32)
    table_values = jnp.concatenate([jnp.cos(angles), -jnp.sin(angles)], axis=0) * factor
    return table_values.astype(jnp.bfloat16)


def whiten(samples, dead_flags, table_values):
    channel_count, windows, length = samples.shape
    bins = table_values.shape[1] // 2
    traces = samples.astype(jnp.float32)
    traces = traces - jnp.mean(traces, axis=-1, keepdims=True)
    tapered = (traces * taper_window(length)).astype(jnp.bfloat16)
    spectra = jnp.dot(
        tapered.reshape(channel_count * windows, length),
        table_values,
        preferred_element_type=jnp.float32,
    )
    real_part = spectra[:, :bins]
    imag_part = spectra[:, bins:]
    energy = real_part * real_part + imag_part * imag_part
    mean_energy = jnp.mean(energy, axis=-1, keepdims=True)
    inverse_scale = lax.rsqrt(energy + 0.25 * mean_energy + 1e-06)
    alive_rows = jnp.repeat((1 - dead_flags).astype(jnp.float32), windows)[:, None]
    whitened = (
        jnp.concatenate([real_part * inverse_scale, imag_part * inverse_scale], axis=1) * alive_rows
    )
    return whitened.astype(jnp.bfloat16).reshape(channel_count, windows, 2 * bins)


def correlate(receivers, sources, lag_weights):
    bins = receivers.shape[-1] // 2
    rec_values = receivers.astype(jnp.float32)
    src_values = sources.astype(jnp.float32)
    rec_re = rec_values[:, None, :, :bins]
    rec_im = rec_values[:, None, :, bins:]
    src_re = src_values[None, :, :, :bins]
    src_im = src_values[None, :, :, bins:]
    cross_re = rec_re * src_re + rec_im * src_im
    cross_im = rec_im * src_re - rec_re * src_im
    cross = jnp.concatenate([cross_re, cross_im], axis=-1).astype(jnp.bfloat16)
    result = jnp.einsum("rgwk,kl->wrgl", cross, lag_weights, preferred_element_type=jnp.float32)
    return result.astype(jnp.bfloat16)


def pick_group(source_count, rows_each):
    chosen = 1
    for candidate in range(1, source_count + 1):
        if source_count % candidate == 0 and candidate * rows_each <= 1024:
            chosen = candidate
    return chosen


def per_device(samples, dead_flags, pair_mask):
    block_size, local_windows, length = samples.shape
    table_values = forward_table(length, F)
    whitened = whiten(samples, dead_flags, table_values)
    subwin = local_windows * lax.axis_size("tm")
    lag_weights = lag_table(length, F, LAGS, 1.0 / math.sqrt(subwin * F))
    incoming = lax.all_gather(whitened, "chan", axis=0, tiled=True)
    source_count = incoming.shape[0]
    group_size = pick_group(source_count, block_size * local_windows)
    grouped = incoming.reshape(source_count // group_size, group_size, local_windows, 2 * F)

    def one_group(group_sources):
        return correlate(whitened, group_sources, lag_weights)[0]

    results = lax.map(one_group, grouped)
    placed = jnp.transpose(results, (1, 0, 2, 3)).reshape(block_size, source_count, LAGS)
    shares = lax.psum_scatter(
        placed.astype(jnp.float32).astype(jnp.bfloat16), "tm", scatter_dimension=1, tiled=True
    ).astype(jnp.float32)
    return shares * pair_mask.astype(jnp.float32)[..., None]


RADIX = 16
LANES = 128
ROWS = 8
MESH = pl.DeviceIdType.MESH


def bin_order(bins):
    share = bins // RADIX
    place = np.arange(bins)
    return place // share + 1 + RADIX * (place % share)


def split_tables(length, bins):
    depth, share = length // RADIX, bins // RADIX
    phases = share // math.gcd(share, LANES)
    steps, lanes = np.arange(depth)[:, None], np.arange(LANES)[None, :]
    table = []
    for phase in range(phases):
        angle = 2.0 * np.pi / depth * (steps * ((phase * LANES + lanes) % share) % depth)
        cos, sin = np.cos(angle), np.sin(angle)
        table.append(np.block([[cos, -sin], [sin, cos]]))
    turn = 2.0 * np.pi / length * (np.arange(1, RADIX + 1)[:, None] * np.arange(depth)[None, :] % length)
    return np.stack(table), np.stack([np.cos(turn), np.sin(turn)])


def folded_lags(lags):
    middle, over = lags // 2, lags - 2 * LANES
    at = np.arange(LANES)
    return np.concatenate([LANES + at - middle, np.where(at < over, LANES, 0) + LANES + at - middle])


def folded_lag_tables(length, order, lags, factor):
    angles = 2.0 * np.pi / length * np.mod(order[:, None] * folded_lags(lags)[None, :], length)
    return (np.stack([np.cos(angles), -np.sin(angles)]) * factor).astype(np.float32)


def folds(lags):
    middle = lags // 2
    return lags % 2 == 1 and 2 * LANES < lags < 3 * LANES and LANES <= middle + 1


def packing(block, length):
    width = block * length // ROWS
    tail = length - width
    return width, tail, width // tail if tail > 0 else 0


def packs(block, length):
    width, tail, chunks = packing(block, length)
    full = block < ROWS and block * length % (ROWS * LANES) == 0
    return full and tail % LANES == 0 and width % tail == 0 and (ROWS - block) * chunks == block


def stage_one(pieces):
    half = RADIX // 2
    sums = [pieces[a] + pieces[RADIX - a] for a in range(1, half)]
    diffs = [pieces[a] - pieces[RADIX - a] for a in range(1, half)]
    even = pieces[0] + pieces[half]
    odd = pieces[0] - pieces[half]

    def real(k):
        total = even if k % 2 == 0 else odd
        for a in range(1, half):
            total = total + sums[a - 1] * float(np.cos(2 * np.pi * a * k / RADIX))
        return total

    def imag(k):
        total = diffs[0] * float(-np.sin(2 * np.pi * k / RADIX))
        for a in range(2, half):
            total = total + diffs[a - 1] * float(-np.sin(2 * np.pi * a * k / RADIX))
        return total

    return [real(k) for k in range(half + 1)], [imag(k) for k in range(1, half)]


def twisted(pieces, turns):
    half = RADIX // 2
    reals, imags = stage_one(pieces)
    rows = []
    for k in range(1, RADIX + 1):
        low = min(k, RADIX - k)
        cos, sin, re = turns[1, k - 1 : k], turns[2, k - 1 : k], reals[low]
        if low == 0 or low == half:
            rows.append(jnp.concatenate([re * cos, -re * sin], axis=1))
            continue
        im = imags[low - 1] if k < half else -imags[low - 1]
        rows.append(jnp.concatenate([re * cos + im * sin, im * cos - re * sin], axis=1))
    return rows


def correlate_sources(recf, srcf, lagv, lags, store):
    tms, block, bins = recf.shape[0], recf.shape[1], recf.shape[2] // 2
    sources = srcf.shape[1]
    even = odd = None
    for first in range(0, bins // LANES, 2):
        parts_re, parts_im = [], []
        for tile in range(first, first + 2):
            lanes = slice(tile * LANES, (tile + 1) * LANES)
            lanes_im = slice(bins + tile * LANES, bins + (tile + 1) * LANES)
            rec_re = [recf[w, :, lanes] for w in range(tms)]
            rec_im = [recf[w, :, lanes_im] for w in range(tms)]
            src_re = [srcf[w, :, lanes] for w in range(tms)]
            src_im = [srcf[w, :, lanes_im] for w in range(tms)]
            rows_re, rows_im = [], []
            for r in range(block):
                total_re = total_im = None
                for w in range(tms):
                    a, c = rec_re[w][r : r + 1, :], rec_im[w][r : r + 1, :]
                    now_re = a * src_re[w] + c * src_im[w]
                    now_im = c * src_re[w] - a * src_im[w]
                    total_re = now_re if total_re is None else total_re + now_re
                    total_im = now_im if total_im is None else total_im + now_im
                rows_re.append(total_re)
                rows_im.append(total_im)
            parts_re.append(jnp.concatenate(rows_re, axis=0).astype(jnp.bfloat16))
            parts_im.append(jnp.concatenate(rows_im, axis=0).astype(jnp.bfloat16))
        depths = slice(first * LANES, (first + 2) * LANES)
        now_even = jnp.dot(
            jnp.concatenate(parts_re, axis=1), lagv[0, depths, :], preferred_element_type=jnp.float32
        )
        now_odd = jnp.dot(
            jnp.concatenate(parts_im, axis=1), lagv[1, depths, :], preferred_element_type=jnp.float32
        )
        even = now_even if even is None else even + now_even
        odd = now_odd if odd is None else odd + now_odd
    ahead = even + odd
    behind = even[:, LANES:] - odd[:, LANES:]
    over = lags - 2 * LANES
    lane = lax.broadcasted_iota(jnp.int32, behind.shape, 1)
    behind = jnp.take_along_axis(behind, (over - 1 - lane + LANES) % LANES, axis=1)
    for r in range(block):
        rows = slice(r * sources, (r + 1) * sources)
        store(r, 0, behind[rows])
        store(r, 1, ahead[rows, :LANES])
        store(r, 2, ahead[rows, LANES : LANES + over])


def taken_half(core, t):
    return jnp.where(t == 0, core, 1 - core)


def finish_kernel(part_ref, srcf, recf, lagv, kept, out_ref):
    own_half = taken_half(lax.axis_index("chan") % 2, lax.axis_index("tm"))
    block, _, lags = part_ref.shape
    sources = srcf.shape[1]
    for r in range(block):
        out_ref[r] = part_ref[r]

    def store(r, tile, values):
        lanes = slice(tile * LANES, tile * LANES + values.shape[1])
        out_ref[r, :sources, lanes] = values * kept[r, :sources, : values.shape[1]]

    @pl.when(own_half == 1)
    def _():
        correlate_sources(recf, srcf, lagv, lags, store)


def push_orders(columns):
    near, far = list(range(columns // 2)), list(range(columns // 2, columns))
    return [near + far[0::2] + far[1::2], near + far]


def fused_kernel(
    sizes, samples_hbm, dead_hbm, mask_hbm, small_hbm, table_ref, lag_ref,
    part_ref, srcf, recf, lagv, kept,
    samples_ref, dead_ref, maskv, small, padded, packed, own, src, rec, table,
    load_sem, send_sem, fwd_sem, slot_sem, half_sem, rec_sem, gate, ready,
):
    chans, tms, block, group, bins = sizes
    me_c, me_t = lax.axis_index("chan"), lax.axis_index("tm")
    core = me_c % 2
    columns = chans // 2
    barrier = pltpu.get_barrier_semaphore()
    sibling = me_c + 1 - 2 * core
    half = group // 2
    own_half = taken_half(core, me_t)
    chip = me_c // 2
    orders = push_orders(columns)
    splits = [columns // 2 + 1, 1]

    def choose(t, values):
        return jnp.where(t == 0, values[0], values[1])

    def is_late(t, at):
        late = [functools.reduce(jnp.logical_or, [at == i for i in o[n:]]) for o, n in zip(orders, splits)]
        return jnp.where(t == 0, late[0].astype(jnp.int32), late[1].astype(jnp.int32))

    part = is_late(me_t, chip)
    home_late = jnp.logical_and(me_t == 1, chip >= columns // 2)
    told_later = jnp.logical_and(home_late, own_half == 0)
    for i in range(half // 2):
        for w in range(tms):
            from_chip = (me_t * group + own_half * half) // 2 + i
            own_chip = jnp.logical_and(from_chip == chip, w == me_t)

            @pl.when(jnp.logical_not(jnp.logical_or(own_chip, told_later)))
            def _():
                pl.semaphore_signal(
                    barrier, inc=1, device_id=(2 * from_chip + part, w), device_id_type=MESH
                )

    for step in range(1, tms):
        pl.semaphore_signal(
            barrier, inc=1, device_id=(2 * chip, (me_t + step) % tms), device_id_type=MESH
        )
    pl.semaphore_signal(barrier, inc=1, device_id=(sibling, me_t), device_id_type=MESH)
    to_t = me_c // group
    slot = me_c % group
    to_half, at = slot // half, slot % half
    inner = jnp.logical_and(to_t == 1, to_half == 0)
    for i in range(columns // 2, columns):

        @pl.when(inner & (core == 0) & jnp.logical_not((me_t == 1) & (chip == i)))
        def _():
            pl.semaphore_signal(barrier, inc=1, device_id=(2 * i + 1, 1), device_id_type=MESH)


    length = samples_ref.shape[-1]
    depth = length // RADIX
    loads = [
        pltpu.make_async_copy(samples_hbm, samples_ref, load_sem.at[0]),
        pltpu.make_async_copy(small_hbm, small, load_sem.at[0]),
        pltpu.make_async_copy(dead_hbm, dead_ref, load_sem.at[0]),
        pltpu.make_async_copy(table_ref, table, load_sem.at[1]),
        pltpu.make_async_copy(mask_hbm, maskv, load_sem.at[2]),
        pltpu.make_async_copy(lag_ref, lagv, load_sem.at[2]),
    ]
    for load in loads:
        load.start()

    for load in loads[:3]:
        load.wait()
    traces = samples_ref[...].astype(jnp.float32)
    traces = traces - jnp.mean(traces, axis=-1, keepdims=True)
    padded[block:, :] = jnp.zeros((ROWS - block, length), jnp.float32)
    for a in range(RADIX):
        lanes = slice(a * depth, (a + 1) * depth)
        padded[:block, lanes] = (traces[:, lanes] * small[0, a : a + 1]).astype(jnp.bfloat16).astype(jnp.float32)
    rows = twisted([padded[:, a * depth : (a + 1) * depth] for a in range(RADIX)], small)
    row = lax.broadcasted_iota(jnp.int32, (ROWS, 1), 0)
    alive = jnp.zeros((ROWS, 1), jnp.float32)
    for r in range(block):
        alive = jnp.where(row == r, (1 - dead_ref[r]).astype(jnp.float32), alive)
    loads[3].wait()
    share = bins // RADIX
    phases = table.shape[0]
    tiles = bins // LANES
    lane = lax.broadcasted_iota(jnp.int32, (1, LANES), 1)
    parts = [None] * tiles
    energy_sum = jnp.zeros((ROWS, LANES), jnp.float32)
    for phase in range(phases):
        members = []
        for tile in range(phase, tiles, phases):
            first, last = tile * LANES // share, (tile * LANES + LANES - 1) // share
            members += [(tile, r) for r in range(first, last + 1)]
        lhs = jnp.concatenate([rows[r] for _, r in members], axis=0).astype(jnp.bfloat16)
        spec = jnp.dot(lhs, table[phase], preferred_element_type=jnp.float32)
        for tile in range(phase, tiles, phases):
            re = im = None
            for index, (which, r) in enumerate(members):
                if which != tile:
                    continue
                now = spec[index * ROWS : (index + 1) * ROWS]
                begin = r * share - tile * LANES
                re = now[:, :LANES] if re is None else jnp.where(lane >= begin, now[:, :LANES], re)
                im = now[:, LANES:] if im is None else jnp.where(lane >= begin, now[:, LANES:], im)
            energy = re * re + im * im
            energy_sum = energy_sum + energy
            parts[tile] = (re, im, energy)
    width, tail, chunks = packing(block, 2 * bins)

    def pack(start, piece):
        if start < width:
            packed[:block, start : start + LANES] = piece[:block]
            return
        for r in range(block):
            first = (r % chunks) * tail + start - width
            packed[block + r // chunks : block + r // chunks + 1, first : first + LANES] = piece[r : r + 1]

    def unpack(values, store):
        store(slice(0, block), slice(0, width), values[:block])
        for r in range(block):
            first = (r % chunks) * tail
            store(
                slice(r, r + 1), slice(width, width + tail),
                values[block + r // chunks : block + r // chunks + 1, first : first + tail],
            )

    mean_energy = jnp.sum(energy_sum, axis=-1, keepdims=True) / bins
    for tile, (re, im, energy) in enumerate(parts):
        scale = lax.rsqrt(energy + 0.25 * mean_energy + 1e-06)
        pack(tile * LANES, re * scale * alive)
        pack(bins + tile * LANES, im * scale * alive)
    own[...] = packed[...].astype(jnp.bfloat16)

    keeps = jnp.logical_and(to_t == me_t, to_half == own_half)
    split = choose(to_t, splits)
    until = jnp.where(inner, columns // 2, columns)
    in_part = jnp.logical_and(to_t == me_t, jnp.logical_and(part == core, jnp.logical_not(jnp.logical_and(inner, core == 1))))
    entered = jnp.where(core == 0, split + 2 * (tms - 1), until - split) + 1 - in_part.astype(jnp.int32)
    greeted = half // 2 * tms - inner.astype(jnp.int32)
    entered = entered + jnp.where(jnp.logical_and(home_late, core == 1), greeted, 0)

    def open_gate():
        pl.semaphore_signal(gate, inc=1, device_id=(sibling, me_t), device_id_type=MESH)

    mine = to_half * columns + at * tms + me_t

    def push(i):
        return pltpu.make_async_remote_copy(
            src_ref=own, dst_ref=src.at[mine], send_sem=send_sem, recv_sem=slot_sem.at[at],
            device_id=(2 * i + taken_half(to_half, to_t), to_t), device_id_type=MESH,
        )

    def start_push(i):
        @pl.when(jnp.logical_not(jnp.logical_and(keeps, i == chip)))
        def _():
            push(i).start()

    def pair_copy(step):
        return pltpu.make_async_remote_copy(
            src_ref=own, dst_ref=rec.at[me_t], send_sem=send_sem, recv_sem=rec_sem,
            device_id=(me_c, (me_t + step) % tms), device_id_type=MESH,
        )

    rec[me_t] = own[...]

    @pl.when(keeps)
    def _():
        src[mine] = own[...]

    @pl.when(core == 0)
    def _():
        pl.semaphore_wait(barrier, entered)
        open_gate()

    @pl.when(core == 1)
    def _():
        pl.semaphore_wait(gate, 1)

    for q in range(max(splits)):
        @pl.when(q < split)
        def _():
            start_push(choose(to_t, [o[q] for o in orders]))

    for step in range(1, tms):
        pair_copy(step).start()

    @pl.when(core == 0)
    def _():
        pl.semaphore_wait(gate, 1)

    @pl.when(core == 1)
    def _():
        pl.semaphore_wait(barrier, entered)
        open_gate()

    for q in range(min(splits), columns):

        @pl.when(jnp.logical_and(q >= split, q < until))
        def _():
            start_push(choose(to_t, [o[q] for o in orders]))

    for i in range(half // 2):
        for w in range(tms):
            to_chip = group // 2 + i

            @pl.when(home_late & (core == 1) & jnp.logical_not((to_chip == chip) & (w == me_t)))
            def _():
                pl.semaphore_signal(ready, inc=1, device_id=(2 * to_chip, w), device_id_type=MESH)

    @pl.when(jnp.logical_and(inner, core == 0))
    def _():
        pl.semaphore_wait(ready, columns // 2 - (me_t == 1).astype(jnp.int32))
        open_gate()

    @pl.when(jnp.logical_and(inner, core == 1))
    def _():
        pl.semaphore_wait(gate, 1)

    for i in range(columns // 2, columns):

        @pl.when(inner)
        def _():
            start_push(i)

    def landed(start, count, sem):
        blocks = src.at[pl.ds(start, count)]
        return pltpu.make_async_copy(blocks, blocks, sem)

    def forward(i):
        blocks = src.at[pl.ds(own_half * columns + i * tms, tms)]
        return pltpu.make_async_remote_copy(
            src_ref=blocks, dst_ref=blocks, send_sem=fwd_sem, recv_sem=half_sem.at[i],
            device_id=(sibling, me_t), device_id_type=MESH,
        )

    sources = half * block

    def unpack_half(h, wait=False):
        for i in range(half):
            if wait:
                landed(h * columns + i * tms, tms, half_sem.at[i]).wait()
            for w in range(tms):

                def store(rows, lanes, piece):
                    srcf[w, i * block + rows.start : i * block + rows.stop, lanes] = piece

                unpack(src[h * columns + i * tms + w].astype(jnp.float32), store)

    for i in range(half):
        holds = jnp.logical_and(keeps, at == i)

        @pl.when(jnp.logical_not(holds))
        def _():
            landed(own_half * columns + i * tms, tms, slot_sem.at[i]).wait()

        @pl.when(holds)
        def _():
            landed(own_half * columns + i * tms, tms - 1, slot_sem.at[i]).wait()

        forward(i).start()
    for load in loads[4:]:
        load.wait()
    keep = maskv[...].astype(jnp.float32)
    count = keep.shape[1]
    diagonal = lax.broadcasted_iota(jnp.int32, (count, count), 0) == lax.broadcasted_iota(jnp.int32, (count, count), 1)
    for r in range(block):
        column = jnp.sum(jnp.where(diagonal, keep[r : r + 1, :], 0.0), axis=1, keepdims=True)
        kept[r] = jnp.broadcast_to(column, (count, LANES))
    pltpu.make_async_copy(rec.at[pl.ds(0, tms - 1)], rec.at[pl.ds(0, tms - 1)], rec_sem).wait()

    for w in range(tms):

        def store_rec(rows, lanes, piece):
            recf[w, rows, lanes] = piece

        unpack(rec[w].astype(jnp.float32), store_rec)

    def store_at(h):
        rows = pl.ds(pl.multiple_of(h * sources, sources), sources)

        def store(r, tile, values):
            lanes = slice(tile * LANES, tile * LANES + values.shape[1])
            part_ref[r, rows, lanes] = values * kept[r, rows, : values.shape[1]]

        return store

    lags = part_ref.shape[-1]
    unpack_half(own_half)
    correlate_sources(recf, srcf, lagv, lags, store_at(own_half))

    @pl.when(own_half == 0)
    def _():
        unpack_half(1 - own_half, wait=True)
        correlate_sources(recf, srcf, lagv, lags, store_at(1 - own_half))

    @pl.when(jnp.logical_not(keeps))
    def _():
        landed(0, columns + tms - 1, send_sem).wait()

    @pl.when(keeps)
    def _():
        landed(0, columns + tms - 2, send_sem).wait()

    landed(0, columns, fwd_sem).wait()

    @pl.when(own_half == 1)
    def _():
        unpack_half(1 - own_half, wait=True)


def fused_device(chans, tms, samples, dead_flags, pair_mask):
    block, _, length = samples.shape
    sources = pair_mask.shape[1]
    group = sources // block
    table, turns = split_tables(length, F)
    lag_weights = folded_lag_tables(length, bin_order(F), LAGS, 1.0 / math.sqrt(tms * F))
    at = np.arange(length)
    taper = 0.5 - 0.5 * np.cos(2.0 * np.pi * (at + 0.5) / length)
    small = np.concatenate([taper.reshape(1, RADIX, length // RADIX), turns]).astype(np.float32)
    vmem, hbm = pl.BlockSpec(memory_space=pltpu.VMEM), pl.BlockSpec(memory_space=pltpu.HBM)
    sem = pltpu.SemaphoreType.DMA
    half = group // 2
    width = packing(block, 2 * F)[0]
    stage = pl.pallas_call(
        functools.partial(fused_kernel, (chans, tms, block, group, F)),
        out_shape=[
            pltpu.VMEM((block, sources, LAGS), jnp.float32),
            pltpu.VMEM((tms, half * block, 2 * F), jnp.float32),
            pltpu.VMEM((tms, block, 2 * F), jnp.float32),
            pltpu.VMEM(lag_weights.shape, jnp.bfloat16),
            pltpu.VMEM((block, sources, LANES), jnp.float32),
        ],
        in_specs=[hbm] * 6,
        out_specs=[vmem] * 5,
        scratch_shapes=[
            pltpu.VMEM((block, length), jnp.bfloat16),
            pltpu.SMEM((block,), jnp.int32),
            pltpu.VMEM((block, sources), jnp.int32),
            pltpu.VMEM(small.shape, jnp.float32),
            pltpu.VMEM((ROWS, length), jnp.float32),
            pltpu.VMEM((ROWS, width), jnp.float32),
            pltpu.VMEM((ROWS, width), jnp.bfloat16),
            pltpu.VMEM((chans, ROWS, width), jnp.bfloat16),
            pltpu.VMEM((tms, ROWS, width), jnp.bfloat16),
            pltpu.VMEM(table.shape, jnp.bfloat16),
            sem((3,)), sem, sem, sem((half,)), sem((half,)), sem, pltpu.SemaphoreType.REGULAR, pltpu.SemaphoreType.REGULAR,
        ],
        compiler_params=pltpu.CompilerParams(
            collective_id=0, has_side_effects=True, vmem_limit_bytes=24 * 1024 * 1024
        ),
    )(
        *(
            pltpu.with_memory_space_constraint(operand, pltpu.HBM)
            for operand in (
                samples.reshape(block, length), dead_flags, pair_mask, jnp.asarray(small),
                jnp.asarray(table, jnp.bfloat16), jnp.asarray(lag_weights, jnp.bfloat16),
            )
        )
    )
    return pl.pallas_call(
        finish_kernel,
        out_shape=jax.ShapeDtypeStruct((block, sources, LAGS), jnp.float32),
        in_specs=[vmem] * 5,
        out_specs=vmem,
        compiler_params=pltpu.CompilerParams(vmem_limit_bytes=16 * 1024 * 1024),
    )(*stage)


def dispatch(chans, tms, samples, dead_flags, pair_mask):
    block, windows, length = samples.shape
    sources = pair_mask.shape[1]
    whole_blocks = sources % (4 * block) == 0 and chans % 8 == 0 and tms == 2 and sources % 16 == 0 and block * chans == sources * tms
    aligned = length == RADIX * LANES and F % LANES == 0 and F % RADIX == 0 and windows == 1
    if whole_blocks and aligned and packs(block, 2 * F) and folds(LAGS):
        return fused_device(chans, tms, samples, dead_flags, pair_mask)
    return per_device(samples, dead_flags, pair_mask)


def solution(mesh):
    in_specs = (P("chan", "tm", None), P("chan"), P("chan", "tm"))
    out_specs = P("chan", "tm", None)
    chans, tms = mesh.shape["chan"], mesh.shape["tm"]
    return jax.shard_map(
        functools.partial(dispatch, chans, tms),
        mesh=mesh, in_specs=in_specs, out_specs=out_specs, check_vma=False,
    )
```

```python
import functools
import math

import jax
import jax.numpy as jnp
import numpy as np
from jax import lax
from jax.experimental import pallas as pl
from jax.experimental.pallas import tpu as pltpu
from jax.sharding import PartitionSpec as P

F = 768
LAGS = 301


def taper_window(length):
    sample_index = jnp.arange(length, dtype=jnp.float32)
    return 0.5 - 0.5 * jnp.cos(2.0 * math.pi * (sample_index + 0.5) / length)


def forward_table(length, bins):
    sample_index = jnp.arange(length, dtype=jnp.int32)
    frequency = jnp.arange(1, bins + 1, dtype=jnp.int32)
    phase_index = sample_index[:, None] * frequency[None, :] % length
    angles = 2.0 * math.pi / length * phase_index.astype(jnp.float32)
    return jnp.concatenate([jnp.cos(angles), -jnp.sin(angles)], axis=1).astype(jnp.bfloat16)


def lag_table(length, bins, lags, factor):
    frequency = jnp.arange(1, bins + 1, dtype=jnp.int32)
    shifts = jnp.arange(lags, dtype=jnp.int32) - (lags - 1) // 2
    phase_index = jnp.mod(frequency[:, None] * shifts[None, :], length)
    angles = 2.0 * math.pi / length * phase_index.astype(jnp.float32)
    table_values = jnp.concatenate([jnp.cos(angles), -jnp.sin(angles)], axis=0) * factor
    return table_values.astype(jnp.bfloat16)


def whiten(samples, dead_flags, table_values):
    channel_count, windows, length = samples.shape
    bins = table_values.shape[1] // 2
    traces = samples.astype(jnp.float32)
    traces = traces - jnp.mean(traces, axis=-1, keepdims=True)
    tapered = (traces * taper_window(length)).astype(jnp.bfloat16)
    spectra = jnp.dot(
        tapered.reshape(channel_count * windows, length),
        table_values,
        preferred_element_type=jnp.float32,
    )
    real_part = spectra[:, :bins]
    imag_part = spectra[:, bins:]
    energy = real_part * real_part + imag_part * imag_part
    mean_energy = jnp.mean(energy, axis=-1, keepdims=True)
    inverse_scale = lax.rsqrt(energy + 0.25 * mean_energy + 1e-06)
    alive_rows = jnp.repeat((1 - dead_flags).astype(jnp.float32), windows)[:, None]
    whitened = (
        jnp.concatenate([real_part * inverse_scale, imag_part * inverse_scale], axis=1) * alive_rows
    )
    return whitened.astype(jnp.bfloat16).reshape(channel_count, windows, 2 * bins)


def correlate(receivers, sources, lag_weights):
    bins = receivers.shape[-1] // 2
    rec_values = receivers.astype(jnp.float32)
    src_values = sources.astype(jnp.float32)
    rec_re = rec_values[:, None, :, :bins]
    rec_im = rec_values[:, None, :, bins:]
    src_re = src_values[None, :, :, :bins]
    src_im = src_values[None, :, :, bins:]
    cross_re = rec_re * src_re + rec_im * src_im
    cross_im = rec_im * src_re - rec_re * src_im
    cross = jnp.concatenate([cross_re, cross_im], axis=-1).astype(jnp.bfloat16)
    result = jnp.einsum("rgwk,kl->wrgl", cross, lag_weights, preferred_element_type=jnp.float32)
    return result.astype(jnp.bfloat16)


def pick_group(source_count, rows_each):
    chosen = 1
    for candidate in range(1, source_count + 1):
        if source_count % candidate == 0 and candidate * rows_each <= 1024:
            chosen = candidate
    return chosen


def per_device(samples, dead_flags, pair_mask):
    block_size, local_windows, length = samples.shape
    table_values = forward_table(length, F)
    whitened = whiten(samples, dead_flags, table_values)
    subwin = local_windows * lax.axis_size("tm")
    lag_weights = lag_table(length, F, LAGS, 1.0 / math.sqrt(subwin * F))
    incoming = lax.all_gather(whitened, "chan", axis=0, tiled=True)
    source_count = incoming.shape[0]
    group_size = pick_group(source_count, block_size * local_windows)
    grouped = incoming.reshape(source_count // group_size, group_size, local_windows, 2 * F)

    def one_group(group_sources):
        return correlate(whitened, group_sources, lag_weights)[0]

    results = lax.map(one_group, grouped)
    placed = jnp.transpose(results, (1, 0, 2, 3)).reshape(block_size, source_count, LAGS)
    shares = lax.psum_scatter(
        placed.astype(jnp.float32).astype(jnp.bfloat16), "tm", scatter_dimension=1, tiled=True
    ).astype(jnp.float32)
    return shares * pair_mask.astype(jnp.float32)[..., None]


RADIX = 16
LANES = 128
ROWS = 8
MESH = pl.DeviceIdType.MESH


def bin_order(bins):
    share = bins // RADIX
    place = np.arange(bins)
    return place // share + 1 + RADIX * (place % share)


def split_tables(length, bins):
    depth, share = length // RADIX, bins // RADIX
    phases = share // math.gcd(share, LANES)
    steps, lanes = np.arange(depth)[:, None], np.arange(LANES)[None, :]
    table = []
    for phase in range(phases):
        angle = 2.0 * np.pi / depth * (steps * ((phase * LANES + lanes) % share) % depth)
        cos, sin = np.cos(angle), np.sin(angle)
        table.append(np.block([[cos, -sin], [sin, cos]]))
    turn = 2.0 * np.pi / length * (np.arange(1, RADIX + 1)[:, None] * np.arange(depth)[None, :] % length)
    return np.stack(table), np.stack([np.cos(turn), np.sin(turn)])


def folded_lags(lags):
    middle, over = lags // 2, lags - 2 * LANES
    at = np.arange(LANES)
    return np.concatenate([LANES + at - middle, np.where(at < over, LANES, 0) + LANES + at - middle])


def folded_lag_tables(length, order, lags, factor):
    angles = 2.0 * np.pi / length * np.mod(order[:, None] * folded_lags(lags)[None, :], length)
    return (np.stack([np.cos(angles), -np.sin(angles)]) * factor).astype(np.float32)


def folds(lags):
    middle = lags // 2
    return lags % 2 == 1 and 2 * LANES < lags < 3 * LANES and LANES <= middle + 1


def packing(block, length):
    width = block * length // ROWS
    tail = length - width
    return width, tail, width // tail if tail > 0 else 0


def packs(block, length):
    width, tail, chunks = packing(block, length)
    full = block < ROWS and block * length % (ROWS * LANES) == 0
    return full and tail % LANES == 0 and width % tail == 0 and (ROWS - block) * chunks == block


def stage_one(pieces):
    half = RADIX // 2
    sums = [pieces[a] + pieces[RADIX - a] for a in range(1, half)]
    diffs = [pieces[a] - pieces[RADIX - a] for a in range(1, half)]
    even = pieces[0] + pieces[half]
    odd = pieces[0] - pieces[half]

    def real(k):
        total = even if k % 2 == 0 else odd
        for a in range(1, half):
            total = total + sums[a - 1] * float(np.cos(2 * np.pi * a * k / RADIX))
        return total

    def imag(k):
        total = diffs[0] * float(-np.sin(2 * np.pi * k / RADIX))
        for a in range(2, half):
            total = total + diffs[a - 1] * float(-np.sin(2 * np.pi * a * k / RADIX))
        return total

    return [real(k) for k in range(half + 1)], [imag(k) for k in range(1, half)]


def twisted(pieces, turns):
    half = RADIX // 2
    reals, imags = stage_one(pieces)
    rows = []
    for k in range(1, RADIX + 1):
        low = min(k, RADIX - k)
        cos, sin, re = turns[1, k - 1 : k], turns[2, k - 1 : k], reals[low]
        if low == 0 or low == half:
            rows.append(jnp.concatenate([re * cos, -re * sin], axis=1))
            continue
        im = imags[low - 1] if k < half else -imags[low - 1]
        rows.append(jnp.concatenate([re * cos + im * sin, im * cos - re * sin], axis=1))
    return rows


def correlate_sources(recf, srcf, lagv, lags, store):
    tms, block, bins = recf.shape[0], recf.shape[1], recf.shape[2] // 2
    sources = srcf.shape[1]
    even = odd = None
    for first in range(0, bins // LANES, 2):
        parts_re, parts_im = [], []
        for tile in range(first, first + 2):
            lanes = slice(tile * LANES, (tile + 1) * LANES)
            lanes_im = slice(bins + tile * LANES, bins + (tile + 1) * LANES)
            rec_re = [recf[w, :, lanes] for w in range(tms)]
            rec_im = [recf[w, :, lanes_im] for w in range(tms)]
            src_re = [srcf[w, :, lanes] for w in range(tms)]
            src_im = [srcf[w, :, lanes_im] for w in range(tms)]
            rows_re, rows_im = [], []
            for r in range(block):
                total_re = total_im = None
                for w in range(tms):
                    a, c = rec_re[w][r : r + 1, :], rec_im[w][r : r + 1, :]
                    now_re = a * src_re[w] + c * src_im[w]
                    now_im = c * src_re[w] - a * src_im[w]
                    total_re = now_re if total_re is None else total_re + now_re
                    total_im = now_im if total_im is None else total_im + now_im
                rows_re.append(total_re)
                rows_im.append(total_im)
            parts_re.append(jnp.concatenate(rows_re, axis=0).astype(jnp.bfloat16))
            parts_im.append(jnp.concatenate(rows_im, axis=0).astype(jnp.bfloat16))
        depths = slice(first * LANES, (first + 2) * LANES)
        now_even = jnp.dot(
            jnp.concatenate(parts_re, axis=1), lagv[0, depths, :], preferred_element_type=jnp.float32
        )
        now_odd = jnp.dot(
            jnp.concatenate(parts_im, axis=1), lagv[1, depths, :], preferred_element_type=jnp.float32
        )
        even = now_even if even is None else even + now_even
        odd = now_odd if odd is None else odd + now_odd
    ahead = even + odd
    behind = even[:, LANES:] - odd[:, LANES:]
    over = lags - 2 * LANES
    lane = lax.broadcasted_iota(jnp.int32, behind.shape, 1)
    behind = jnp.take_along_axis(behind, (over - 1 - lane + LANES) % LANES, axis=1)
    for r in range(block):
        rows = slice(r * sources, (r + 1) * sources)
        store(r, 0, behind[rows])
        store(r, 1, ahead[rows, :LANES])
        store(r, 2, ahead[rows, LANES : LANES + over])


def taken_half(core, t):
    return jnp.where(t == 0, core, 1 - core)


def finish_kernel(part_ref, srcf, recf, lagv, kept, out_ref):
    own_half = taken_half(lax.axis_index("chan") % 2, lax.axis_index("tm"))
    block, _, lags = part_ref.shape
    sources = srcf.shape[1]
    for r in range(block):
        out_ref[r] = part_ref[r]

    def store(r, tile, values):
        lanes = slice(tile * LANES, tile * LANES + values.shape[1])
        out_ref[r, :sources, lanes] = values * kept[r, :sources, : values.shape[1]]

    @pl.when(own_half == 1)
    def _():
        correlate_sources(recf, srcf, lagv, lags, store)


def push_orders(columns):
    near, far = list(range(columns // 2)), list(range(columns // 2, columns))
    return [near + far[0::2] + far[1::2], near + far]


def fused_kernel(
    sizes, samples_hbm, dead_hbm, mask_hbm, small_hbm, table_ref, lag_ref,
    part_ref, srcf, recf, lagv, kept,
    samples_ref, dead_ref, maskv, small, padded, packed, own, src, rec, table,
    load_sem, send_sem, fwd_sem, slot_sem, half_sem, rec_sem, gate, ready,
):
    chans, tms, block, group, bins = sizes
    me_c, me_t = lax.axis_index("chan"), lax.axis_index("tm")
    core = me_c % 2
    columns = chans // 2
    barrier = pltpu.get_barrier_semaphore()
    sibling = me_c + 1 - 2 * core
    half = group // 2
    own_half = taken_half(core, me_t)
    chip = me_c // 2
    orders = push_orders(columns)
    splits = [columns // 2 + 1, 1]

    def choose(t, values):
        return jnp.where(t == 0, values[0], values[1])

    def is_late(t, at):
        late = [functools.reduce(jnp.logical_or, [at == i for i in o[n:]]) for o, n in zip(orders, splits)]
        return jnp.where(t == 0, late[0].astype(jnp.int32), late[1].astype(jnp.int32))

    part = is_late(me_t, chip)
    home_late = jnp.logical_and(me_t == 1, chip >= columns // 2)
    told_later = jnp.logical_and(home_late, own_half == 0)
    for i in range(half // 2):
        for w in range(tms):
            from_chip = (me_t * group + own_half * half) // 2 + i
            own_chip = jnp.logical_and(from_chip == chip, w == me_t)

            @pl.when(jnp.logical_not(jnp.logical_or(own_chip, told_later)))
            def _():
                pl.semaphore_signal(
                    barrier, inc=1, device_id=(2 * from_chip + part, w), device_id_type=MESH
                )

    for step in range(1, tms):
        pl.semaphore_signal(
            barrier, inc=1, device_id=(2 * chip, (me_t + step) % tms), device_id_type=MESH
        )
    pl.semaphore_signal(barrier, inc=1, device_id=(sibling, me_t), device_id_type=MESH)
    to_t = me_c // group
    slot = me_c % group
    to_half, at = slot // half, slot % half
    inner = jnp.logical_and(to_t == 1, to_half == 0)
    for i in range(columns // 2, columns):

        @pl.when(inner & (core == 0) & jnp.logical_not((me_t == 1) & (chip == i)))
        def _():
            pl.semaphore_signal(barrier, inc=1, device_id=(2 * i + 1, 1), device_id_type=MESH)


    length = samples_ref.shape[-1]
    depth = length // RADIX
    loads = [
        pltpu.make_async_copy(samples_hbm, samples_ref, load_sem.at[0]),
        pltpu.make_async_copy(small_hbm, small, load_sem.at[0]),
        pltpu.make_async_copy(dead_hbm, dead_ref, load_sem.at[0]),
        pltpu.make_async_copy(table_ref, table, load_sem.at[1]),
        pltpu.make_async_copy(mask_hbm, maskv, load_sem.at[2]),
        pltpu.make_async_copy(lag_ref, lagv, load_sem.at[2]),
    ]
    for load in loads:
        load.start()

    for load in loads[:3]:
        load.wait()
    traces = samples_ref[...].astype(jnp.float32)
    traces = traces - jnp.mean(traces, axis=-1, keepdims=True)
    padded[block:, :] = jnp.zeros((ROWS - block, length), jnp.float32)
    for a in range(RADIX):
        lanes = slice(a * depth, (a + 1) * depth)
        padded[:block, lanes] = (traces[:, lanes] * small[0, a : a + 1]).astype(jnp.bfloat16).astype(jnp.float32)
    rows = twisted([padded[:, a * depth : (a + 1) * depth] for a in range(RADIX)], small)
    row = lax.broadcasted_iota(jnp.int32, (ROWS, 1), 0)
    alive = jnp.zeros((ROWS, 1), jnp.float32)
    for r in range(block):
        alive = jnp.where(row == r, (1 - dead_ref[r]).astype(jnp.float32), alive)
    loads[3].wait()
    share = bins // RADIX
    phases = table.shape[0]
    tiles = bins // LANES
    lane = lax.broadcasted_iota(jnp.int32, (1, LANES), 1)
    parts = [None] * tiles
    energy_sum = jnp.zeros((ROWS, LANES), jnp.float32)
    for phase in range(phases):
        members = []
        for tile in range(phase, tiles, phases):
            first, last = tile * LANES // share, (tile * LANES + LANES - 1) // share
            members += [(tile, r) for r in range(first, last + 1)]
        lhs = jnp.concatenate([rows[r] for _, r in members], axis=0).astype(jnp.bfloat16)
        spec = jnp.dot(lhs, table[phase], preferred_element_type=jnp.float32)
        for tile in range(phase, tiles, phases):
            re = im = None
            for index, (which, r) in enumerate(members):
                if which != tile:
                    continue
                now = spec[index * ROWS : (index + 1) * ROWS]
                begin = r * share - tile * LANES
                re = now[:, :LANES] if re is None else jnp.where(lane >= begin, now[:, :LANES], re)
                im = now[:, LANES:] if im is None else jnp.where(lane >= begin, now[:, LANES:], im)
            energy = re * re + im * im
            energy_sum = energy_sum + energy
            parts[tile] = (re, im, energy)
    width, tail, chunks = packing(block, 2 * bins)

    def pack(start, piece):
        if start < width:
            packed[:block, start : start + LANES] = piece[:block]
            return
        for r in range(block):
            first = (r % chunks) * tail + start - width
            packed[block + r // chunks : block + r // chunks + 1, first : first + LANES] = piece[r : r + 1]

    def unpack(values, store):
        store(slice(0, block), slice(0, width), values[:block])
        for r in range(block):
            first = (r % chunks) * tail
            store(
                slice(r, r + 1), slice(width, width + tail),
                values[block + r // chunks : block + r // chunks + 1, first : first + tail],
            )

    mean_energy = jnp.sum(energy_sum, axis=-1, keepdims=True) / bins
    for tile, (re, im, energy) in enumerate(parts):
        scale = lax.rsqrt(energy + 0.25 * mean_energy + 1e-06)
        pack(tile * LANES, re * scale * alive)
        pack(bins + tile * LANES, im * scale * alive)
    own[...] = packed[...].astype(jnp.bfloat16)

    keeps = jnp.logical_and(to_t == me_t, to_half == own_half)
    split = choose(to_t, splits)
    until = jnp.where(inner, columns // 2, columns)
    in_part = jnp.logical_and(to_t == me_t, jnp.logical_and(part == core, jnp.logical_not(jnp.logical_and(inner, core == 1))))
    entered = jnp.where(core == 0, split + 2 * (tms - 1), until - split) + 1 - in_part.astype(jnp.int32)
    greeted = half // 2 * tms - inner.astype(jnp.int32)
    entered = entered + jnp.where(jnp.logical_and(home_late, core == 1), greeted, 0)

    def open_gate():
        pl.semaphore_signal(gate, inc=1, device_id=(sibling, me_t), device_id_type=MESH)

    mine = to_half * columns + at * tms + me_t

    def push(i):
        return pltpu.make_async_remote_copy(
            src_ref=own, dst_ref=src.at[mine], send_sem=send_sem, recv_sem=slot_sem.at[at],
            device_id=(2 * i + taken_half(to_half, to_t), to_t), device_id_type=MESH,
        )

    def start_push(i):
        @pl.when(jnp.logical_not(jnp.logical_and(keeps, i == chip)))
        def _():
            push(i).start()

    def pair_copy(step):
        return pltpu.make_async_remote_copy(
            src_ref=own, dst_ref=rec.at[me_t], send_sem=send_sem, recv_sem=rec_sem,
            device_id=(me_c, (me_t + step) % tms), device_id_type=MESH,
        )


    @pl.when(keeps)
    def _():
        src[mine] = own[...]

    @pl.when(core == 0)
    def _():
        pl.semaphore_wait(barrier, entered)
        open_gate()

    @pl.when(core == 1)
    def _():
        pl.semaphore_wait(gate, 1)

    for q in range(max(splits)):
        @pl.when(q < split)
        def _():
            start_push(choose(to_t, [o[q] for o in orders]))

    rec[me_t] = own[...]
    for step in range(1, tms):
        pair_copy(step).start()

    @pl.when(core == 0)
    def _():
        pl.semaphore_wait(gate, 1)

    @pl.when(core == 1)
    def _():
        pl.semaphore_wait(barrier, entered)
        open_gate()

    for q in range(min(splits), columns):

        @pl.when(jnp.logical_and(q >= split, q < until))
        def _():
            start_push(choose(to_t, [o[q] for o in orders]))

    for i in range(half // 2):
        for w in range(tms):
            to_chip = group // 2 + i

            @pl.when(home_late & (core == 1) & jnp.logical_not((to_chip == chip) & (w == me_t)))
            def _():
                pl.semaphore_signal(ready, inc=1, device_id=(2 * to_chip, w), device_id_type=MESH)

    @pl.when(jnp.logical_and(inner, core == 0))
    def _():
        pl.semaphore_wait(ready, columns // 2 - (me_t == 1).astype(jnp.int32))
        open_gate()

    @pl.when(jnp.logical_and(inner, core == 1))
    def _():
        pl.semaphore_wait(gate, 1)

    for i in range(columns // 2, columns):

        @pl.when(inner)
        def _():
            start_push(i)

    def landed(start, count, sem):
        blocks = src.at[pl.ds(start, count)]
        return pltpu.make_async_copy(blocks, blocks, sem)

    def forward(i):
        blocks = src.at[pl.ds(own_half * columns + i * tms, tms)]
        return pltpu.make_async_remote_copy(
            src_ref=blocks, dst_ref=blocks, send_sem=fwd_sem, recv_sem=half_sem.at[i],
            device_id=(sibling, me_t), device_id_type=MESH,
        )

    sources = half * block

    def unpack_half(h, wait=False):
        for i in range(half):
            if wait:
                landed(h * columns + i * tms, tms, half_sem.at[i]).wait()
            for w in range(tms):

                def store(rows, lanes, piece):
                    srcf[w, i * block + rows.start : i * block + rows.stop, lanes] = piece

                unpack(src[h * columns + i * tms + w].astype(jnp.float32), store)

    for load in loads[4:]:
        load.wait()
    keep = maskv[...].astype(jnp.float32)
    count = keep.shape[1]
    diagonal = lax.broadcasted_iota(jnp.int32, (count, count), 0) == lax.broadcasted_iota(jnp.int32, (count, count), 1)
    for r in range(block):
        column = jnp.sum(jnp.where(diagonal, keep[r : r + 1, :], 0.0), axis=1, keepdims=True)
        kept[r] = jnp.broadcast_to(column, (count, LANES))
    for i in range(half):
        holds = jnp.logical_and(keeps, at == i)

        @pl.when(jnp.logical_not(holds))
        def _():
            landed(own_half * columns + i * tms, tms, slot_sem.at[i]).wait()

        @pl.when(holds)
        def _():
            landed(own_half * columns + i * tms, tms - 1, slot_sem.at[i]).wait()

        forward(i).start()
    pltpu.make_async_copy(rec.at[pl.ds(0, tms - 1)], rec.at[pl.ds(0, tms - 1)], rec_sem).wait()

    for w in range(tms):

        def store_rec(rows, lanes, piece):
            recf[w, rows, lanes] = piece

        unpack(rec[w].astype(jnp.float32), store_rec)

    def store_at(h):
        rows = pl.ds(pl.multiple_of(h * sources, sources), sources)

        def store(r, tile, values):
            lanes = slice(tile * LANES, tile * LANES + values.shape[1])
            part_ref[r, rows, lanes] = values * kept[r, rows, : values.shape[1]]

        return store

    lags = part_ref.shape[-1]
    unpack_half(own_half)
    correlate_sources(recf, srcf, lagv, lags, store_at(own_half))

    @pl.when(own_half == 0)
    def _():
        unpack_half(1 - own_half, wait=True)
        correlate_sources(recf, srcf, lagv, lags, store_at(1 - own_half))

    @pl.when(jnp.logical_not(keeps))
    def _():
        landed(0, columns + tms - 1, send_sem).wait()

    @pl.when(keeps)
    def _():
        landed(0, columns + tms - 2, send_sem).wait()

    landed(0, columns, fwd_sem).wait()

    @pl.when(own_half == 1)
    def _():
        unpack_half(1 - own_half, wait=True)


def fused_device(chans, tms, samples, dead_flags, pair_mask):
    block, _, length = samples.shape
    sources = pair_mask.shape[1]
    group = sources // block
    table, turns = split_tables(length, F)
    lag_weights = folded_lag_tables(length, bin_order(F), LAGS, 1.0 / math.sqrt(tms * F))
    at = np.arange(length)
    taper = 0.5 - 0.5 * np.cos(2.0 * np.pi * (at + 0.5) / length)
    small = np.concatenate([taper.reshape(1, RADIX, length // RADIX), turns]).astype(np.float32)
    vmem, hbm = pl.BlockSpec(memory_space=pltpu.VMEM), pl.BlockSpec(memory_space=pltpu.HBM)
    sem = pltpu.SemaphoreType.DMA
    half = group // 2
    width = packing(block, 2 * F)[0]
    stage = pl.pallas_call(
        functools.partial(fused_kernel, (chans, tms, block, group, F)),
        out_shape=[
            pltpu.VMEM((block, sources, LAGS), jnp.float32),
            pltpu.VMEM((tms, half * block, 2 * F), jnp.float32),
            pltpu.VMEM((tms, block, 2 * F), jnp.float32),
            pltpu.VMEM(lag_weights.shape, jnp.bfloat16),
            pltpu.VMEM((block, sources, LANES), jnp.float32),
        ],
        in_specs=[hbm] * 6,
        out_specs=[vmem] * 5,
        scratch_shapes=[
            pltpu.VMEM((block, length), jnp.bfloat16),
            pltpu.SMEM((block,), jnp.int32),
            pltpu.VMEM((block, sources), jnp.int32),
            pltpu.VMEM(small.shape, jnp.float32),
            pltpu.VMEM((ROWS, length), jnp.float32),
            pltpu.VMEM((ROWS, width), jnp.float32),
            pltpu.VMEM((ROWS, width), jnp.bfloat16),
            pltpu.VMEM((chans, ROWS, width), jnp.bfloat16),
            pltpu.VMEM((tms, ROWS, width), jnp.bfloat16),
            pltpu.VMEM(table.shape, jnp.bfloat16),
            sem((3,)), sem, sem, sem((half,)), sem((half,)), sem, pltpu.SemaphoreType.REGULAR, pltpu.SemaphoreType.REGULAR,
        ],
        compiler_params=pltpu.CompilerParams(
            collective_id=0, has_side_effects=True, vmem_limit_bytes=24 * 1024 * 1024
        ),
    )(
        *(
            pltpu.with_memory_space_constraint(operand, pltpu.HBM)
            for operand in (
                samples.reshape(block, length), dead_flags, pair_mask, jnp.asarray(small),
                jnp.asarray(table, jnp.bfloat16), jnp.asarray(lag_weights, jnp.bfloat16),
            )
        )
    )
    return pl.pallas_call(
        finish_kernel,
        out_shape=jax.ShapeDtypeStruct((block, sources, LAGS), jnp.float32),
        in_specs=[vmem] * 5,
        out_specs=vmem,
        compiler_params=pltpu.CompilerParams(vmem_limit_bytes=16 * 1024 * 1024),
    )(*stage)


def dispatch(chans, tms, samples, dead_flags, pair_mask):
    block, windows, length = samples.shape
    sources = pair_mask.shape[1]
    whole_blocks = sources % (4 * block) == 0 and chans % 8 == 0 and tms == 2 and sources % 16 == 0 and block * chans == sources * tms
    aligned = length == RADIX * LANES and F % LANES == 0 and F % RADIX == 0 and windows == 1
    if whole_blocks and aligned and packs(block, 2 * F) and folds(LAGS):
        return fused_device(chans, tms, samples, dead_flags, pair_mask)
    return per_device(samples, dead_flags, pair_mask)


def solution(mesh):
    in_specs = (P("chan", "tm", None), P("chan"), P("chan", "tm"))
    out_specs = P("chan", "tm", None)
    chans, tms = mesh.shape["chan"], mesh.shape["tm"]
    return jax.shard_map(
        functools.partial(dispatch, chans, tms),
        mesh=mesh, in_specs=in_specs, out_specs=out_specs, check_vma=False,
    )
```

```python
import functools
import math

import jax
import jax.numpy as jnp
import numpy as np
from jax import lax
from jax.experimental import pallas as pl
from jax.experimental.pallas import tpu as pltpu
from jax.sharding import PartitionSpec as P

F = 768
LAGS = 301


def taper_window(length):
    sample_index = jnp.arange(length, dtype=jnp.float32)
    return 0.5 - 0.5 * jnp.cos(2.0 * math.pi * (sample_index + 0.5) / length)


def forward_table(length, bins):
    sample_index = jnp.arange(length, dtype=jnp.int32)
    frequency = jnp.arange(1, bins + 1, dtype=jnp.int32)
    phase_index = sample_index[:, None] * frequency[None, :] % length
    angles = 2.0 * math.pi / length * phase_index.astype(jnp.float32)
    return jnp.concatenate([jnp.cos(angles), -jnp.sin(angles)], axis=1).astype(jnp.bfloat16)


def lag_table(length, bins, lags, factor):
    frequency = jnp.arange(1, bins + 1, dtype=jnp.int32)
    shifts = jnp.arange(lags, dtype=jnp.int32) - (lags - 1) // 2
    phase_index = jnp.mod(frequency[:, None] * shifts[None, :], length)
    angles = 2.0 * math.pi / length * phase_index.astype(jnp.float32)
    table_values = jnp.concatenate([jnp.cos(angles), -jnp.sin(angles)], axis=0) * factor
    return table_values.astype(jnp.bfloat16)


def whiten(samples, dead_flags, table_values):
    channel_count, windows, length = samples.shape
    bins = table_values.shape[1] // 2
    traces = samples.astype(jnp.float32)
    traces = traces - jnp.mean(traces, axis=-1, keepdims=True)
    tapered = (traces * taper_window(length)).astype(jnp.bfloat16)
    spectra = jnp.dot(
        tapered.reshape(channel_count * windows, length),
        table_values,
        preferred_element_type=jnp.float32,
    )
    real_part = spectra[:, :bins]
    imag_part = spectra[:, bins:]
    energy = real_part * real_part + imag_part * imag_part
    mean_energy = jnp.mean(energy, axis=-1, keepdims=True)
    inverse_scale = lax.rsqrt(energy + 0.25 * mean_energy + 1e-06)
    alive_rows = jnp.repeat((1 - dead_flags).astype(jnp.float32), windows)[:, None]
    whitened = (
        jnp.concatenate([real_part * inverse_scale, imag_part * inverse_scale], axis=1) * alive_rows
    )
    return whitened.astype(jnp.bfloat16).reshape(channel_count, windows, 2 * bins)


def correlate(receivers, sources, lag_weights):
    bins = receivers.shape[-1] // 2
    rec_values = receivers.astype(jnp.float32)
    src_values = sources.astype(jnp.float32)
    rec_re = rec_values[:, None, :, :bins]
    rec_im = rec_values[:, None, :, bins:]
    src_re = src_values[None, :, :, :bins]
    src_im = src_values[None, :, :, bins:]
    cross_re = rec_re * src_re + rec_im * src_im
    cross_im = rec_im * src_re - rec_re * src_im
    cross = jnp.concatenate([cross_re, cross_im], axis=-1).astype(jnp.bfloat16)
    result = jnp.einsum("rgwk,kl->wrgl", cross, lag_weights, preferred_element_type=jnp.float32)
    return result.astype(jnp.bfloat16)


def pick_group(source_count, rows_each):
    chosen = 1
    for candidate in range(1, source_count + 1):
        if source_count % candidate == 0 and candidate * rows_each <= 1024:
            chosen = candidate
    return chosen


def per_device(samples, dead_flags, pair_mask):
    block_size, local_windows, length = samples.shape
    table_values = forward_table(length, F)
    whitened = whiten(samples, dead_flags, table_values)
    subwin = local_windows * lax.axis_size("tm")
    lag_weights = lag_table(length, F, LAGS, 1.0 / math.sqrt(subwin * F))
    incoming = lax.all_gather(whitened, "chan", axis=0, tiled=True)
    source_count = incoming.shape[0]
    group_size = pick_group(source_count, block_size * local_windows)
    grouped = incoming.reshape(source_count // group_size, group_size, local_windows, 2 * F)

    def one_group(group_sources):
        return correlate(whitened, group_sources, lag_weights)[0]

    results = lax.map(one_group, grouped)
    placed = jnp.transpose(results, (1, 0, 2, 3)).reshape(block_size, source_count, LAGS)
    shares = lax.psum_scatter(
        placed.astype(jnp.float32).astype(jnp.bfloat16), "tm", scatter_dimension=1, tiled=True
    ).astype(jnp.float32)
    return shares * pair_mask.astype(jnp.float32)[..., None]


RADIX = 16
LANES = 128
ROWS = 8
MESH = pl.DeviceIdType.MESH


def bin_order(bins):
    share = bins // RADIX
    place = np.arange(bins)
    return place // share + 1 + RADIX * (place % share)


def split_tables(length, bins):
    depth, share = length // RADIX, bins // RADIX
    phases = share // math.gcd(share, LANES)
    steps, lanes = np.arange(depth)[:, None], np.arange(LANES)[None, :]
    table = []
    for phase in range(phases):
        angle = 2.0 * np.pi / depth * (steps * ((phase * LANES + lanes) % share) % depth)
        cos, sin = np.cos(angle), np.sin(angle)
        table.append(np.block([[cos, -sin], [sin, cos]]))
    turn = 2.0 * np.pi / length * (np.arange(1, RADIX + 1)[:, None] * np.arange(depth)[None, :] % length)
    return np.stack(table), np.stack([np.cos(turn), np.sin(turn)])


def folded_lags(lags):
    middle, over = lags // 2, lags - 2 * LANES
    at = np.arange(LANES)
    return np.concatenate([LANES + at - middle, np.where(at < over, LANES, 0) + LANES + at - middle])


def folded_lag_tables(length, order, lags, factor):
    angles = 2.0 * np.pi / length * np.mod(order[:, None] * folded_lags(lags)[None, :], length)
    return (np.stack([np.cos(angles), -np.sin(angles)]) * factor).astype(np.float32)


def folds(lags):
    middle = lags // 2
    return lags % 2 == 1 and 2 * LANES < lags < 3 * LANES and LANES <= middle + 1


def packing(block, length):
    width = block * length // ROWS
    tail = length - width
    return width, tail, width // tail if tail > 0 else 0


def packs(block, length):
    width, tail, chunks = packing(block, length)
    full = block < ROWS and block * length % (ROWS * LANES) == 0
    return full and tail % LANES == 0 and width % tail == 0 and (ROWS - block) * chunks == block


def stage_one(pieces):
    half = RADIX // 2
    sums = [pieces[a] + pieces[RADIX - a] for a in range(1, half)]
    diffs = [pieces[a] - pieces[RADIX - a] for a in range(1, half)]
    even = pieces[0] + pieces[half]
    odd = pieces[0] - pieces[half]

    def real(k):
        total = even if k % 2 == 0 else odd
        for a in range(1, half):
            total = total + sums[a - 1] * float(np.cos(2 * np.pi * a * k / RADIX))
        return total

    def imag(k):
        total = diffs[0] * float(-np.sin(2 * np.pi * k / RADIX))
        for a in range(2, half):
            total = total + diffs[a - 1] * float(-np.sin(2 * np.pi * a * k / RADIX))
        return total

    return [real(k) for k in range(half + 1)], [imag(k) for k in range(1, half)]


def twisted(pieces, turns):
    half = RADIX // 2
    reals, imags = stage_one(pieces)
    rows = []
    for k in range(1, RADIX + 1):
        low = min(k, RADIX - k)
        cos, sin, re = turns[1, k - 1 : k], turns[2, k - 1 : k], reals[low]
        if low == 0 or low == half:
            rows.append(jnp.concatenate([re * cos, -re * sin], axis=1))
            continue
        im = imags[low - 1] if k < half else -imags[low - 1]
        rows.append(jnp.concatenate([re * cos + im * sin, im * cos - re * sin], axis=1))
    return rows


def correlate_sources(recf, srcf, lagv, lags, store):
    tms, block, bins = recf.shape[0], recf.shape[1], recf.shape[2] // 2
    sources = srcf.shape[1]
    even = odd = None
    for first in range(0, bins // LANES, 2):
        parts_re, parts_im = [], []
        for tile in range(first, first + 2):
            lanes = slice(tile * LANES, (tile + 1) * LANES)
            lanes_im = slice(bins + tile * LANES, bins + (tile + 1) * LANES)
            rec_re = [recf[w, :, lanes] for w in range(tms)]
            rec_im = [recf[w, :, lanes_im] for w in range(tms)]
            src_re = [srcf[w, :, lanes] for w in range(tms)]
            src_im = [srcf[w, :, lanes_im] for w in range(tms)]
            rows_re, rows_im = [], []
            for r in range(block):
                total_re = total_im = None
                for w in range(tms):
                    a, c = rec_re[w][r : r + 1, :], rec_im[w][r : r + 1, :]
                    now_re = a * src_re[w] + c * src_im[w]
                    now_im = c * src_re[w] - a * src_im[w]
                    total_re = now_re if total_re is None else total_re + now_re
                    total_im = now_im if total_im is None else total_im + now_im
                rows_re.append(total_re)
                rows_im.append(total_im)
            parts_re.append(jnp.concatenate(rows_re, axis=0).astype(jnp.bfloat16))
            parts_im.append(jnp.concatenate(rows_im, axis=0).astype(jnp.bfloat16))
        depths = slice(first * LANES, (first + 2) * LANES)
        now_even = jnp.dot(
            jnp.concatenate(parts_re, axis=1), lagv[0, depths, :], preferred_element_type=jnp.float32
        )
        now_odd = jnp.dot(
            jnp.concatenate(parts_im, axis=1), lagv[1, depths, :], preferred_element_type=jnp.float32
        )
        even = now_even if even is None else even + now_even
        odd = now_odd if odd is None else odd + now_odd
    ahead = even + odd
    behind = even[:, LANES:] - odd[:, LANES:]
    over = lags - 2 * LANES
    lane = lax.broadcasted_iota(jnp.int32, behind.shape, 1)
    behind = jnp.take_along_axis(behind, (over - 1 - lane + LANES) % LANES, axis=1)
    for r in range(block):
        rows = slice(r * sources, (r + 1) * sources)
        store(r, 0, behind[rows])
        store(r, 1, ahead[rows, :LANES])
        store(r, 2, ahead[rows, LANES : LANES + over])


def taken_half(core, t):
    return jnp.where(t == 0, core, 1 - core)


def finish_kernel(part_ref, srcf, recf, lagv, kept, out_ref):
    own_half = taken_half(lax.axis_index("chan") % 2, lax.axis_index("tm"))
    block, _, lags = part_ref.shape
    sources = srcf.shape[1]
    for r in range(block):
        out_ref[r] = part_ref[r]

    def store(r, tile, values):
        lanes = slice(tile * LANES, tile * LANES + values.shape[1])
        out_ref[r, :sources, lanes] = values * kept[r, :sources, : values.shape[1]]

    @pl.when(own_half == 1)
    def _():
        correlate_sources(recf, srcf, lagv, lags, store)


def push_orders(columns):
    near, far = list(range(columns // 2)), list(range(columns // 2, columns))
    return [near + far[0::2] + far[1::2], near + far]


def fused_kernel(
    sizes, samples_hbm, dead_hbm, mask_hbm, small_hbm, table_ref, lag_ref,
    part_ref, srcf, recf, lagv, kept,
    samples_ref, dead_ref, maskv, small, padded, packed, own, src, rec, table,
    load_sem, send_sem, fwd_sem, slot_sem, half_sem, rec_sem, gate, ready,
):
    chans, tms, block, group, bins = sizes
    me_c, me_t = lax.axis_index("chan"), lax.axis_index("tm")
    core = me_c % 2
    columns = chans // 2
    barrier = pltpu.get_barrier_semaphore()
    sibling = me_c + 1 - 2 * core
    half = group // 2
    own_half = taken_half(core, me_t)
    chip = me_c // 2
    orders = push_orders(columns)
    splits = [columns // 2 + 1, 1]

    def choose(t, values):
        return jnp.where(t == 0, values[0], values[1])

    def is_late(t, at):
        late = [functools.reduce(jnp.logical_or, [at == i for i in o[n:]]) for o, n in zip(orders, splits)]
        return jnp.where(t == 0, late[0].astype(jnp.int32), late[1].astype(jnp.int32))

    part = is_late(me_t, chip)
    home_late = jnp.logical_and(me_t == 1, chip >= columns // 2)
    told_later = jnp.logical_and(home_late, own_half == 0)
    for i in range(half // 2):
        for w in range(tms):
            from_chip = (me_t * group + own_half * half) // 2 + i
            own_chip = jnp.logical_and(from_chip == chip, w == me_t)

            @pl.when(jnp.logical_not(jnp.logical_or(own_chip, told_later)))
            def _():
                pl.semaphore_signal(
                    barrier, inc=1, device_id=(2 * from_chip + part, w), device_id_type=MESH
                )

    for step in range(1, tms):
        pl.semaphore_signal(
            barrier, inc=1, device_id=(2 * chip, (me_t + step) % tms), device_id_type=MESH
        )
    pl.semaphore_signal(barrier, inc=1, device_id=(sibling, me_t), device_id_type=MESH)
    to_t = me_c // group
    slot = me_c % group
    to_half, at = slot // half, slot % half
    inner = jnp.logical_and(to_t == 1, to_half == 0)
    for i in range(columns // 2, columns):

        @pl.when(inner & (core == 0) & jnp.logical_not((me_t == 1) & (chip == i)))
        def _():
            pl.semaphore_signal(barrier, inc=1, device_id=(2 * i + 1, 1), device_id_type=MESH)


    length = samples_ref.shape[-1]
    depth = length // RADIX
    loads = [
        pltpu.make_async_copy(samples_hbm, samples_ref, load_sem.at[0]),
        pltpu.make_async_copy(small_hbm, small, load_sem.at[0]),
        pltpu.make_async_copy(dead_hbm, dead_ref, load_sem.at[0]),
        pltpu.make_async_copy(table_ref, table, load_sem.at[1]),
        pltpu.make_async_copy(mask_hbm, maskv, load_sem.at[2]),
        pltpu.make_async_copy(lag_ref, lagv, load_sem.at[2]),
    ]
    for load in loads:
        load.start()

    for load in loads[:3]:
        load.wait()
    traces = samples_ref[...].astype(jnp.float32)
    traces = traces - jnp.mean(traces, axis=-1, keepdims=True)
    padded[block:, :] = jnp.zeros((ROWS - block, length), jnp.float32)
    for a in range(RADIX):
        lanes = slice(a * depth, (a + 1) * depth)
        padded[:block, lanes] = (traces[:, lanes] * small[0, a : a + 1]).astype(jnp.bfloat16).astype(jnp.float32)
    rows = twisted([padded[:, a * depth : (a + 1) * depth] for a in range(RADIX)], small)
    row = lax.broadcasted_iota(jnp.int32, (ROWS, 1), 0)
    alive = jnp.zeros((ROWS, 1), jnp.float32)
    for r in range(block):
        alive = jnp.where(row == r, (1 - dead_ref[r]).astype(jnp.float32), alive)
    loads[3].wait()
    share = bins // RADIX
    phases = table.shape[0]
    tiles = bins // LANES
    lane = lax.broadcasted_iota(jnp.int32, (1, LANES), 1)
    parts = [None] * tiles
    energy_sum = jnp.zeros((ROWS, LANES), jnp.float32)
    for phase in range(phases):
        members = []
        for tile in range(phase, tiles, phases):
            first, last = tile * LANES // share, (tile * LANES + LANES - 1) // share
            members += [(tile, r) for r in range(first, last + 1)]
        lhs = jnp.concatenate([rows[r] for _, r in members], axis=0).astype(jnp.bfloat16)
        spec = jnp.dot(lhs, table[phase], preferred_element_type=jnp.float32)
        for tile in range(phase, tiles, phases):
            re = im = None
            for index, (which, r) in enumerate(members):
                if which != tile:
                    continue
                now = spec[index * ROWS : (index + 1) * ROWS]
                begin = r * share - tile * LANES
                re = now[:, :LANES] if re is None else jnp.where(lane >= begin, now[:, :LANES], re)
                im = now[:, LANES:] if im is None else jnp.where(lane >= begin, now[:, LANES:], im)
            energy = re * re + im * im
            energy_sum = energy_sum + energy
            parts[tile] = (re, im, energy)
    width, tail, chunks = packing(block, 2 * bins)

    def pack(start, piece):
        if start < width:
            packed[:block, start : start + LANES] = piece[:block]
            return
        for r in range(block):
            first = (r % chunks) * tail + start - width
            packed[block + r // chunks : block + r // chunks + 1, first : first + LANES] = piece[r : r + 1]

    def unpack(values, store):
        store(slice(0, block), slice(0, width), values[:block])
        for r in range(block):
            first = (r % chunks) * tail
            store(
                slice(r, r + 1), slice(width, width + tail),
                values[block + r // chunks : block + r // chunks + 1, first : first + tail],
            )

    mean_energy = jnp.sum(energy_sum, axis=-1, keepdims=True) / bins
    for tile, (re, im, energy) in enumerate(parts):
        scale = lax.rsqrt(energy + 0.25 * mean_energy + 1e-06)
        pack(tile * LANES, re * scale * alive)
        pack(bins + tile * LANES, im * scale * alive)
    own[...] = packed[...].astype(jnp.bfloat16)

    keeps = jnp.logical_and(to_t == me_t, to_half == own_half)
    split = choose(to_t, splits)
    until = jnp.where(inner, columns // 2, columns)
    in_part = jnp.logical_and(to_t == me_t, jnp.logical_and(part == core, jnp.logical_not(jnp.logical_and(inner, core == 1))))
    entered = jnp.where(core == 0, split + 2 * (tms - 1), until - split) + 1 - in_part.astype(jnp.int32)
    greeted = half // 2 * tms - inner.astype(jnp.int32)
    entered = entered + jnp.where(jnp.logical_and(home_late, core == 1), greeted, 0)

    def open_gate():
        pl.semaphore_signal(gate, inc=1, device_id=(sibling, me_t), device_id_type=MESH)

    mine = to_half * columns + at * tms + me_t

    def push(i):
        return pltpu.make_async_remote_copy(
            src_ref=own, dst_ref=src.at[mine], send_sem=send_sem, recv_sem=slot_sem.at[at // 2],
            device_id=(2 * i + taken_half(to_half, to_t), to_t), device_id_type=MESH,
        )

    def start_push(i):
        @pl.when(jnp.logical_not(jnp.logical_and(keeps, i == chip)))
        def _():
            push(i).start()

    def pair_copy(step):
        return pltpu.make_async_remote_copy(
            src_ref=own, dst_ref=rec.at[me_t], send_sem=send_sem, recv_sem=rec_sem,
            device_id=(me_c, (me_t + step) % tms), device_id_type=MESH,
        )


    @pl.when(keeps)
    def _():
        src[mine] = own[...]

    @pl.when(core == 0)
    def _():
        pl.semaphore_wait(barrier, entered)
        open_gate()

    @pl.when(core == 1)
    def _():
        pl.semaphore_wait(gate, 1)

    for q in range(max(splits)):
        @pl.when(q < split)
        def _():
            start_push(choose(to_t, [o[q] for o in orders]))

    rec[me_t] = own[...]
    for step in range(1, tms):
        pair_copy(step).start()

    @pl.when(core == 0)
    def _():
        pl.semaphore_wait(gate, 1)

    @pl.when(core == 1)
    def _():
        pl.semaphore_wait(barrier, entered)
        open_gate()

    for q in range(min(splits), columns):

        @pl.when(jnp.logical_and(q >= split, q < until))
        def _():
            start_push(choose(to_t, [o[q] for o in orders]))

    for i in range(half // 2):
        for w in range(tms):
            to_chip = group // 2 + i

            @pl.when(home_late & (core == 1) & jnp.logical_not((to_chip == chip) & (w == me_t)))
            def _():
                pl.semaphore_signal(ready, inc=1, device_id=(2 * to_chip, w), device_id_type=MESH)

    @pl.when(jnp.logical_and(inner, core == 0))
    def _():
        pl.semaphore_wait(ready, columns // 2 - (me_t == 1).astype(jnp.int32))
        open_gate()

    @pl.when(jnp.logical_and(inner, core == 1))
    def _():
        pl.semaphore_wait(gate, 1)

    for i in range(columns // 2, columns):

        @pl.when(inner)
        def _():
            start_push(i)

    def landed(start, count, sem):
        blocks = src.at[pl.ds(start, count)]
        return pltpu.make_async_copy(blocks, blocks, sem)

    def forward(i):
        blocks = src.at[pl.ds(own_half * columns + i * 2 * tms, 2 * tms)]
        return pltpu.make_async_remote_copy(
            src_ref=blocks, dst_ref=blocks, send_sem=fwd_sem, recv_sem=half_sem.at[i],
            device_id=(sibling, me_t), device_id_type=MESH,
        )

    sources = half * block

    def unpack_half(h, wait=False):
        for i in range(half):
            if wait and i % 2 == 0:
                landed(h * columns + i * tms, 2 * tms, half_sem.at[i // 2]).wait()
            for w in range(tms):

                def store(rows, lanes, piece):
                    srcf[w, i * block + rows.start : i * block + rows.stop, lanes] = piece

                unpack(src[h * columns + i * tms + w].astype(jnp.float32), store)

    for load in loads[4:]:
        load.wait()
    keep = maskv[...].astype(jnp.float32)
    count = keep.shape[1]
    diagonal = lax.broadcasted_iota(jnp.int32, (count, count), 0) == lax.broadcasted_iota(jnp.int32, (count, count), 1)
    for r in range(block):
        column = jnp.sum(jnp.where(diagonal, keep[r : r + 1, :], 0.0), axis=1, keepdims=True)
        kept[r] = jnp.broadcast_to(column, (count, LANES))
    pair = 2 * tms
    for i in range(half // 2):
        holds = jnp.logical_and(keeps, at // 2 == i)

        @pl.when(jnp.logical_not(holds))
        def _():
            landed(own_half * columns + i * pair, pair, slot_sem.at[i]).wait()

        @pl.when(holds)
        def _():
            landed(own_half * columns + i * pair, pair - 1, slot_sem.at[i]).wait()

        forward(i).start()
    pltpu.make_async_copy(rec.at[pl.ds(0, tms - 1)], rec.at[pl.ds(0, tms - 1)], rec_sem).wait()

    for w in range(tms):

        def store_rec(rows, lanes, piece):
            recf[w, rows, lanes] = piece

        unpack(rec[w].astype(jnp.float32), store_rec)

    def store_at(h):
        rows = pl.ds(pl.multiple_of(h * sources, sources), sources)

        def store(r, tile, values):
            lanes = slice(tile * LANES, tile * LANES + values.shape[1])
            part_ref[r, rows, lanes] = values * kept[r, rows, : values.shape[1]]

        return store

    lags = part_ref.shape[-1]
    unpack_half(own_half)
    correlate_sources(recf, srcf, lagv, lags, store_at(own_half))

    @pl.when(own_half == 0)
    def _():
        unpack_half(1 - own_half, wait=True)
        correlate_sources(recf, srcf, lagv, lags, store_at(1 - own_half))

    @pl.when(jnp.logical_not(keeps))
    def _():
        landed(0, columns + tms - 1, send_sem).wait()

    @pl.when(keeps)
    def _():
        landed(0, columns + tms - 2, send_sem).wait()

    landed(0, columns, fwd_sem).wait()

    @pl.when(own_half == 1)
    def _():
        unpack_half(1 - own_half, wait=True)


def fused_device(chans, tms, samples, dead_flags, pair_mask):
    block, _, length = samples.shape
    sources = pair_mask.shape[1]
    group = sources // block
    table, turns = split_tables(length, F)
    lag_weights = folded_lag_tables(length, bin_order(F), LAGS, 1.0 / math.sqrt(tms * F))
    at = np.arange(length)
    taper = 0.5 - 0.5 * np.cos(2.0 * np.pi * (at + 0.5) / length)
    small = np.concatenate([taper.reshape(1, RADIX, length // RADIX), turns]).astype(np.float32)
    vmem, hbm = pl.BlockSpec(memory_space=pltpu.VMEM), pl.BlockSpec(memory_space=pltpu.HBM)
    sem = pltpu.SemaphoreType.DMA
    half = group // 2
    width = packing(block, 2 * F)[0]
    stage = pl.pallas_call(
        functools.partial(fused_kernel, (chans, tms, block, group, F)),
        out_shape=[
            pltpu.VMEM((block, sources, LAGS), jnp.float32),
            pltpu.VMEM((tms, half * block, 2 * F), jnp.float32),
            pltpu.VMEM((tms, block, 2 * F), jnp.float32),
            pltpu.VMEM(lag_weights.shape, jnp.bfloat16),
            pltpu.VMEM((block, sources, LANES), jnp.float32),
        ],
        in_specs=[hbm] * 6,
        out_specs=[vmem] * 5,
        scratch_shapes=[
            pltpu.VMEM((block, length), jnp.bfloat16),
            pltpu.SMEM((block,), jnp.int32),
            pltpu.VMEM((block, sources), jnp.int32),
            pltpu.VMEM(small.shape, jnp.float32),
            pltpu.VMEM((ROWS, length), jnp.float32),
            pltpu.VMEM((ROWS, width), jnp.float32),
            pltpu.VMEM((ROWS, width), jnp.bfloat16),
            pltpu.VMEM((chans, ROWS, width), jnp.bfloat16),
            pltpu.VMEM((tms, ROWS, width), jnp.bfloat16),
            pltpu.VMEM(table.shape, jnp.bfloat16),
            sem((3,)), sem, sem, sem((half // 2,)), sem((half // 2,)), sem, pltpu.SemaphoreType.REGULAR, pltpu.SemaphoreType.REGULAR,
        ],
        compiler_params=pltpu.CompilerParams(
            collective_id=0, has_side_effects=True, vmem_limit_bytes=24 * 1024 * 1024
        ),
    )(
        *(
            pltpu.with_memory_space_constraint(operand, pltpu.HBM)
            for operand in (
                samples.reshape(block, length), dead_flags, pair_mask, jnp.asarray(small),
                jnp.asarray(table, jnp.bfloat16), jnp.asarray(lag_weights, jnp.bfloat16),
            )
        )
    )
    return pl.pallas_call(
        finish_kernel,
        out_shape=jax.ShapeDtypeStruct((block, sources, LAGS), jnp.float32),
        in_specs=[vmem] * 5,
        out_specs=vmem,
        compiler_params=pltpu.CompilerParams(vmem_limit_bytes=16 * 1024 * 1024),
    )(*stage)


def dispatch(chans, tms, samples, dead_flags, pair_mask):
    block, windows, length = samples.shape
    sources = pair_mask.shape[1]
    whole_blocks = sources % (4 * block) == 0 and chans % 8 == 0 and tms == 2 and sources % 16 == 0 and block * chans == sources * tms
    aligned = length == RADIX * LANES and F % LANES == 0 and F % RADIX == 0 and windows == 1
    if whole_blocks and aligned and packs(block, 2 * F) and folds(LAGS):
        return fused_device(chans, tms, samples, dead_flags, pair_mask)
    return per_device(samples, dead_flags, pair_mask)


def solution(mesh):
    in_specs = (P("chan", "tm", None), P("chan"), P("chan", "tm"))
    out_specs = P("chan", "tm", None)
    chans, tms = mesh.shape["chan"], mesh.shape["tm"]
    return jax.shard_map(
        functools.partial(dispatch, chans, tms),
        mesh=mesh, in_specs=in_specs, out_specs=out_specs, check_vma=False,
    )
```
